32 devices in a mesh: col: 16 (over z, x, core), orb: 2 (over y).
Axes of the slice: x: 2, y: 2, z: 4, core: 2. Of those that a mesh axis runs over, the one named last changes fastest.
Arguments:
- slab_occ: bfloat16 [1024, 400], P('col', 'orb'), may hold values from -6 to 6
- slab_vir: bfloat16 [1024, 2400], P('col', 'orb'), may hold values from -6 to 6
- orbitals_occ: bfloat16 [400, 16384], P('orb', 'col'), may hold values from -0.3125 to 0.3125
- orbitals_vir: bfloat16 [2400, 16384], P('orb', 'col'), may hold values from -0.125 to 0.125
- occ_energy: float32 [400], P('orb'), may hold values from -2 to -0.1
- vir_energy: float32 [2400], P('orb'), may hold values from 0.1 to 3
- screened: bfloat16 [1024, 16384], P('col'), may hold values from -6 to 6
Outputs:
- occ_kernel: bfloat16 [1024, 400], P(('col', 'orb'))
- vir_kernel: bfloat16 [1024, 2400], P(('col', 'orb'))
The draws below stay inside these ranges and needn't reach their ends.
All inputs are finite; a program needn't handle non-finite values.
Results may differ from the reference program's by a relative error of at most 0.014.
Values may be sent and summed in bfloat16 or wider, within the bound.
A program may use at most 64 MiB of HBM per device.

```python
import jax
import jax.numpy as jnp
from jax import lax

NO = 400
NV = 2400
ROWS = 1024
COL_DEV = 1024
NR = 16384


def with_spikes(result, own_key, source, target, parts, factor):
    owner, partner = [(jnp.arange(result.shape[position]) // (result.shape[position] // parts)).reshape([-1 if axis == position else 1 for axis in range(result.ndim)]) for position in (source, target)]
    chosen = jax.random.permutation(own_key, parts)[partner]
    strong = (owner == chosen) | (owner == (partner + parts // 2) % parts)
    return jnp.where(strong, factor * result, result)


def levels(key, shape, split, smallest, high):
    level, own = 1.0, jax.random.fold_in(key, 6)
    for position, blocks in split:
        heights = jnp.exp(jax.random.uniform(jax.random.fold_in(own, position), (blocks,), jnp.float32, smallest / len(split), high / len(split)))
        level = level * jnp.repeat(heights, shape[position] // blocks).reshape([-1 if axis == position else 1 for axis in range(len(shape))])
    return level


def gaussian(key, extent, deviation, most, split=(), kind=jnp.bfloat16):
    entries = jax.random.normal(key, extent, jnp.float32) * deviation
    if len(split) > 0:
        entries = levels(key, extent, split, -0.22, 0.18) * entries
    return jnp.clip(entries, min=-most, max=most).astype(kind)


def bell_draw_with(rng, extent, scale, reach, split, heavy, kind=jnp.bfloat16):
    result = scale * jax.random.normal(rng, extent, jnp.float32)
    if split:
        result = result * levels(rng, extent, split, -0.22, 0.18)
    return jnp.clip(with_spikes(result, jax.random.fold_in(rng, 3), *heavy), -reach, reach).astype(kind)


def setup_inputs(seed: int = 0) -> dict:
    keys = jax.random.split(jax.random.key(seed), 8)
    return {
        "slab_occ": gaussian(keys[0], (ROWS, NO), 1.0, 6.0, ((0, 16), (1, 2))),
        "slab_vir": gaussian(keys[1], (ROWS, NV), 1.0, 6.0, ((0, 16), (1, 2))),
        "orbitals_occ": gaussian(keys[2], (NO, NR), NO ** -0.5, 0.3125, ((0, 2), (1, 16))),
        "orbitals_vir": gaussian(keys[3], (NV, NR), NV ** -0.5, 0.125, ((0, 2), (1, 16))),
        "occ_energy": jnp.clip(-2.0 + 1.9 * jax.random.uniform(keys[4], (NO,), jnp.float32) ** levels(keys[4], (NO,), ((0, 2),), -0.2, 0.2), -2.0, -0.1),
        "vir_energy": jnp.clip(0.1 + 2.9 * jax.random.uniform(keys[5], (NV,), jnp.float32) ** levels(keys[5], (NV,), ((0, 2),), -0.2, 0.2), 0.1, 3.0),
        "screened": bell_draw_with(keys[6], (ROWS, NR), (80 / NR ** 0.5), 6.0, ((0, 16),), (1, 0, 16, 2.0)),
    }


def reference(slab_occ, slab_vir, orbitals_occ, orbitals_vir, occ_energy, vir_energy, screened):
    scaled_occ = (slab_occ.astype(jnp.float32) * jnp.exp(occ_energy)[None, :]).astype(jnp.bfloat16)
    scaled_vir = (slab_vir.astype(jnp.float32) * jnp.exp(-vir_energy)[None, :]).astype(jnp.bfloat16)
    width = COL_DEV
    count = NR // width

    def advance(carry, index):
        acc_occ, acc_vir = carry
        start = (index * width).astype(jnp.int32)
        occ_cols = lax.dynamic_slice_in_dim(orbitals_occ, start, width, 1)
        vir_cols = lax.dynamic_slice_in_dim(orbitals_vir, start, width, 1)
        screen = lax.dynamic_slice_in_dim(screened, start, width, 1).astype(jnp.float32)
        green_occ = jnp.dot(scaled_occ, occ_cols, preferred_element_type=jnp.float32)
        green_vir = jnp.dot(scaled_vir, vir_cols, preferred_element_type=jnp.float32)
        occ_side = (green_vir * screen).astype(jnp.bfloat16)
        vir_side = (green_occ * screen).astype(jnp.bfloat16)
        dims = (((1,), (1,)), ((), ()))
        acc_occ = acc_occ + lax.dot_general(occ_side, occ_cols, dims, preferred_element_type=jnp.float32)
        acc_vir = acc_vir + lax.dot_general(vir_side, vir_cols, dims, preferred_element_type=jnp.float32)
        return (acc_occ, acc_vir), None

    init = (jnp.zeros((ROWS, NO), jnp.float32), jnp.zeros((ROWS, NV), jnp.float32))
    (acc_occ, acc_vir), unused = lax.scan(advance, init, jnp.arange(count, dtype=jnp.int32))
    return acc_occ.astype(jnp.bfloat16), acc_vir.astype(jnp.bfloat16)
```

```python
import functools

import jax
import jax.numpy as jnp
from jax import lax
from jax.experimental import pallas as pl
from jax.experimental.pallas import tpu as pltpu
from jax.sharding import PartitionSpec as P

MESH = pl.DeviceIdType.MESH
LAGS = (1, 2)
ANY = pl.BlockSpec(memory_space=pl.ANY)
VMEM = pl.BlockSpec(memory_space=pltpu.VMEM)


def place(n_col):
    me = lax.axis_index("col")
    far, mid, core = me // 4, lax.rem(me // 2, 2), lax.rem(me, 2)
    return me, far, mid, core, lambda f, m, c: (f * 2 + m) * 2 + c


def greet(cols, orbs):
    barrier = pltpu.get_barrier_semaphore()
    for col in cols:
        pl.semaphore_signal(barrier, inc=1, device_id={"col": col}, device_id_type=MESH)
    for orb in orbs:
        pl.semaphore_signal(barrier, inc=1, device_id={"orb": orb}, device_id_type=MESH)
    pl.semaphore_wait(barrier, len(cols) + len(orbs))


def sender():
    sends = []

    def push(src, dst, send, recv, device):
        copy = pltpu.make_async_remote_copy(
            src_ref=src, dst_ref=dst, send_sem=send, recv_sem=recv,
            device_id=device, device_id_type=MESH,
        )
        copy.start()
        sends.append(copy)
        return copy

    return sends, push


def landed(ref, send, recv, device):
    pltpu.make_async_remote_copy(
        src_ref=ref, dst_ref=ref, send_sem=send, recv_sem=recv,
        device_id=device, device_id_type=MESH,
    ).wait_recv()


def spread(n_col, push, swap, slab, screen, slabs, screens, local_sem,
           orb_send, slab_send, slab_recv, screen_send, screen_recv):
    n_far = n_col // 4
    me, far, mid, core, index = place(n_col)
    part = lax.axis_index("orb")
    other = 1 - part
    others = [lax.rem(me + d, n_col) for d in range(1, n_col)]

    def arrived(k, col):
        landed(slabs.at[k, col], orb_send.at[swap], slab_recv.at[k, col], {"orb": other})

    counter = [0]

    def give(k, col, target, src=None):
        push(
            slabs.at[k, col] if src is None else src, slabs.at[k, col],
            slab_send.at[counter[0]], slab_recv.at[k, col], {"col": target},
        )
        counter[0] += 1

    x_peer, core_peer = index(far, 1 - mid, core), index(far, mid, 1 - core)
    fars = [lax.rem(far + d, n_far) for d in range(1, n_far)]
    own = slab.at[part]
    targets = [index(f, mid, core) for f in fars] + [x_peer, core_peer]
    for target in targets:
        give(0, me, target, own)
    arrived(1, me)
    for target in targets:
        give(1, me, target)
    for n, p in enumerate(others):
        push(screen.at[p], screens.at[me], screen_send.at[n], screen_recv.at[me], {"col": p})
    local = [
        pltpu.make_async_copy(own, slabs.at[0, me], local_sem.at[0]),
        pltpu.make_async_copy(screen.at[me], screens.at[me], local_sem.at[1]),
    ]
    for copy in local:
        copy.start()
    for f in fars:
        col = index(f, mid, core)
        for k in range(2):
            arrived(k, col)
            give(k, col, x_peer)
            give(k, col, core_peer)
    for f in [far] + fars:
        col = index(f, 1 - mid, core)
        for k in range(2):
            arrived(k, col)
            give(k, col, core_peer)
    for f in [far] + fars:
        for m in (mid, 1 - mid):
            for k in range(2):
                arrived(k, index(f, m, 1 - core))
    for p in others:
        landed(screens.at[p], orb_send.at[swap], screen_recv.at[p], {"orb": other})
    for copy in local:
        copy.wait()


def spread_semaphores(n_col):
    n_far = n_col // 4
    dma = pltpu.SemaphoreType.DMA
    n_give = 2 * ((n_far + 1) + 2 * (n_far - 1) + n_far)
    return [dma((n_give,)), dma((2, n_col)), dma((n_col,)), dma((n_col,))]


def gather_kernel(
    n_col, slab, occ, vir, screen, slabs, peer_occ, peer_vir, screens,
    local_sem, orb_send, orb_recv, slab_send, slab_recv, screen_send, screen_recv,
):
    me = lax.axis_index("col")
    other = 1 - lax.axis_index("orb")
    greet([lax.rem(me + d, n_col) for d in range(1, n_col)], [other])
    sends, push = sender()
    push(slab.at[other], slabs.at[1, me], orb_send.at[2], slab_recv.at[1, me], {"orb": other})
    push(vir, peer_vir, orb_send.at[0], orb_recv.at[0], {"orb": other})
    push(occ, peer_occ, orb_send.at[1], orb_recv.at[1], {"orb": other})
    spread(n_col, push, 2, slab, screen, slabs, screens, local_sem,
           orb_send, slab_send, slab_recv, screen_send, screen_recv)
    for n, ref in ((0, peer_vir), (1, peer_occ)):
        landed(ref, orb_send.at[n], orb_recv.at[n], {"orb": other})
    for copy in sends:
        copy.wait_send()


def gather(n_col, slab, occ, vir, screen):
    dma = pltpu.SemaphoreType.DMA
    return pl.pallas_call(
        functools.partial(gather_kernel, n_col),
        out_shape=(
            jax.ShapeDtypeStruct((2, n_col) + slab.shape[1:], slab.dtype),
            jax.ShapeDtypeStruct(occ.shape, occ.dtype),
            jax.ShapeDtypeStruct(vir.shape, vir.dtype),
            jax.ShapeDtypeStruct(screen.shape, screen.dtype),
        ),
        in_specs=[ANY] * 4,
        out_specs=(ANY,) * 4,
        scratch_shapes=[dma((2,)), dma((3,)), dma((2,))] + spread_semaphores(n_col),
        compiler_params=pltpu.CompilerParams(collective_id=0, has_side_effects=True),
    )(slab, occ, vir, screen)


def reduce_rows(n_col, pieces, ins, refs, ready, finish, flush=()):
    n_far = n_col // 4
    near, out_x, in_x, total, out_far, in_far = [
        refs[i * pieces : (i + 1) * pieces] for i in range(6)
    ]
    near_send, near_recv, x_send, x_recv, far_send, far_recv = refs[6 * pieces :]
    me, far, mid, core, index = place(n_col)
    x_peer, core_peer = index(far, 1 - mid, core), index(far, mid, 1 - core)
    fars = [lax.rem(far + d, n_far) for d in range(1, n_far)]
    sends, push = sender()
    wide = lambda value: value.astype(jnp.float32)
    first, second, third = [], [], []

    def to_core(t):
        ready(t)
        first.append(
            [
                push(
                    ins[t].at[:, m, 1 - core], near[t].at[slot],
                    near_send.at[t, slot], near_recv.at[t, slot], {"col": core_peer},
                )
                for slot, m in ((0, 1 - mid), (1, mid))
            ]
        )

    def to_mid(t):
        first[t][0].wait_recv()
        for f in range(n_far):
            out_x[t][f] = (wide(ins[t][f, 1 - mid, core]) + wide(near[t][0, f])).astype(
                out_x[t].dtype
            )
        second.append(push(out_x[t], in_x[t], x_send.at[t], x_recv.at[t], {"col": x_peer}))
        first[t][1].wait_recv()
        for f in range(n_far):
            total[t][f] = wide(ins[t][f, mid, core]) + wide(near[t][1, f])

    def to_far(t):
        second[t].wait_recv()
        for f in range(n_far):
            total[t][f] = total[t][f] + wide(in_x[t][f])
            out_far[t][f] = total[t][f].astype(out_far[t].dtype)
        for d, f in enumerate(fars):
            third.append(
                push(
                    out_far[t].at[f], in_far[t].at[d],
                    far_send.at[t, d], far_recv.at[t, d], {"col": index(f, mid, core)},
                )
            )

    acts, count = (to_core, to_mid, to_far), [0, 0, 0]

    def advance(stage, end):
        while count[stage] < end:
            acts[stage](count[stage])
            count[stage] += 1

    for t in range(pieces):
        if t in flush:
            advance(1, t)
            advance(2, t)
        advance(0, t + 1)
        advance(1, t + 1 - LAGS[0])
        advance(2, t + 1 - sum(LAGS))
    advance(1, pieces)
    advance(2, pieces)
    for t in range(pieces):
        value = total[t][far]
        for d in range(n_far - 1):
            third[t * (n_far - 1) + d].wait_recv()
            value = value + wide(in_far[t][d])
        finish(t, value)
    for made in sends:
        made.wait_send()


def reduce_scratch(n_col, block, kind):
    n_far = n_col // 4
    dma = pltpu.SemaphoreType.DMA
    pieces = len(block)

    def buffers(lead, dtype=kind):
        return [pltpu.VMEM(lead + tuple(b), dtype) for b in block]

    return (
        buffers((2, n_far))
        + buffers((n_far,))
        + buffers((n_far,))
        + buffers((n_far,), jnp.float32)
        + buffers((n_far,))
        + buffers((n_far - 1,))
        + [
            dma((pieces, 2)), dma((pieces, 2)), dma((pieces,)), dma((pieces,)),
            dma((pieces, n_far - 1)), dma((pieces, n_far - 1)),
        ]
    )


def scatter_kernel(n_col, pieces, *refs):
    me, far, mid, core, index = place(n_col)
    n_far = n_col // 4
    fars = [lax.rem(far + d, n_far) for d in range(1, n_far)]
    greet(
        [index(far, mid, 1 - core), index(far, 1 - mid, core)]
        + [index(f, mid, core) for f in fars],
        [],
    )
    outs = refs[pieces : 2 * pieces]

    def finish(t, value):
        outs[t][...] = value.astype(outs[t].dtype)

    reduce_rows(n_col, pieces, refs[:pieces], refs[2 * pieces :], lambda t: None, finish)


def scatter(n_col, terms):
    pieces = len(terms)
    block, kind = [t.shape[-2:] for t in terms], terms[0].dtype
    return pl.pallas_call(
        functools.partial(scatter_kernel, n_col, pieces),
        out_shape=[jax.ShapeDtypeStruct(b, kind) for b in block],
        in_specs=[VMEM] * pieces,
        out_specs=[VMEM] * pieces,
        scratch_shapes=reduce_scratch(n_col, block, kind),
        compiler_params=pltpu.CompilerParams(collective_id=1, has_side_effects=True),
    )(*terms)


def order(far, j):
    if j == 0:
        return far
    if j == 1:
        return far + 1 - 2 * lax.rem(far, 2)
    return 2 - far // 2 if j == 2 else 3 - 3 * (far // 2)


def fused_kernel(n_col, slab_occ, slab_vir, occ, vir, occ_energy, vir_energy, screen, *refs):
    out_occ, out_vir = refs[:2]
    (raw_occ, raw_vir, e_occ, e_vir, sv, so, ov, od, screens, green, green_out, green_in, side,
     part_vir, part_occ, near_vir, near_occ, out_x_vir, out_x_occ, in_x_vir, in_x_occ,
     sum_vir, sum_occ, out_far_vir, out_far_occ, in_far_vir, in_far_occ,
     end_out_vir, end_out_occ, end_in_vir, end_in_occ) = refs[2:33]
    (load_sem, slab_send, slab_recv, swap_send, swap_recv, screen_send, screen_recv,
     green_send, green_recv, side_send, side_recv, near_send, near_recv, x_send, x_recv,
     far_send, far_recv, end_send, end_recv) = refs[33:]
    n_far = n_col // 4
    me, far, mid, core, index = place(n_col)
    part = lax.axis_index("orb")
    other = 1 - part
    x_peer, core_peer = index(far, 1 - mid, core), index(far, mid, 1 - core)
    diagonal = index(far, 1 - mid, 1 - core)
    inner = lax.rem(far, 3) > 0
    planes = [order(far, j) for j in range(n_far)]
    n_occ = occ.shape[0]
    n_vir = vir.shape[0]
    half = ov.shape[2]
    block = sv.shape[1]
    rows = 4 * block
    kind = sv.dtype
    wide = lambda value: value.astype(jnp.float32)

    def dot(a, b):
        return jnp.dot(a, b, preferred_element_type=jnp.float32)

    def dot_t(a, b):
        return lax.dot_general(a, b, (((1,), (1,)), ((), ())), preferred_element_type=jnp.float32)

    barrier = pltpu.get_barrier_semaphore()
    for d in range(1, n_col):
        pl.semaphore_signal(
            barrier, inc=1, device_id={"col": lax.rem(me + d, n_col)}, device_id_type=MESH
        )
    pl.semaphore_signal(barrier, inc=1, device_id={"orb": other}, device_id_type=MESH)

    def piece(p, k):
        start = p * (2 * half) + k * half
        return screen.at[:, pl.ds(pl.multiple_of(start, half), half)]

    def columns_of(ref, k):
        return ref.at[:, pl.ds(pl.multiple_of(k * half, half), half)]

    loads = [
        pltpu.make_async_copy(src, dst, load_sem.at[n])
        for n, (src, dst) in enumerate(
            (
                (vir_energy, e_vir), (slab_vir, raw_vir), (occ_energy, e_occ), (slab_occ, raw_occ),
                (columns_of(vir, other), ov.at[other, pl.ds(0, n_vir)]),
                (columns_of(vir, part), ov.at[part, pl.ds(0, n_vir)]),
                (columns_of(occ, part), od.at[part, pl.ds(0, n_occ)]),
                (piece(me, part), screens.at[me]),
            )
        )
    ]
    for load in loads:
        load.start()
    for ref, n in ((ov, n_vir), (od, n_occ)):
        short = ref.shape[1] - n
        if short:
            for k in range(2):
                ref[k, pl.ds(n, short)] = jnp.zeros((short, half), kind)
    for load in loads[:4]:
        load.wait()
    sv[me, :, :n_vir] = (wide(raw_vir[...]) * jnp.exp(-e_vir[...])).astype(kind)
    if sv.shape[2] > n_vir:
        sv[me, :, n_vir:] = jnp.zeros((block, sv.shape[2] - n_vir), kind)
    so[me, part, :, :n_occ] = (wide(raw_occ[...]) * jnp.exp(e_occ[...])).astype(kind)
    if so.shape[3] > n_occ:
        so[me, part, :, n_occ:] = jnp.zeros((block, so.shape[3] - n_occ), kind)
    pl.semaphore_wait(barrier, n_col)

    sends = []

    def push(src, dst, send, recv, device, only=None):
        copy = pltpu.make_async_remote_copy(
            src_ref=src, dst_ref=dst, send_sem=send, recv_sem=recv,
            device_id=device, device_id_type=MESH,
        )
        if only is None:
            copy.start()
        else:
            pl.when(only)(copy.start)
        sends.append((only, copy))
        return copy

    slabs = (sv, so)
    counter = [0]

    def give(k, col, target, only=None):
        push(slabs[k].at[col], slabs[k].at[col], slab_send.at[counter[0]], slab_recv.at[k, col],
             {"col": target}, only)
        counter[0] += 1

    def arrived(k, col):
        landed(slabs[k].at[col], swap_send.at[0], slab_recv.at[k, col], {"orb": other})

    def give_own(k):
        give(k, me, x_peer)
        give(k, me, index(planes[1], mid, core))
        give(k, me, index(3 - far, mid, core), inner)
        give(k, me, core_peer)

    def relay(k, j):
        col = index(planes[j], mid, core)
        arrived(k, col)
        step = 3 - far if j == 1 else 3 * far - 3
        give(k, col, index(step, mid, core), inner)
        give(k, col, x_peer)
        give(k, col, core_peer)

    def cross(k, j):
        col = index(planes[j], 1 - mid, core)
        arrived(k, col)
        give(k, col, core_peer)

    def settle(k, j):
        arrived(k, index(planes[j], mid, 1 - core))
        arrived(k, index(planes[j], 1 - mid, 1 - core))

    screen_count = [0]

    def give_screen(target):
        push(piece(target, part), screens.at[me], screen_send.at[screen_count[0]],
             screen_recv.at[me], {"col": target})
        screen_count[0] += 1

    def give_screens(j):
        for m, c in ((mid, core), (1 - mid, core), (mid, 1 - core), (1 - mid, 1 - core)):
            give_screen(index(planes[j], m, c))

    def screened(j):
        for m, c in ((mid, core), (1 - mid, core), (mid, 1 - core), (1 - mid, 1 - core)):
            if j == 0 and m is mid and c is core:
                loads[7].wait()
            else:
                col = index(planes[j], m, c)
                landed(screens.at[col], swap_send.at[0], screen_recv.at[col], {"orb": other})

    def plane(j):
        return pl.ds(planes[j] * 4, 4)

    def shade(j, cut):
        return wide(screens[plane(j), :, cut].reshape((rows, -1)))

    cuts = [slice(start, start + 256) for start in range(0, half, 256)]
    swaps = {}

    def make_green(j):
        slab = sv[plane(j)].reshape((rows, -1))
        for cut in cuts:
            green_out[j, :, cut] = dot(slab, ov[other, :, cut]).astype(kind)
        swaps["green", j] = push(green_out.at[j], green_in.at[j], green_send.at[j],
                                 green_recv.at[j], {"orb": other})
        for cut in cuts:
            green[j, :, cut] = dot(slab, ov[part, :, cut])

    def make_side(j):
        for cut in cuts:
            value = dot(so[plane(j), 0].reshape((rows, -1)), od[0, :, cut])
            value = value + dot(so[plane(j), 1].reshape((rows, -1)), od[1, :, cut])
            side[j, part, :, cut] = (value * shade(j, cut)).astype(kind)
        swaps["side", j] = push(side.at[j, part], side.at[j, part], side_send.at[j],
                                side_recv.at[j], {"orb": other})

    class Reduce:
        def __init__(self, n, part, near, out_x, in_x, total, out_far, in_far, end_out, end_in):
            self.n, self.part, self.near, self.out_x, self.in_x = n, part, near, out_x, in_x
            self.total, self.out_far, self.in_far = total, out_far, in_far
            self.end_out, self.end_in = end_out, end_in
            self.first, self.second, self.third = {}, {}, {}

        def to_core(self, j):
            n = self.n
            self.first[j] = [
                push(self.part.at[j, m, 1 - core], self.near.at[j, slot],
                     near_send.at[n, j, slot], near_recv.at[n, j, slot], {"col": core_peer})
                for slot, m in ((0, 1 - mid), (1, mid))
            ]

        def to_mid(self, j):
            n = self.n
            self.first[j][0].wait_recv()
            self.out_x[j] = (wide(self.part[j, 1 - mid, core]) + wide(self.near[j, 0])).astype(kind)
            self.second[j] = push(self.out_x.at[j], self.in_x.at[j], x_send.at[n, j],
                                  x_recv.at[n, j], {"col": x_peer})
            self.first[j][1].wait_recv()
            self.total[j] = wide(self.part[j, mid, core]) + wide(self.near[j, 1])

        def to_far(self, j):
            n = self.n
            self.second[j].wait_recv()
            value = self.total[j] + wide(self.in_x[j])
            if j == 0:
                self.total[0] = value
            else:
                self.out_far[j - 1] = value.astype(kind)
                push(self.out_far.at[j - 1], self.in_far.at[far], far_send.at[n, j - 1],
                     far_recv.at[n, far], {"col": index(planes[j], mid, core)})

        def gather(self):
            n = self.n
            value = self.total[0]
            for j in range(1, n_far):
                source = planes[j]
                landed(self.in_far.at[source], swap_send.at[0], far_recv.at[n, source], {"orb": other})
                value = value + wide(self.in_far[source])
            self.total[0] = value
            lines = block // 2
            mine = pl.ds(pl.multiple_of(part * lines, lines), lines)
            theirs = pl.ds(pl.multiple_of(other * lines, lines), lines)
            self.end_out[...] = self.total[0, theirs].astype(kind)
            self.last = push(self.end_out, self.end_in, end_send.at[n], end_recv.at[n], {"orb": other})
            self.mine = mine

        def end(self):
            self.last.wait_recv()
            return self.total[0, self.mine], wide(self.end_in[...])

    of_vir = Reduce(0, part_vir, near_vir, out_x_vir, in_x_vir, sum_vir, out_far_vir, in_far_vir,
                    end_out_vir, end_in_vir)
    of_occ = Reduce(1, part_occ, near_occ, out_x_occ, in_x_occ, sum_occ, out_far_occ, in_far_occ,
                    end_out_occ, end_in_occ)

    def project_vir(j):
        swaps["side", j].wait_recv()
        width = part_vir.shape[-1]
        for start in range(0, width, 256):
            cut = slice(start, min(start + 256, width))
            term = dot_t(side[j, 0], ov[0, cut]) + dot_t(side[j, 1], ov[1, cut])
            part_vir[j, :, :, :, cut] = term.astype(kind).reshape((2, 2, block, -1))
        of_vir.to_core(j)

    def project_occ(j):
        swaps["green", j].wait_recv()
        value = (green[j] + wide(green_in[j])) * shade(j, slice(0, half))
        value = value.astype(kind)
        wide_occ = od.shape[1]
        for k in range(2):
            term = dot_t(value, od[k]).astype(kind)
            part_occ[j, :, :, :, slice(k * wide_occ, (k + 1) * wide_occ)] = term.reshape(
                (2, 2, block, -1)
            )
        of_occ.to_core(j)

    push(so.at[me, part], so.at[me, part], swap_send.at[0], swap_recv.at[0], {"orb": other})
    swap = push(columns_of(occ, other), od.at[part, pl.ds(0, n_occ)], swap_send.at[1],
                swap_recv.at[1], {"orb": other})
    give_own(0)
    for target in (x_peer, core_peer, diagonal):
        give_screen(target)
    give_screens(1)
    landed(so.at[me, other], swap_send.at[0], swap_recv.at[0], {"orb": other})
    give_own(1)
    for load in loads[4:7]:
        load.wait()
    cross(0, 0)
    relay(0, 1)
    settle(0, 0)
    make_green(0)
    cross(1, 0)
    relay(1, 1)
    give_screens(2)
    settle(1, 0)
    screened(0)
    swap.wait_recv()
    make_side(0)
    relay(0, 2)
    relay(1, 2)
    give_screens(3)
    cross(0, 1)
    settle(0, 1)
    make_green(1)
    cross(1, 1)
    settle(1, 1)
    screened(1)
    make_side(1)
    relay(0, 3)
    relay(1, 3)
    cross(0, 2)
    cross(1, 2)
    settle(0, 2)
    make_green(2)
    project_vir(0)
    project_occ(0)
    settle(1, 2)
    of_vir.to_mid(0)
    screened(2)
    make_side(2)
    of_occ.to_mid(0)
    cross(0, 3)
    cross(1, 3)
    settle(0, 3)
    settle(1, 3)
    screened(3)
    make_side(3)
    make_green(3)
    of_vir.to_far(0)
    of_occ.to_far(0)
    for j in range(1, n_far):
        vir_first = j < n_far - 1
        acts = [(project_vir, of_vir), (project_occ, of_occ)]
        for act, _ in acts:
            act(j)
        for _, reduce in acts:
            if j > 1:
                reduce.to_far(j - 1)
            reduce.to_mid(j)
    for reduce in (of_vir, of_occ):
        reduce.to_far(n_far - 1)
    of_vir.gather()
    of_occ.gather()
    low = part == 0
    own, peer = of_vir.end()
    own, peer = own[:, :n_vir], peer[:, :n_vir]
    out_vir[:, :n_vir] = jnp.where(low, own, peer).astype(kind)
    out_vir[:, n_vir:] = jnp.where(low, peer, own).astype(kind)
    own, peer = of_occ.end()
    value = own + peer
    wide_occ = od.shape[1]
    out_occ[:, :n_occ] = value[:, :n_occ].astype(kind)
    out_occ[:, n_occ:] = value[:, wide_occ : wide_occ + n_occ].astype(kind)
    for only, copy in sends:
        if only is None:
            copy.wait_send()
        else:
            pl.when(only)(copy.wait_send)


def fused(n_col, slab_occ, slab_vir, occ, vir, occ_energy, vir_energy, screen):
    up = lambda n: -(-n // 128) * 128
    block = slab_occ.shape[0]
    n_occ, columns = occ.shape
    n_vir = vir.shape[0]
    kind, f32 = slab_occ.dtype, jnp.float32
    half = columns // 2
    wide_occ, wide_vir = up(n_occ), up(n_vir)
    n_far = n_col // 4
    rows = 4 * block
    both = 2 * wide_occ
    dma = pltpu.SemaphoreType.DMA

    def pair(lead, lines, dtype=kind):
        return [pltpu.VMEM(lead + (lines, w), dtype) for w in (wide_vir, both)]

    return pl.pallas_call(
        functools.partial(fused_kernel, n_col),
        out_shape=[
            jax.ShapeDtypeStruct((block // 2, 2 * n), kind) for n in (n_occ, n_vir)
        ],
        in_specs=[ANY] * 7,
        out_specs=[VMEM] * 2,
        scratch_shapes=[
            pltpu.VMEM(slab_occ.shape, kind),
            pltpu.VMEM(slab_vir.shape, kind),
            pltpu.VMEM(occ_energy.shape, f32),
            pltpu.VMEM(vir_energy.shape, f32),
            pltpu.VMEM((n_col, block, wide_vir), kind),
            pltpu.VMEM((n_col, 2, block, wide_occ), kind),
            pltpu.VMEM((2, wide_vir, half), kind),
            pltpu.VMEM((2, wide_occ, half), kind),
            pltpu.VMEM((n_col, block, half), kind),
            pltpu.VMEM((n_far, rows, half), f32),
            pltpu.VMEM((n_far, rows, half), kind),
            pltpu.VMEM((n_far, rows, half), kind),
            pltpu.VMEM((n_far, 2, rows, half), kind),
        ]
        + pair((n_far, 2, 2), block)
        + pair((n_far, 2), block)
        + pair((n_far,), block)
        + pair((n_far,), block)
        + pair((n_far,), block, f32)
        + pair((n_far - 1,), block)
        + pair((n_far,), block)
        + pair((), block // 2)
        + pair((), block // 2)
        + [
            dma((8,)), dma((34,)), dma((2, n_col)), dma((2,)), dma((2,)), dma((n_col,)), dma((n_col,)),
            dma((n_far,)), dma((n_far,)), dma((n_far,)), dma((n_far,)),
            dma((2, n_far, 2)), dma((2, n_far, 2)), dma((2, n_far)), dma((2, n_far)),
            dma((2, n_far - 1)), dma((2, n_far)), dma((2,)), dma((2,)),
        ],
        compiler_params=pltpu.CompilerParams(collective_id=2, has_side_effects=True),
    )(slab_occ, slab_vir, occ, vir, occ_energy, vir_energy, screen)


def local(slab_occ, slab_vir, orbitals_occ, orbitals_vir, occ_energy, vir_energy, screened):
    n_orb, n_col = lax.axis_size("orb"), lax.axis_size("col")
    part = lax.axis_index("orb")
    block = slab_occ.shape[0] // n_orb
    n_occ, columns = orbitals_occ.shape
    n_vir = orbitals_vir.shape[0]
    kind = slab_occ.dtype
    if n_col == 16 and n_orb == 2 and block % 16 == 0 and columns % 512 == 0:
        return tuple(
            fused(
                n_col, slab_occ, slab_vir, orbitals_occ, orbitals_vir,
                occ_energy[None, :], vir_energy[None, :], screened,
            )
        )
    up = lambda n: -(-n // 128) * 128
    scaled_occ = (slab_occ.astype(jnp.float32) * jnp.exp(occ_energy)[None, :]).astype(kind)
    scaled_vir = (slab_vir.astype(jnp.float32) * jnp.exp(-vir_energy)[None, :]).astype(kind)
    start = up(n_vir)
    slab = jnp.concatenate(
        [
            jnp.pad(scaled_vir, ((0, 0), (0, start - n_vir))),
            jnp.pad(scaled_occ, ((0, 0), (0, up(n_occ) - n_occ))),
        ],
        axis=1,
    ).reshape((n_orb, block, start + up(n_occ)))
    mine = lax.dynamic_slice_in_dim(screened, part * block, block, 0)
    mine = mine.reshape((block, n_col, columns)).transpose((1, 0, 2))

    def order(own, peer, n):
        own, peer = own[:, :n], peer[:, :n]
        return jnp.where(
            part == 0, jnp.concatenate([own, peer], 1), jnp.concatenate([peer, own], 1)
        )

    slabs, peer_occ, peer_vir, screens = gather(n_col, slab, orbitals_occ, orbitals_vir, mine)
    slabs = slabs.reshape((2, n_col * block, slab.shape[2]))
    own_slab, peer_slab = slabs[0], slabs[1]

    def dot(a, b):
        return jnp.dot(a, b, preferred_element_type=jnp.float32)

    green_vir = dot(own_slab[:, :n_vir], orbitals_vir) + dot(peer_slab[:, :n_vir], peer_vir)
    green_occ = dot(own_slab[:, start : start + n_occ], orbitals_occ) + dot(
        peer_slab[:, start : start + n_occ], peer_occ
    )
    screen = screens.reshape((n_col * block, columns)).astype(jnp.float32)
    occ_side = (green_vir * screen).astype(kind)
    vir_side = (green_occ * screen).astype(kind)
    dims = (((1,), (1,)), ((), ()))

    def project(side, orbitals):
        term = lax.dot_general(side, orbitals, dims, preferred_element_type=jnp.float32)
        return term.astype(kind).reshape((n_col // 4, 2, 2, block, orbitals.shape[0]))

    vir_own, vir_peer, occ_own, occ_peer = scatter(
        n_col,
        [
            project(vir_side, orbitals_vir),
            project(vir_side, peer_vir),
            project(occ_side, orbitals_occ),
            project(occ_side, peer_occ),
        ],
    )

    return order(occ_own, occ_peer, n_occ), order(vir_own, vir_peer, n_vir)


def solution(mesh):
    return jax.shard_map(
        local,
        mesh=mesh,
        in_specs=(
            P("col", "orb"),
            P("col", "orb"),
            P("orb", "col"),
            P("orb", "col"),
            P("orb"),
            P("orb"),
            P("col", None),
        ),
        out_specs=(P(("col", "orb"), None), P(("col", "orb"), None)),
        check_vma=False,
    )
```

```python
import functools

import jax
import jax.numpy as jnp
from jax import lax
from jax.experimental import pallas as pl
from jax.experimental.pallas import tpu as pltpu
from jax.sharding import PartitionSpec as P

MESH = pl.DeviceIdType.MESH
LAGS = (1, 2)
ANY = pl.BlockSpec(memory_space=pl.ANY)
VMEM = pl.BlockSpec(memory_space=pltpu.VMEM)


def place(n_col):
    me = lax.axis_index("col")
    far, mid, core = me // 4, lax.rem(me // 2, 2), lax.rem(me, 2)
    return me, far, mid, core, lambda f, m, c: (f * 2 + m) * 2 + c


def greet(cols, orbs):
    barrier = pltpu.get_barrier_semaphore()
    for col in cols:
        pl.semaphore_signal(barrier, inc=1, device_id={"col": col}, device_id_type=MESH)
    for orb in orbs:
        pl.semaphore_signal(barrier, inc=1, device_id={"orb": orb}, device_id_type=MESH)
    pl.semaphore_wait(barrier, len(cols) + len(orbs))


def sender():
    sends = []

    def push(src, dst, send, recv, device):
        copy = pltpu.make_async_remote_copy(
            src_ref=src, dst_ref=dst, send_sem=send, recv_sem=recv,
            device_id=device, device_id_type=MESH,
        )
        copy.start()
        sends.append(copy)
        return copy

    return sends, push


def landed(ref, send, recv, device):
    pltpu.make_async_remote_copy(
        src_ref=ref, dst_ref=ref, send_sem=send, recv_sem=recv,
        device_id=device, device_id_type=MESH,
    ).wait_recv()


def spread(n_col, push, swap, slab, screen, slabs, screens, local_sem,
           orb_send, slab_send, slab_recv, screen_send, screen_recv):
    n_far = n_col // 4
    me, far, mid, core, index = place(n_col)
    part = lax.axis_index("orb")
    other = 1 - part
    others = [lax.rem(me + d, n_col) for d in range(1, n_col)]

    def arrived(k, col):
        landed(slabs.at[k, col], orb_send.at[swap], slab_recv.at[k, col], {"orb": other})

    counter = [0]

    def give(k, col, target, src=None):
        push(
            slabs.at[k, col] if src is None else src, slabs.at[k, col],
            slab_send.at[counter[0]], slab_recv.at[k, col], {"col": target},
        )
        counter[0] += 1

    x_peer, core_peer = index(far, 1 - mid, core), index(far, mid, 1 - core)
    fars = [lax.rem(far + d, n_far) for d in range(1, n_far)]
    own = slab.at[part]
    targets = [index(f, mid, core) for f in fars] + [x_peer, core_peer]
    for target in targets:
        give(0, me, target, own)
    arrived(1, me)
    for target in targets:
        give(1, me, target)
    for n, p in enumerate(others):
        push(screen.at[p], screens.at[me], screen_send.at[n], screen_recv.at[me], {"col": p})
    local = [
        pltpu.make_async_copy(own, slabs.at[0, me], local_sem.at[0]),
        pltpu.make_async_copy(screen.at[me], screens.at[me], local_sem.at[1]),
    ]
    for copy in local:
        copy.start()
    for f in fars:
        col = index(f, mid, core)
        for k in range(2):
            arrived(k, col)
            give(k, col, x_peer)
            give(k, col, core_peer)
    for f in [far] + fars:
        col = index(f, 1 - mid, core)
        for k in range(2):
            arrived(k, col)
            give(k, col, core_peer)
    for f in [far] + fars:
        for m in (mid, 1 - mid):
            for k in range(2):
                arrived(k, index(f, m, 1 - core))
    for p in others:
        landed(screens.at[p], orb_send.at[swap], screen_recv.at[p], {"orb": other})
    for copy in local:
        copy.wait()


def spread_semaphores(n_col):
    n_far = n_col // 4
    dma = pltpu.SemaphoreType.DMA
    n_give = 2 * ((n_far + 1) + 2 * (n_far - 1) + n_far)
    return [dma((n_give,)), dma((2, n_col)), dma((n_col,)), dma((n_col,))]


def gather_kernel(
    n_col, slab, occ, vir, screen, slabs, peer_occ, peer_vir, screens,
    local_sem, orb_send, orb_recv, slab_send, slab_recv, screen_send, screen_recv,
):
    me = lax.axis_index("col")
    other = 1 - lax.axis_index("orb")
    greet([lax.rem(me + d, n_col) for d in range(1, n_col)], [other])
    sends, push = sender()
    push(slab.at[other], slabs.at[1, me], orb_send.at[2], slab_recv.at[1, me], {"orb": other})
    push(vir, peer_vir, orb_send.at[0], orb_recv.at[0], {"orb": other})
    push(occ, peer_occ, orb_send.at[1], orb_recv.at[1], {"orb": other})
    spread(n_col, push, 2, slab, screen, slabs, screens, local_sem,
           orb_send, slab_send, slab_recv, screen_send, screen_recv)
    for n, ref in ((0, peer_vir), (1, peer_occ)):
        landed(ref, orb_send.at[n], orb_recv.at[n], {"orb": other})
    for copy in sends:
        copy.wait_send()


def gather(n_col, slab, occ, vir, screen):
    dma = pltpu.SemaphoreType.DMA
    return pl.pallas_call(
        functools.partial(gather_kernel, n_col),
        out_shape=(
            jax.ShapeDtypeStruct((2, n_col) + slab.shape[1:], slab.dtype),
            jax.ShapeDtypeStruct(occ.shape, occ.dtype),
            jax.ShapeDtypeStruct(vir.shape, vir.dtype),
            jax.ShapeDtypeStruct(screen.shape, screen.dtype),
        ),
        in_specs=[ANY] * 4,
        out_specs=(ANY,) * 4,
        scratch_shapes=[dma((2,)), dma((3,)), dma((2,))] + spread_semaphores(n_col),
        compiler_params=pltpu.CompilerParams(collective_id=0, has_side_effects=True),
    )(slab, occ, vir, screen)


def reduce_rows(n_col, pieces, ins, refs, ready, finish, flush=()):
    n_far = n_col // 4
    near, out_x, in_x, total, out_far, in_far = [
        refs[i * pieces : (i + 1) * pieces] for i in range(6)
    ]
    near_send, near_recv, x_send, x_recv, far_send, far_recv = refs[6 * pieces :]
    me, far, mid, core, index = place(n_col)
    x_peer, core_peer = index(far, 1 - mid, core), index(far, mid, 1 - core)
    fars = [lax.rem(far + d, n_far) for d in range(1, n_far)]
    sends, push = sender()
    wide = lambda value: value.astype(jnp.float32)
    first, second, third = [], [], []

    def to_core(t):
        ready(t)
        first.append(
            [
                push(
                    ins[t].at[:, m, 1 - core], near[t].at[slot],
                    near_send.at[t, slot], near_recv.at[t, slot], {"col": core_peer},
                )
                for slot, m in ((0, 1 - mid), (1, mid))
            ]
        )

    def to_mid(t):
        first[t][0].wait_recv()
        for f in range(n_far):
            out_x[t][f] = (wide(ins[t][f, 1 - mid, core]) + wide(near[t][0, f])).astype(
                out_x[t].dtype
            )
        second.append(push(out_x[t], in_x[t], x_send.at[t], x_recv.at[t], {"col": x_peer}))
        first[t][1].wait_recv()
        for f in range(n_far):
            total[t][f] = wide(ins[t][f, mid, core]) + wide(near[t][1, f])

    def to_far(t):
        second[t].wait_recv()
        for f in range(n_far):
            total[t][f] = total[t][f] + wide(in_x[t][f])
            out_far[t][f] = total[t][f].astype(out_far[t].dtype)
        for d, f in enumerate(fars):
            third.append(
                push(
                    out_far[t].at[f], in_far[t].at[d],
                    far_send.at[t, d], far_recv.at[t, d], {"col": index(f, mid, core)},
                )
            )

    acts, count = (to_core, to_mid, to_far), [0, 0, 0]

    def advance(stage, end):
        while count[stage] < end:
            acts[stage](count[stage])
            count[stage] += 1

    for t in range(pieces):
        if t in flush:
            advance(1, t)
            advance(2, t)
        advance(0, t + 1)
        advance(1, t + 1 - LAGS[0])
        advance(2, t + 1 - sum(LAGS))
    advance(1, pieces)
    advance(2, pieces)
    for t in range(pieces):
        value = total[t][far]
        for d in range(n_far - 1):
            third[t * (n_far - 1) + d].wait_recv()
            value = value + wide(in_far[t][d])
        finish(t, value)
    for made in sends:
        made.wait_send()


def reduce_scratch(n_col, block, kind):
    n_far = n_col // 4
    dma = pltpu.SemaphoreType.DMA
    pieces = len(block)

    def buffers(lead, dtype=kind):
        return [pltpu.VMEM(lead + tuple(b), dtype) for b in block]

    return (
        buffers((2, n_far))
        + buffers((n_far,))
        + buffers((n_far,))
        + buffers((n_far,), jnp.float32)
        + buffers((n_far,))
        + buffers((n_far - 1,))
        + [
            dma((pieces, 2)), dma((pieces, 2)), dma((pieces,)), dma((pieces,)),
            dma((pieces, n_far - 1)), dma((pieces, n_far - 1)),
        ]
    )


def scatter_kernel(n_col, pieces, *refs):
    me, far, mid, core, index = place(n_col)
    n_far = n_col // 4
    fars = [lax.rem(far + d, n_far) for d in range(1, n_far)]
    greet(
        [index(far, mid, 1 - core), index(far, 1 - mid, core)]
        + [index(f, mid, core) for f in fars],
        [],
    )
    outs = refs[pieces : 2 * pieces]

    def finish(t, value):
        outs[t][...] = value.astype(outs[t].dtype)

    reduce_rows(n_col, pieces, refs[:pieces], refs[2 * pieces :], lambda t: None, finish)


def scatter(n_col, terms):
    pieces = len(terms)
    block, kind = [t.shape[-2:] for t in terms], terms[0].dtype
    return pl.pallas_call(
        functools.partial(scatter_kernel, n_col, pieces),
        out_shape=[jax.ShapeDtypeStruct(b, kind) for b in block],
        in_specs=[VMEM] * pieces,
        out_specs=[VMEM] * pieces,
        scratch_shapes=reduce_scratch(n_col, block, kind),
        compiler_params=pltpu.CompilerParams(collective_id=1, has_side_effects=True),
    )(*terms)


def order(far, j):
    if j == 0:
        return far
    if j == 1:
        return far + 1 - 2 * lax.rem(far, 2)
    return lax.rem(far + 2, 4) if j == 2 else 3 - far


def fused_kernel(n_col, slab_occ, slab_vir, occ, vir, occ_energy, vir_energy, screen, *refs):
    out_occ, out_vir = refs[:2]
    (raw_occ, raw_vir, e_occ, e_vir, sv, so, ov, od, screens, green, green_out, green_in, side,
     part_vir, part_occ, near_vir, near_occ, out_x_vir, out_x_occ, in_x_vir, in_x_occ,
     sum_vir, sum_occ, out_far_vir, out_far_occ, in_far_vir, in_far_occ,
     end_out_vir, end_out_occ, end_in_vir, end_in_occ) = refs[2:33]
    (load_sem, slab_send, slab_recv, swap_send, swap_recv, screen_send, screen_recv,
     green_send, green_recv, side_send, side_recv, near_send, near_recv, x_send, x_recv,
     far_send, far_recv, end_send, end_recv) = refs[33:]
    n_far = n_col // 4
    me, far, mid, core, index = place(n_col)
    part = lax.axis_index("orb")
    other = 1 - part
    x_peer, core_peer = index(far, 1 - mid, core), index(far, mid, 1 - core)
    other_mid = 1 - mid
    diagonal = index(far, other_mid, 1 - core)
    inner = lax.rem(far, 3) > 0
    outer = lax.rem(far, 3) == 0
    planes = [order(far, j) for j in range(n_far)]
    n_occ = occ.shape[0]
    n_vir = vir.shape[0]
    half = ov.shape[2]
    block = sv.shape[1]
    rows = 4 * block
    kind = sv.dtype
    wide = lambda value: value.astype(jnp.float32)

    def dot(a, b):
        return jnp.dot(a, b, preferred_element_type=jnp.float32)

    def dot_t(a, b):
        return lax.dot_general(a, b, (((1,), (1,)), ((), ())), preferred_element_type=jnp.float32)

    barrier = pltpu.get_barrier_semaphore()
    for d in range(1, n_col):
        pl.semaphore_signal(
            barrier, inc=1, device_id={"col": lax.rem(me + d, n_col)}, device_id_type=MESH
        )
    pl.semaphore_signal(barrier, inc=1, device_id={"orb": other}, device_id_type=MESH)

    def piece(p, k):
        start = p * (2 * half) + k * half
        return screen.at[:, pl.ds(pl.multiple_of(start, half), half)]

    def columns_of(ref, k):
        return ref.at[:, pl.ds(pl.multiple_of(k * half, half), half)]

    loads = [
        pltpu.make_async_copy(src, dst, load_sem.at[n])
        for n, (src, dst) in enumerate(
            (
                (vir_energy, e_vir), (slab_vir, raw_vir), (occ_energy, e_occ), (slab_occ, raw_occ),
                (columns_of(vir, other), ov.at[other, pl.ds(0, n_vir)]),
                (columns_of(vir, part), ov.at[part, pl.ds(0, n_vir)]),
                (columns_of(occ, part), od.at[part, pl.ds(0, n_occ)]),
                (piece(me, part), screens.at[me]),
            )
        )
    ]
    for load in loads:
        load.start()
    for ref, n in ((ov, n_vir), (od, n_occ)):
        short = ref.shape[1] - n
        if short:
            for k in range(2):
                ref[k, pl.ds(n, short)] = jnp.zeros((short, half), kind)
    for load in loads[:4]:
        load.wait()
    sv[me, :, :n_vir] = (wide(raw_vir[...]) * jnp.exp(-e_vir[...])[None, :]).astype(kind)
    if sv.shape[2] > n_vir:
        sv[me, :, n_vir:] = jnp.zeros((block, sv.shape[2] - n_vir), kind)
    so[me, part, :, :n_occ] = (wide(raw_occ[...]) * jnp.exp(e_occ[...])[None, :]).astype(kind)
    if so.shape[3] > n_occ:
        so[me, part, :, n_occ:] = jnp.zeros((block, so.shape[3] - n_occ), kind)
    pl.semaphore_wait(barrier, n_col)

    sends = []

    def push(src, dst, send, recv, device, only=None):
        copy = pltpu.make_async_remote_copy(
            src_ref=src, dst_ref=dst, send_sem=send, recv_sem=recv,
            device_id=device, device_id_type=MESH,
        )
        if only is None:
            copy.start()
        else:
            pl.when(only)(copy.start)
        sends.append((only, copy))
        return copy

    slabs = (sv, so)
    counter = [0]

    def give(k, col, target, only=None):
        push(slabs[k].at[col], slabs[k].at[col], slab_send.at[counter[0]], slab_recv.at[k, col],
             {"col": target}, only)
        counter[0] += 1

    def arrived(k, col, only=None):
        def act():
            landed(slabs[k].at[col], swap_send.at[0], slab_recv.at[k, col], {"orb": other})

        act() if only is None else pl.when(only)(act)

    def give_own(k):
        give(k, me, x_peer)
        give(k, me, index(planes[1], mid, core))
        give(k, me, index(planes[3], mid, core), inner)
        give(k, me, core_peer)

    def relay(k, j, only=None):
        col = index(planes[j], mid, core)
        arrived(k, col, only)
        step = planes[3 if j == 1 else 1]
        if only is not outer:
            give(k, col, index(step, mid, core), inner)
        give(k, col, x_peer, only)
        give(k, col, core_peer, only)

    def cross(k, j):
        col = index(planes[j], 1 - mid, core)
        arrived(k, col)
        give(k, col, core_peer)

    def settle(k, j):
        arrived(k, index(planes[j], mid, 1 - core))
        arrived(k, index(planes[j], 1 - mid, 1 - core))

    screen_count = [0]

    def give_screen(target):
        push(piece(target, part), screens.at[me], screen_send.at[screen_count[0]],
             screen_recv.at[me], {"col": target})
        screen_count[0] += 1

    def give_screens(j):
        for m, c in ((mid, core), (1 - mid, core), (mid, 1 - core), (1 - mid, 1 - core)):
            give_screen(index(planes[j], m, c))

    def screened(j):
        for m, c in ((mid, core), (1 - mid, core), (mid, 1 - core), (1 - mid, 1 - core)):
            if j == 0 and m is mid and c is core:
                loads[7].wait()
            else:
                col = index(planes[j], m, c)
                landed(screens.at[col], swap_send.at[0], screen_recv.at[col], {"orb": other})

    def plane(j):
        return pl.ds(planes[j] * 4, 4)

    def shade(j, cut):
        return wide(screens[plane(j), :, cut].reshape((rows, -1)))

    cuts = [slice(start, start + 256) for start in range(0, half, 256)]
    swaps = {}

    def chip(m):
        return pl.ds(planes[0] * 4 + 2 * m, 2), pl.ds(pl.multiple_of(m * (2 * block), 2 * block), 2 * block)

    def make_green(j, m=None):
        owners, lines = (plane(j), pl.ds(0, rows)) if m is None else chip(m)
        slot = j if m is not other_mid else n_far
        slab = sv[owners].reshape((-1, sv.shape[2]))
        for cut in cuts:
            green_out[j, lines, cut] = dot(slab, ov[other, :, cut]).astype(kind)
        swaps["green", slot] = push(green_out.at[j, lines], green_in.at[j, lines], green_send.at[slot],
                                    green_recv.at[slot], {"orb": other})
        for cut in cuts:
            green[j, lines, cut] = dot(slab, ov[part, :, cut])

    def make_side(j):
        for cut in cuts:
            value = dot(so[plane(j), 0].reshape((rows, -1)), od[0, :, cut])
            value = value + dot(so[plane(j), 1].reshape((rows, -1)), od[1, :, cut])
            side[j, part, :, cut] = (value * shade(j, cut)).astype(kind)
        swaps["side", j] = push(side.at[j, part], side.at[j, part], side_send.at[j],
                                side_recv.at[j], {"orb": other})

    class Reduce:
        def __init__(self, n, part, near, out_x, in_x, total, out_far, in_far, end_out, end_in):
            self.n, self.part, self.near, self.out_x, self.in_x = n, part, near, out_x, in_x
            self.total, self.out_far, self.in_far = total, out_far, in_far
            self.end_out, self.end_in = end_out, end_in
            self.first, self.second, self.third = {}, {}, {}

        def to_core(self, j, slots=(0, 1)):
            n = self.n
            for slot in slots:
                m = (other_mid, mid)[slot]
                self.first[j, slot] = push(
                    self.part.at[j, m, 1 - core], self.near.at[j, slot],
                    near_send.at[n, j, slot], near_recv.at[n, j, slot], {"col": core_peer},
                )

        def to_mid(self, j):
            n = self.n
            self.first[j, 0].wait_recv()
            self.out_x[j] = (wide(self.part[j, 1 - mid, core]) + wide(self.near[j, 0])).astype(kind)
            self.second[j] = push(self.out_x.at[j], self.in_x.at[j], x_send.at[n, j],
                                  x_recv.at[n, j], {"col": x_peer})
            self.first[j, 1].wait_recv()
            self.total[j] = wide(self.part[j, mid, core]) + wide(self.near[j, 1])

        def to_far(self, j):
            n = self.n
            self.second[j].wait_recv()
            value = self.total[j] + wide(self.in_x[j])
            if j == 0:
                self.total[0] = value
            else:
                self.out_far[j - 1] = value.astype(kind)
                push(self.out_far.at[j - 1], self.in_far.at[far], far_send.at[n, j - 1],
                     far_recv.at[n, far], {"col": index(planes[j], mid, core)})

        def gather(self):
            n = self.n
            value = self.total[0]
            for j in range(1, n_far):
                source = planes[j]
                landed(self.in_far.at[source], swap_send.at[0], far_recv.at[n, source], {"orb": other})
                value = value + wide(self.in_far[source])
            self.total[0] = value
            lines = block // 2
            mine = pl.ds(pl.multiple_of(part * lines, lines), lines)
            theirs = pl.ds(pl.multiple_of(other * lines, lines), lines)
            self.end_out[...] = self.total[0, theirs].astype(kind)
            self.last = push(self.end_out, self.end_in, end_send.at[n], end_recv.at[n], {"orb": other})
            self.mine = mine

        def end(self):
            self.last.wait_recv()
            return self.total[0, self.mine], wide(self.end_in[...])

    of_vir = Reduce(0, part_vir, near_vir, out_x_vir, in_x_vir, sum_vir, out_far_vir, in_far_vir,
                    end_out_vir, end_in_vir)
    of_occ = Reduce(1, part_occ, near_occ, out_x_occ, in_x_occ, sum_occ, out_far_occ, in_far_occ,
                    end_out_occ, end_in_occ)

    def project_vir(j):
        swaps["side", j].wait_recv()
        width = part_vir.shape[-1]
        for start in range(0, width, 256):
            cut = slice(start, min(start + 256, width))
            term = dot_t(side[j, 0], ov[0, cut]) + dot_t(side[j, 1], ov[1, cut])
            part_vir[j, :, :, :, cut] = term.astype(kind).reshape((2, 2, block, -1))
        of_vir.to_core(j)

    def project_occ(j, m=None):
        slot = j if m is not other_mid else n_far
        swaps["green", slot].wait_recv()
        owners, lines = (plane(j), pl.ds(0, rows)) if m is None else chip(m)
        shades = wide(screens[owners].reshape((-1, half)))
        value = (green[j, lines] + wide(green_in[j, lines])) * shades
        value = value.astype(kind)
        wide_occ = od.shape[1]
        for k in range(2):
            term = dot_t(value, od[k]).astype(kind).reshape((-1, 2, block, wide_occ))
            cut = slice(k * wide_occ, (k + 1) * wide_occ)
            if m is None:
                part_occ[j, :, :, :, cut] = term
            else:
                part_occ[j, m, :, :, cut] = term[0]
        of_occ.to_core(j, (0, 1) if m is None else (0,) if m is other_mid else (1,))

    push(so.at[me, part], so.at[me, part], swap_send.at[0], swap_recv.at[0], {"orb": other})
    swap = push(columns_of(occ, other), od.at[part, pl.ds(0, n_occ)], swap_send.at[1],
                swap_recv.at[1], {"orb": other})
    give_own(0)
    for load in loads[4:7]:
        load.wait()
    arrived(0, core_peer)
    make_green(0, mid)
    landed(so.at[me, other], swap_send.at[0], swap_recv.at[0], {"orb": other})
    give_own(1)
    for target in (x_peer, core_peer, diagonal):
        give_screen(target)
    give_screens(1)
    cross(1, 0)
    relay(1, 1)
    relay(1, 3, inner)
    relay(0, 1)
    give_screens(2)
    settle(1, 0)
    screened(0)
    swap.wait_recv()
    make_side(0)
    cross(0, 0)
    relay(1, 2, inner)
    give_screens(3)
    relay(0, 3, inner)
    cross(1, 1)
    settle(1, 1)
    screened(1)
    make_side(1)
    relay(1, 2, outer)
    cross(0, 1)
    settle(0, 1)
    make_green(1)
    project_vir(0)
    relay(1, 3, outer)
    cross(1, 2)
    settle(1, 2)
    of_vir.to_mid(0)
    relay(0, 2, inner)
    screened(2)
    make_side(2)
    cross(1, 3)
    relay(0, 2, outer)
    project_vir(1)
    of_vir.to_far(0)
    of_vir.to_mid(1)
    settle(1, 3)
    screened(3)
    make_side(3)
    cross(0, 2)
    settle(0, 2)
    make_green(2)
    relay(0, 3, outer)
    project_vir(2)
    of_vir.to_far(1)
    of_vir.to_mid(2)
    cross(0, 3)
    settle(0, 3)
    make_green(3)
    arrived(0, diagonal)
    make_green(0, other_mid)
    project_occ(0, mid)
    project_occ(1)
    of_occ.to_mid(1)
    project_vir(3)
    of_vir.to_far(2)
    of_occ.to_far(1)
    of_vir.to_mid(3)
    project_occ(2)
    of_occ.to_mid(2)
    of_vir.to_far(3)
    project_occ(3)
    of_occ.to_far(2)
    of_occ.to_mid(3)
    of_vir.gather()
    project_occ(0, other_mid)
    of_occ.to_mid(0)
    of_occ.to_far(3)
    low = part == 0
    own, peer = of_vir.end()
    own, peer = own[:, :n_vir], peer[:, :n_vir]
    out_vir[:, :n_vir] = jnp.where(low, own, peer).astype(kind)
    out_vir[:, n_vir:] = jnp.where(low, peer, own).astype(kind)
    of_occ.to_far(0)
    of_occ.gather()
    own, peer = of_occ.end()
    value = own + peer
    wide_occ = od.shape[1]
    out_occ[:, :n_occ] = value[:, :n_occ].astype(kind)
    out_occ[:, n_occ:] = value[:, wide_occ : wide_occ + n_occ].astype(kind)
    for only, copy in sends:
        if only is None:
            copy.wait_send()
        else:
            pl.when(only)(copy.wait_send)


def fused(n_col, slab_occ, slab_vir, occ, vir, occ_energy, vir_energy, screen):
    up = lambda n: -(-n // 128) * 128
    block = slab_occ.shape[0]
    n_occ, columns = occ.shape
    n_vir = vir.shape[0]
    kind, f32 = slab_occ.dtype, jnp.float32
    half = columns // 2
    wide_occ, wide_vir = up(n_occ), up(n_vir)
    n_far = n_col // 4
    rows = 4 * block
    both = 2 * wide_occ
    dma = pltpu.SemaphoreType.DMA

    def pair(lead, lines, dtype=kind):
        return [pltpu.VMEM(lead + (lines, w), dtype) for w in (wide_vir, both)]

    return pl.pallas_call(
        functools.partial(fused_kernel, n_col),
        out_shape=[
            jax.ShapeDtypeStruct((block // 2, 2 * n), kind) for n in (n_occ, n_vir)
        ],
        in_specs=[ANY] * 7,
        out_specs=[VMEM] * 2,
        scratch_shapes=[
            pltpu.VMEM(slab_occ.shape, kind),
            pltpu.VMEM(slab_vir.shape, kind),
            pltpu.VMEM(occ_energy.shape, f32),
            pltpu.VMEM(vir_energy.shape, f32),
            pltpu.VMEM((n_col, block, wide_vir), kind),
            pltpu.VMEM((n_col, 2, block, wide_occ), kind),
            pltpu.VMEM((2, wide_vir, half), kind),
            pltpu.VMEM((2, wide_occ, half), kind),
            pltpu.VMEM((n_col, block, half), kind),
            pltpu.VMEM((n_far, rows, half), f32),
            pltpu.VMEM((n_far, rows, half), kind),
            pltpu.VMEM((n_far, rows, half), kind),
            pltpu.VMEM((n_far, 2, rows, half), kind),
        ]
        + pair((n_far, 2, 2), block)
        + pair((n_far, 2), block)
        + pair((n_far,), block)
        + pair((n_far,), block)
        + pair((n_far,), block, f32)
        + pair((n_far - 1,), block)
        + pair((n_far,), block)
        + pair((), block // 2)
        + pair((), block // 2)
        + [
            dma((8,)), dma((42,)), dma((2, n_col)), dma((2,)), dma((2,)), dma((n_col,)), dma((n_col,)),
            dma((n_far + 1,)), dma((n_far + 1,)), dma((n_far,)), dma((n_far,)),
            dma((2, n_far, 2)), dma((2, n_far, 2)), dma((2, n_far)), dma((2, n_far)),
            dma((2, n_far - 1)), dma((2, n_far)), dma((2,)), dma((2,)),
        ],
        compiler_params=pltpu.CompilerParams(collective_id=2, has_side_effects=True),
    )(slab_occ, slab_vir, occ, vir, occ_energy, vir_energy, screen)


def local(slab_occ, slab_vir, orbitals_occ, orbitals_vir, occ_energy, vir_energy, screened):
    n_orb, n_col = lax.axis_size("orb"), lax.axis_size("col")
    part = lax.axis_index("orb")
    block = slab_occ.shape[0] // n_orb
    n_occ, columns = orbitals_occ.shape
    n_vir = orbitals_vir.shape[0]
    kind = slab_occ.dtype
    if n_col == 16 and n_orb == 2 and block % 16 == 0 and columns % 512 == 0:
        return tuple(
            fused(
                n_col, slab_occ, slab_vir, orbitals_occ, orbitals_vir,
                occ_energy, vir_energy, screened,
            )
        )
    up = lambda n: -(-n // 128) * 128
    scaled_occ = (slab_occ.astype(jnp.float32) * jnp.exp(occ_energy)[None, :]).astype(kind)
    scaled_vir = (slab_vir.astype(jnp.float32) * jnp.exp(-vir_energy)[None, :]).astype(kind)
    start = up(n_vir)
    slab = jnp.concatenate(
        [
            jnp.pad(scaled_vir, ((0, 0), (0, start - n_vir))),
            jnp.pad(scaled_occ, ((0, 0), (0, up(n_occ) - n_occ))),
        ],
        axis=1,
    ).reshape((n_orb, block, start + up(n_occ)))
    mine = lax.dynamic_slice_in_dim(screened, part * block, block, 0)
    mine = mine.reshape((block, n_col, columns)).transpose((1, 0, 2))

    def order(own, peer, n):
        own, peer = own[:, :n], peer[:, :n]
        return jnp.where(
            part == 0, jnp.concatenate([own, peer], 1), jnp.concatenate([peer, own], 1)
        )

    slabs, peer_occ, peer_vir, screens = gather(n_col, slab, orbitals_occ, orbitals_vir, mine)
    slabs = slabs.reshape((2, n_col * block, slab.shape[2]))
    own_slab, peer_slab = slabs[0], slabs[1]

    def dot(a, b):
        return jnp.dot(a, b, preferred_element_type=jnp.float32)

    green_vir = dot(own_slab[:, :n_vir], orbitals_vir) + dot(peer_slab[:, :n_vir], peer_vir)
    green_occ = dot(own_slab[:, start : start + n_occ], orbitals_occ) + dot(
        peer_slab[:, start : start + n_occ], peer_occ
    )
    screen = screens.reshape((n_col * block, columns)).astype(jnp.float32)
    occ_side = (green_vir * screen).astype(kind)
    vir_side = (green_occ * screen).astype(kind)
    dims = (((1,), (1,)), ((), ()))

    def project(side, orbitals):
        term = lax.dot_general(side, orbitals, dims, preferred_element_type=jnp.float32)
        return term.astype(kind).reshape((n_col // 4, 2, 2, block, orbitals.shape[0]))

    vir_own, vir_peer, occ_own, occ_peer = scatter(
        n_col,
        [
            project(vir_side, orbitals_vir),
            project(vir_side, peer_vir),
            project(occ_side, orbitals_occ),
            project(occ_side, peer_occ),
        ],
    )

    return order(occ_own, occ_peer, n_occ), order(vir_own, vir_peer, n_vir)


def solution(mesh):
    return jax.shard_map(
        local,
        mesh=mesh,
        in_specs=(
            P("col", "orb"),
            P("col", "orb"),
            P("orb", "col"),
            P("orb", "col"),
            P("orb"),
            P("orb"),
            P("col", None),
        ),
        out_specs=(P(("col", "orb"), None), P(("col", "orb"), None)),
        check_vma=False,
    )
```

```python
import functools

import jax
import jax.numpy as jnp
from jax import lax
from jax.experimental import pallas as pl
from jax.experimental.pallas import tpu as pltpu
from jax.sharding import PartitionSpec as P

MESH = pl.DeviceIdType.MESH
LAGS = (1, 2)
ANY = pl.BlockSpec(memory_space=pl.ANY)
VMEM = pl.BlockSpec(memory_space=pltpu.VMEM)


def place(n_col):
    me = lax.axis_index("col")
    far, mid, core = me // 4, lax.rem(me // 2, 2), lax.rem(me, 2)
    return me, far, mid, core, lambda f, m, c: (f * 2 + m) * 2 + c


def greet(cols, orbs):
    barrier = pltpu.get_barrier_semaphore()
    for col in cols:
        pl.semaphore_signal(barrier, inc=1, device_id={"col": col}, device_id_type=MESH)
    for orb in orbs:
        pl.semaphore_signal(barrier, inc=1, device_id={"orb": orb}, device_id_type=MESH)
    pl.semaphore_wait(barrier, len(cols) + len(orbs))


def sender():
    sends = []

    def push(src, dst, send, recv, device):
        copy = pltpu.make_async_remote_copy(
            src_ref=src, dst_ref=dst, send_sem=send, recv_sem=recv,
            device_id=device, device_id_type=MESH,
        )
        copy.start()
        sends.append(copy)
        return copy

    return sends, push


def landed(ref, send, recv, device):
    pltpu.make_async_remote_copy(
        src_ref=ref, dst_ref=ref, send_sem=send, recv_sem=recv,
        device_id=device, device_id_type=MESH,
    ).wait_recv()


def spread(n_col, push, swap, slab, screen, slabs, screens, local_sem,
           orb_send, slab_send, slab_recv, screen_send, screen_recv):
    n_far = n_col // 4
    me, far, mid, core, index = place(n_col)
    part = lax.axis_index("orb")
    other = 1 - part
    others = [lax.rem(me + d, n_col) for d in range(1, n_col)]

    def arrived(k, col):
        landed(slabs.at[k, col], orb_send.at[swap], slab_recv.at[k, col], {"orb": other})

    counter = [0]

    def give(k, col, target, src=None):
        push(
            slabs.at[k, col] if src is None else src, slabs.at[k, col],
            slab_send.at[counter[0]], slab_recv.at[k, col], {"col": target},
        )
        counter[0] += 1

    x_peer, core_peer = index(far, 1 - mid, core), index(far, mid, 1 - core)
    fars = [lax.rem(far + d, n_far) for d in range(1, n_far)]
    own = slab.at[part]
    targets = [index(f, mid, core) for f in fars] + [x_peer, core_peer]
    for target in targets:
        give(0, me, target, own)
    arrived(1, me)
    for target in targets:
        give(1, me, target)
    for n, p in enumerate(others):
        push(screen.at[p], screens.at[me], screen_send.at[n], screen_recv.at[me], {"col": p})
    local = [
        pltpu.make_async_copy(own, slabs.at[0, me], local_sem.at[0]),
        pltpu.make_async_copy(screen.at[me], screens.at[me], local_sem.at[1]),
    ]
    for copy in local:
        copy.start()
    for f in fars:
        col = index(f, mid, core)
        for k in range(2):
            arrived(k, col)
            give(k, col, x_peer)
            give(k, col, core_peer)
    for f in [far] + fars:
        col = index(f, 1 - mid, core)
        for k in range(2):
            arrived(k, col)
            give(k, col, core_peer)
    for f in [far] + fars:
        for m in (mid, 1 - mid):
            for k in range(2):
                arrived(k, index(f, m, 1 - core))
    for p in others:
        landed(screens.at[p], orb_send.at[swap], screen_recv.at[p], {"orb": other})
    for copy in local:
        copy.wait()


def spread_semaphores(n_col):
    n_far = n_col // 4
    dma = pltpu.SemaphoreType.DMA
    n_give = 2 * ((n_far + 1) + 2 * (n_far - 1) + n_far)
    return [dma((n_give,)), dma((2, n_col)), dma((n_col,)), dma((n_col,))]


def gather_kernel(
    n_col, slab, occ, vir, screen, slabs, peer_occ, peer_vir, screens,
    local_sem, orb_send, orb_recv, slab_send, slab_recv, screen_send, screen_recv,
):
    me = lax.axis_index("col")
    other = 1 - lax.axis_index("orb")
    greet([lax.rem(me + d, n_col) for d in range(1, n_col)], [other])
    sends, push = sender()
    push(slab.at[other], slabs.at[1, me], orb_send.at[2], slab_recv.at[1, me], {"orb": other})
    push(vir, peer_vir, orb_send.at[0], orb_recv.at[0], {"orb": other})
    push(occ, peer_occ, orb_send.at[1], orb_recv.at[1], {"orb": other})
    spread(n_col, push, 2, slab, screen, slabs, screens, local_sem,
           orb_send, slab_send, slab_recv, screen_send, screen_recv)
    for n, ref in ((0, peer_vir), (1, peer_occ)):
        landed(ref, orb_send.at[n], orb_recv.at[n], {"orb": other})
    for copy in sends:
        copy.wait_send()


def gather(n_col, slab, occ, vir, screen):
    dma = pltpu.SemaphoreType.DMA
    return pl.pallas_call(
        functools.partial(gather_kernel, n_col),
        out_shape=(
            jax.ShapeDtypeStruct((2, n_col) + slab.shape[1:], slab.dtype),
            jax.ShapeDtypeStruct(occ.shape, occ.dtype),
            jax.ShapeDtypeStruct(vir.shape, vir.dtype),
            jax.ShapeDtypeStruct(screen.shape, screen.dtype),
        ),
        in_specs=[ANY] * 4,
        out_specs=(ANY,) * 4,
        scratch_shapes=[dma((2,)), dma((3,)), dma((2,))] + spread_semaphores(n_col),
        compiler_params=pltpu.CompilerParams(collective_id=0, has_side_effects=True),
    )(slab, occ, vir, screen)


def reduce_rows(n_col, pieces, ins, refs, ready, finish, flush=()):
    n_far = n_col // 4
    near, out_x, in_x, total, out_far, in_far = [
        refs[i * pieces : (i + 1) * pieces] for i in range(6)
    ]
    near_send, near_recv, x_send, x_recv, far_send, far_recv = refs[6 * pieces :]
    me, far, mid, core, index = place(n_col)
    x_peer, core_peer = index(far, 1 - mid, core), index(far, mid, 1 - core)
    fars = [lax.rem(far + d, n_far) for d in range(1, n_far)]
    sends, push = sender()
    wide = lambda value: value.astype(jnp.float32)
    first, second, third = [], [], []

    def to_core(t):
        ready(t)
        first.append(
            [
                push(
                    ins[t].at[:, m, 1 - core], near[t].at[slot],
                    near_send.at[t, slot], near_recv.at[t, slot], {"col": core_peer},
                )
                for slot, m in ((0, 1 - mid), (1, mid))
            ]
        )

    def to_mid(t):
        first[t][0].wait_recv()
        for f in range(n_far):
            out_x[t][f] = (wide(ins[t][f, 1 - mid, core]) + wide(near[t][0, f])).astype(
                out_x[t].dtype
            )
        second.append(push(out_x[t], in_x[t], x_send.at[t], x_recv.at[t], {"col": x_peer}))
        first[t][1].wait_recv()
        for f in range(n_far):
            total[t][f] = wide(ins[t][f, mid, core]) + wide(near[t][1, f])

    def to_far(t):
        second[t].wait_recv()
        for f in range(n_far):
            total[t][f] = total[t][f] + wide(in_x[t][f])
            out_far[t][f] = total[t][f].astype(out_far[t].dtype)
        for d, f in enumerate(fars):
            third.append(
                push(
                    out_far[t].at[f], in_far[t].at[d],
                    far_send.at[t, d], far_recv.at[t, d], {"col": index(f, mid, core)},
                )
            )

    acts, count = (to_core, to_mid, to_far), [0, 0, 0]

    def advance(stage, end):
        while count[stage] < end:
            acts[stage](count[stage])
            count[stage] += 1

    for t in range(pieces):
        if t in flush:
            advance(1, t)
            advance(2, t)
        advance(0, t + 1)
        advance(1, t + 1 - LAGS[0])
        advance(2, t + 1 - sum(LAGS))
    advance(1, pieces)
    advance(2, pieces)
    for t in range(pieces):
        value = total[t][far]
        for d in range(n_far - 1):
            third[t * (n_far - 1) + d].wait_recv()
            value = value + wide(in_far[t][d])
        finish(t, value)
    for made in sends:
        made.wait_send()


def reduce_scratch(n_col, block, kind):
    n_far = n_col // 4
    dma = pltpu.SemaphoreType.DMA
    pieces = len(block)

    def buffers(lead, dtype=kind):
        return [pltpu.VMEM(lead + tuple(b), dtype) for b in block]

    return (
        buffers((2, n_far))
        + buffers((n_far,))
        + buffers((n_far,))
        + buffers((n_far,), jnp.float32)
        + buffers((n_far,))
        + buffers((n_far - 1,))
        + [
            dma((pieces, 2)), dma((pieces, 2)), dma((pieces,)), dma((pieces,)),
            dma((pieces, n_far - 1)), dma((pieces, n_far - 1)),
        ]
    )


def scatter_kernel(n_col, pieces, *refs):
    me, far, mid, core, index = place(n_col)
    n_far = n_col // 4
    fars = [lax.rem(far + d, n_far) for d in range(1, n_far)]
    greet(
        [index(far, mid, 1 - core), index(far, 1 - mid, core)]
        + [index(f, mid, core) for f in fars],
        [],
    )
    outs = refs[pieces : 2 * pieces]

    def finish(t, value):
        outs[t][...] = value.astype(outs[t].dtype)

    reduce_rows(n_col, pieces, refs[:pieces], refs[2 * pieces :], lambda t: None, finish)


def scatter(n_col, terms):
    pieces = len(terms)
    block, kind = [t.shape[-2:] for t in terms], terms[0].dtype
    return pl.pallas_call(
        functools.partial(scatter_kernel, n_col, pieces),
        out_shape=[jax.ShapeDtypeStruct(b, kind) for b in block],
        in_specs=[VMEM] * pieces,
        out_specs=[VMEM] * pieces,
        scratch_shapes=reduce_scratch(n_col, block, kind),
        compiler_params=pltpu.CompilerParams(collective_id=1, has_side_effects=True),
    )(*terms)


def order(far, j):
    if j == 0:
        return far
    if j == 1:
        return far + 1 - 2 * lax.rem(far, 2)
    return lax.rem(far + 2, 4) if j == 2 else 3 - far


def fused_kernel(n_col, slab_occ, slab_vir, occ, vir, occ_energy, vir_energy, screen, *refs):
    out_occ, out_vir = refs[:2]
    (raw_occ, raw_vir, e_occ, e_vir, sv, so, ov, od, screens, green, green_out, green_in, side,
     part_vir, part_occ, near_vir, near_occ, out_x_vir, out_x_occ, in_x_vir, in_x_occ,
     sum_vir, sum_occ, out_far_vir, out_far_occ, in_far_vir, in_far_occ,
     end_out_vir, end_out_occ, end_in_vir, end_in_occ) = refs[2:33]
    (load_sem, slab_send, slab_recv, swap_send, swap_recv, screen_send, screen_recv,
     green_send, green_recv, side_send, side_recv, near_send, near_recv, x_send, x_recv,
     far_send, far_recv, end_send, end_recv) = refs[33:]
    n_far = n_col // 4
    me, far, mid, core, index = place(n_col)
    part = lax.axis_index("orb")
    other = 1 - part
    x_peer, core_peer = index(far, 1 - mid, core), index(far, mid, 1 - core)
    other_mid = 1 - mid
    diagonal = index(far, other_mid, 1 - core)
    inner = lax.rem(far, 3) > 0
    outer = lax.rem(far, 3) == 0
    planes = [order(far, j) for j in range(n_far)]
    n_occ = occ.shape[0]
    n_vir = vir.shape[0]
    half = ov.shape[2]
    block = sv.shape[1]
    rows = 4 * block
    kind = sv.dtype
    wide = lambda value: value.astype(jnp.float32)

    def dot(a, b):
        return jnp.dot(a, b, preferred_element_type=jnp.float32)

    def dot_t(a, b):
        return lax.dot_general(a, b, (((1,), (1,)), ((), ())), preferred_element_type=jnp.float32)

    barrier = pltpu.get_barrier_semaphore()
    for d in range(1, n_col):
        pl.semaphore_signal(
            barrier, inc=1, device_id={"col": lax.rem(me + d, n_col)}, device_id_type=MESH
        )
    pl.semaphore_signal(barrier, inc=1, device_id={"orb": other}, device_id_type=MESH)

    def piece(p, k):
        start = p * (2 * half) + k * half
        return screen.at[:, pl.ds(pl.multiple_of(start, half), half)]

    def columns_of(ref, k):
        return ref.at[:, pl.ds(pl.multiple_of(k * half, half), half)]

    loads = [
        pltpu.make_async_copy(src, dst, load_sem.at[n])
        for n, (src, dst) in enumerate(
            (
                (vir_energy, e_vir), (slab_vir, raw_vir), (occ_energy, e_occ), (slab_occ, raw_occ),
                (columns_of(vir, other), ov.at[other, pl.ds(0, n_vir)]),
                (columns_of(vir, part), ov.at[part, pl.ds(0, n_vir)]),
                (columns_of(occ, part), od.at[part, pl.ds(0, n_occ)]),
                (piece(me, part), screens.at[me]),
            )
        )
    ]
    for load in loads:
        load.start()
    for ref, n in ((ov, n_vir), (od, n_occ)):
        short = ref.shape[1] - n
        if short:
            for k in range(2):
                ref[k, pl.ds(n, short)] = jnp.zeros((short, half), kind)
    for load in loads[:4]:
        load.wait()
    sv[me, :, :n_vir] = (wide(raw_vir[...]) * jnp.exp(-e_vir[...])[None, :]).astype(kind)
    if sv.shape[2] > n_vir:
        sv[me, :, n_vir:] = jnp.zeros((block, sv.shape[2] - n_vir), kind)
    so[me, part, :, :n_occ] = (wide(raw_occ[...]) * jnp.exp(e_occ[...])[None, :]).astype(kind)
    if so.shape[3] > n_occ:
        so[me, part, :, n_occ:] = jnp.zeros((block, so.shape[3] - n_occ), kind)
    pl.semaphore_wait(barrier, n_col)

    sends = []

    def push(src, dst, send, recv, device, only=None):
        copy = pltpu.make_async_remote_copy(
            src_ref=src, dst_ref=dst, send_sem=send, recv_sem=recv,
            device_id=device, device_id_type=MESH,
        )
        if only is None:
            copy.start()
        else:
            pl.when(only)(copy.start)
        sends.append((only, copy))
        return copy

    slabs = (sv, so)
    counter = [0]

    def give(k, col, target, only=None):
        push(slabs[k].at[col], slabs[k].at[col], slab_send.at[counter[0]], slab_recv.at[k, col],
             {"col": target}, only)
        counter[0] += 1

    def arrived(k, col, only=None):
        def act():
            landed(slabs[k].at[col], swap_send.at[0], slab_recv.at[k, col], {"orb": other})

        act() if only is None else pl.when(only)(act)

    def give_own(k):
        give(k, me, x_peer)
        give(k, me, index(planes[1], mid, core))
        give(k, me, index(planes[3], mid, core), inner)
        give(k, me, core_peer)

    def relay(k, j, only=None):
        col = index(planes[j], mid, core)
        arrived(k, col, only)
        step = planes[3 if j == 1 else 1]
        if only is not outer:
            give(k, col, index(step, mid, core), inner)
        give(k, col, x_peer, only)
        give(k, col, core_peer, only)

    def cross(k, j):
        col = index(planes[j], 1 - mid, core)
        arrived(k, col)
        give(k, col, core_peer)

    def settle(k, j):
        arrived(k, index(planes[j], mid, 1 - core))
        arrived(k, index(planes[j], 1 - mid, 1 - core))

    screen_count = [0]

    def give_screen(target):
        push(piece(target, part), screens.at[me], screen_send.at[screen_count[0]],
             screen_recv.at[me], {"col": target})
        screen_count[0] += 1

    def give_screens(j):
        for m, c in ((mid, core), (1 - mid, core), (mid, 1 - core), (1 - mid, 1 - core)):
            give_screen(index(planes[j], m, c))

    def screened(j):
        for m, c in ((mid, core), (1 - mid, core), (mid, 1 - core), (1 - mid, 1 - core)):
            if j == 0 and m is mid and c is core:
                loads[7].wait()
            else:
                col = index(planes[j], m, c)
                landed(screens.at[col], swap_send.at[0], screen_recv.at[col], {"orb": other})

    def plane(j):
        return pl.ds(planes[j] * 4, 4)

    def shade(j, cut):
        return wide(screens[plane(j), :, cut].reshape((rows, -1)))

    cuts = [slice(start, start + 256) for start in range(0, half, 256)]
    swaps = {}

    def chip(m):
        return pl.ds(planes[0] * 4 + 2 * m, 2), pl.ds(pl.multiple_of(m * (2 * block), 2 * block), 2 * block)

    def make_green(j, m=None):
        owners, lines = (plane(j), pl.ds(0, rows)) if m is None else chip(m)
        slot = j if m is not other_mid else n_far
        slab = sv[owners].reshape((-1, sv.shape[2]))
        for cut in cuts:
            green_out[j, lines, cut] = dot(slab, ov[other, :, cut]).astype(kind)
        swaps["green", slot] = push(green_out.at[j, lines], green_in.at[j, lines], green_send.at[slot],
                                    green_recv.at[slot], {"orb": other})
        for cut in cuts:
            green[j, lines, cut] = dot(slab, ov[part, :, cut])

    def make_side(j):
        for cut in cuts:
            value = dot(so[plane(j), 0].reshape((rows, -1)), od[0, :, cut])
            value = value + dot(so[plane(j), 1].reshape((rows, -1)), od[1, :, cut])
            side[j, part, :, cut] = (value * shade(j, cut)).astype(kind)
        swaps["side", j] = push(side.at[j, part], side.at[j, part], side_send.at[j],
                                side_recv.at[j], {"orb": other})

    class Reduce:
        def __init__(self, n, part, near, out_x, in_x, total, out_far, in_far, end_out, end_in):
            self.n, self.part, self.near, self.out_x, self.in_x = n, part, near, out_x, in_x
            self.total, self.out_far, self.in_far = total, out_far, in_far
            self.end_out, self.end_in = end_out, end_in
            self.first, self.second, self.third = {}, {}, {}

        def to_core(self, j, slots=(0, 1)):
            n = self.n
            for slot in slots:
                m = (other_mid, mid)[slot]
                self.first[j, slot] = push(
                    self.part.at[j, m, 1 - core], self.near.at[j, slot],
                    near_send.at[n, j, slot], near_recv.at[n, j, slot], {"col": core_peer},
                )

        def to_mid(self, j):
            n = self.n
            self.first[j, 0].wait_recv()
            self.out_x[j] = (wide(self.part[j, 1 - mid, core]) + wide(self.near[j, 0])).astype(kind)
            self.second[j] = push(self.out_x.at[j], self.in_x.at[j], x_send.at[n, j],
                                  x_recv.at[n, j], {"col": x_peer})
            self.first[j, 1].wait_recv()
            self.total[j] = wide(self.part[j, mid, core]) + wide(self.near[j, 1])

        def to_far(self, j):
            n = self.n
            self.second[j].wait_recv()
            self.total[j] = self.total[j] + wide(self.in_x[j])
            if j == n_far - 1:
                pl.when(inner)(functools.partial(self.take, planes[2], j))
            if j > 0:
                self.out_far[j - 1] = self.total[j].astype(kind)
                target, slot = planes[j], far
                if j == 2:
                    target = lax.select(inner, planes[2], planes[1])
                    slot = lax.select(inner, far, planes[3])
                push(self.out_far.at[j - 1], self.in_far.at[slot], far_send.at[n, j - 1],
                     far_recv.at[n, slot], {"col": index(target, mid, core)})

        def take(self, source, j):
            landed(self.in_far.at[source], swap_send.at[0], far_recv.at[self.n, source], {"orb": other})
            self.total[j] = self.total[j] + wide(self.in_far[source])

        def gather(self):
            n = self.n
            self.take(planes[1], 0)
            pl.when(outer)(functools.partial(self.take, planes[2], 0))
            self.take(planes[3], 0)
            lines = block // 2
            mine = pl.ds(pl.multiple_of(part * lines, lines), lines)
            theirs = pl.ds(pl.multiple_of(other * lines, lines), lines)
            self.end_out[...] = self.total[0, theirs].astype(kind)
            self.last = push(self.end_out, self.end_in, end_send.at[n], end_recv.at[n], {"orb": other})
            self.mine = mine

        def end(self):
            self.last.wait_recv()
            return self.total[0, self.mine], wide(self.end_in[...])

    of_vir = Reduce(0, part_vir, near_vir, out_x_vir, in_x_vir, sum_vir, out_far_vir, in_far_vir,
                    end_out_vir, end_in_vir)
    of_occ = Reduce(1, part_occ, near_occ, out_x_occ, in_x_occ, sum_occ, out_far_occ, in_far_occ,
                    end_out_occ, end_in_occ)

    def project_vir(j):
        swaps["side", j].wait_recv()
        width = part_vir.shape[-1]
        for start in range(0, width, 256):
            cut = slice(start, min(start + 256, width))
            term = dot_t(side[j, 0], ov[0, cut]) + dot_t(side[j, 1], ov[1, cut])
            part_vir[j, :, :, :, cut] = term.astype(kind).reshape((2, 2, block, -1))
        of_vir.to_core(j)

    def project_occ(j, m=None):
        slot = j if m is not other_mid else n_far
        swaps["green", slot].wait_recv()
        owners, lines = (plane(j), pl.ds(0, rows)) if m is None else chip(m)
        shades = wide(screens[owners].reshape((-1, half)))
        value = (green[j, lines] + wide(green_in[j, lines])) * shades
        value = value.astype(kind)
        wide_occ = od.shape[1]
        for k in range(2):
            term = dot_t(value, od[k]).astype(kind).reshape((-1, 2, block, wide_occ))
            cut = slice(k * wide_occ, (k + 1) * wide_occ)
            if m is None:
                part_occ[j, :, :, :, cut] = term
            else:
                part_occ[j, m, :, :, cut] = term[0]
        of_occ.to_core(j, (0, 1) if m is None else (0,) if m is other_mid else (1,))

    push(so.at[me, part], so.at[me, part], swap_send.at[0], swap_recv.at[0], {"orb": other})
    swap = push(columns_of(occ, other), od.at[part, pl.ds(0, n_occ)], swap_send.at[1],
                swap_recv.at[1], {"orb": other})
    give_own(0)
    for load in loads[4:7]:
        load.wait()
    arrived(0, core_peer)
    make_green(0, mid)
    landed(so.at[me, other], swap_send.at[0], swap_recv.at[0], {"orb": other})
    give_own(1)
    for target in (x_peer, core_peer, diagonal):
        give_screen(target)
    give_screens(1)
    cross(1, 0)
    relay(1, 1)
    relay(1, 3, inner)
    relay(0, 1)
    give_screens(2)
    settle(1, 0)
    screened(0)
    swap.wait_recv()
    make_side(0)
    cross(0, 0)
    relay(1, 2, inner)
    give_screens(3)
    relay(0, 3, inner)
    cross(1, 1)
    settle(1, 1)
    screened(1)
    make_side(1)
    relay(1, 2, outer)
    cross(0, 1)
    settle(0, 1)
    make_green(1)
    project_vir(0)
    relay(1, 3, outer)
    cross(1, 2)
    of_vir.to_mid(0)
    relay(0, 2, inner)
    settle(1, 2)
    screened(2)
    make_side(2)
    cross(1, 3)
    relay(0, 2, outer)
    project_vir(1)
    of_vir.to_far(0)
    project_occ(0, mid)
    settle(1, 3)
    screened(3)
    make_side(3)
    of_vir.to_mid(1)
    cross(0, 2)
    settle(0, 2)
    make_green(2)
    relay(0, 3, outer)
    project_vir(2)
    project_occ(1)
    of_vir.to_far(1)
    cross(0, 3)
    of_vir.to_mid(2)
    of_occ.to_mid(1)
    settle(0, 3)
    make_green(3)
    arrived(0, diagonal)
    make_green(0, other_mid)
    project_vir(3)
    of_vir.to_far(2)
    of_occ.to_far(1)
    of_vir.to_mid(3)
    project_occ(2)
    of_occ.to_mid(2)
    of_vir.to_far(3)
    project_occ(3)
    of_occ.to_far(2)
    of_occ.to_mid(3)
    project_occ(0, other_mid)
    of_occ.to_mid(0)
    of_occ.to_far(3)
    of_vir.gather()
    of_occ.to_far(0)
    of_occ.gather()
    low = part == 0
    own, peer = of_vir.end()
    own, peer = own[:, :n_vir], peer[:, :n_vir]
    out_vir[:, :n_vir] = jnp.where(low, own, peer).astype(kind)
    out_vir[:, n_vir:] = jnp.where(low, peer, own).astype(kind)
    own, peer = of_occ.end()
    value = own + peer
    wide_occ = od.shape[1]
    out_occ[:, :n_occ] = value[:, :n_occ].astype(kind)
    out_occ[:, n_occ:] = value[:, wide_occ : wide_occ + n_occ].astype(kind)
    for only, copy in sends:
        if only is None:
            copy.wait_send()
        else:
            pl.when(only)(copy.wait_send)


def fused(n_col, slab_occ, slab_vir, occ, vir, occ_energy, vir_energy, screen):
    up = lambda n: -(-n // 128) * 128
    block = slab_occ.shape[0]
    n_occ, columns = occ.shape
    n_vir = vir.shape[0]
    kind, f32 = slab_occ.dtype, jnp.float32
    half = columns // 2
    wide_occ, wide_vir = up(n_occ), up(n_vir)
    n_far = n_col // 4
    rows = 4 * block
    both = 2 * wide_occ
    dma = pltpu.SemaphoreType.DMA

    def pair(lead, lines, dtype=kind):
        return [pltpu.VMEM(lead + (lines, w), dtype) for w in (wide_vir, both)]

    return pl.pallas_call(
        functools.partial(fused_kernel, n_col),
        out_shape=[pltpu.VMEM((block // 2, 2 * n), kind) for n in (n_occ, n_vir)],
        in_specs=[ANY] * 7,
        out_specs=[VMEM] * 2,
        scratch_shapes=[
            pltpu.VMEM(slab_occ.shape, kind),
            pltpu.VMEM(slab_vir.shape, kind),
            pltpu.VMEM(occ_energy.shape, f32),
            pltpu.VMEM(vir_energy.shape, f32),
            pltpu.VMEM((n_col, block, wide_vir), kind),
            pltpu.VMEM((n_col, 2, block, wide_occ), kind),
            pltpu.VMEM((2, wide_vir, half), kind),
            pltpu.VMEM((2, wide_occ, half), kind),
            pltpu.VMEM((n_col, block, half), kind),
            pltpu.VMEM((n_far, rows, half), f32),
            pltpu.VMEM((n_far, rows, half), kind),
            pltpu.VMEM((n_far, rows, half), kind),
            pltpu.VMEM((n_far, 2, rows, half), kind),
        ]
        + pair((n_far, 2, 2), block)
        + pair((n_far, 2), block)
        + pair((n_far,), block)
        + pair((n_far,), block)
        + pair((n_far,), block, f32)
        + pair((n_far - 1,), block)
        + pair((n_far,), block)
        + pair((), block // 2)
        + pair((), block // 2)
        + [
            dma((8,)), dma((42,)), dma((2, n_col)), dma((2,)), dma((2,)), dma((n_col,)), dma((n_col,)),
            dma((n_far + 1,)), dma((n_far + 1,)), dma((n_far,)), dma((n_far,)),
            dma((2, n_far, 2)), dma((2, n_far, 2)), dma((2, n_far)), dma((2, n_far)),
            dma((2, n_far - 1)), dma((2, n_far)), dma((2,)), dma((2,)),
        ],
        compiler_params=pltpu.CompilerParams(
            collective_id=2, has_side_effects=True, vmem_limit_bytes=60 * 2**20
        ),
    )(slab_occ, slab_vir, occ, vir, occ_energy, vir_energy, screen)


def local(slab_occ, slab_vir, orbitals_occ, orbitals_vir, occ_energy, vir_energy, screened):
    n_orb, n_col = lax.axis_size("orb"), lax.axis_size("col")
    part = lax.axis_index("orb")
    block = slab_occ.shape[0] // n_orb
    n_occ, columns = orbitals_occ.shape
    n_vir = orbitals_vir.shape[0]
    kind = slab_occ.dtype
    if n_col == 16 and n_orb == 2 and block % 16 == 0 and columns % 512 == 0:
        return tuple(
            fused(
                n_col, slab_occ, slab_vir, orbitals_occ, orbitals_vir,
                occ_energy, vir_energy, screened,
            )
        )
    up = lambda n: -(-n // 128) * 128
    scaled_occ = (slab_occ.astype(jnp.float32) * jnp.exp(occ_energy)[None, :]).astype(kind)
    scaled_vir = (slab_vir.astype(jnp.float32) * jnp.exp(-vir_energy)[None, :]).astype(kind)
    start = up(n_vir)
    slab = jnp.concatenate(
        [
            jnp.pad(scaled_vir, ((0, 0), (0, start - n_vir))),
            jnp.pad(scaled_occ, ((0, 0), (0, up(n_occ) - n_occ))),
        ],
        axis=1,
    ).reshape((n_orb, block, start + up(n_occ)))
    mine = lax.dynamic_slice_in_dim(screened, part * block, block, 0)
    mine = mine.reshape((block, n_col, columns)).transpose((1, 0, 2))

    def order(own, peer, n):
        own, peer = own[:, :n], peer[:, :n]
        return jnp.where(
            part == 0, jnp.concatenate([own, peer], 1), jnp.concatenate([peer, own], 1)
        )

    slabs, peer_occ, peer_vir, screens = gather(n_col, slab, orbitals_occ, orbitals_vir, mine)
    slabs = slabs.reshape((2, n_col * block, slab.shape[2]))
    own_slab, peer_slab = slabs[0], slabs[1]

    def dot(a, b):
        return jnp.dot(a, b, preferred_element_type=jnp.float32)

    green_vir = dot(own_slab[:, :n_vir], orbitals_vir) + dot(peer_slab[:, :n_vir], peer_vir)
    green_occ = dot(own_slab[:, start : start + n_occ], orbitals_occ) + dot(
        peer_slab[:, start : start + n_occ], peer_occ
    )
    screen = screens.reshape((n_col * block, columns)).astype(jnp.float32)
    occ_side = (green_vir * screen).astype(kind)
    vir_side = (green_occ * screen).astype(kind)
    dims = (((1,), (1,)), ((), ()))

    def project(side, orbitals):
        term = lax.dot_general(side, orbitals, dims, preferred_element_type=jnp.float32)
        return term.astype(kind).reshape((n_col // 4, 2, 2, block, orbitals.shape[0]))

    vir_own, vir_peer, occ_own, occ_peer = scatter(
        n_col,
        [
            project(vir_side, orbitals_vir),
            project(vir_side, peer_vir),
            project(occ_side, orbitals_occ),
            project(occ_side, peer_occ),
        ],
    )

    return order(occ_own, occ_peer, n_occ), order(vir_own, vir_peer, n_vir)


def solution(mesh):
    return jax.shard_map(
        local,
        mesh=mesh,
        in_specs=(
            P("col", "orb"),
            P("col", "orb"),
            P("orb", "col"),
            P("orb", "col"),
            P("orb"),
            P("orb"),
            P("col", None),
        ),
        out_specs=(P(("col", "orb"), None), P(("col", "orb"), None)),
        check_vma=False,
    )
```

```python
import functools

import jax
import jax.numpy as jnp
from jax import lax
from jax.experimental import pallas as pl
from jax.experimental.pallas import tpu as pltpu
from jax.sharding import PartitionSpec as P

MESH = pl.DeviceIdType.MESH
LAGS = (1, 2)
ANY = pl.BlockSpec(memory_space=pl.ANY)
VMEM = pl.BlockSpec(memory_space=pltpu.VMEM)


def place(n_col):
    me = lax.axis_index("col")
    far, mid, core = me // 4, lax.rem(me // 2, 2), lax.rem(me, 2)
    return me, far, mid, core, lambda f, m, c: (f * 2 + m) * 2 + c


def greet(cols, orbs):
    barrier = pltpu.get_barrier_semaphore()
    for col in cols:
        pl.semaphore_signal(barrier, inc=1, device_id={"col": col}, device_id_type=MESH)
    for orb in orbs:
        pl.semaphore_signal(barrier, inc=1, device_id={"orb": orb}, device_id_type=MESH)
    pl.semaphore_wait(barrier, len(cols) + len(orbs))


def sender():
    sends = []

    def push(src, dst, send, recv, device):
        copy = pltpu.make_async_remote_copy(
            src_ref=src, dst_ref=dst, send_sem=send, recv_sem=recv,
            device_id=device, device_id_type=MESH,
        )
        copy.start()
        sends.append(copy)
        return copy

    return sends, push


def landed(ref, send, recv, device):
    pltpu.make_async_remote_copy(
        src_ref=ref, dst_ref=ref, send_sem=send, recv_sem=recv,
        device_id=device, device_id_type=MESH,
    ).wait_recv()


def spread(n_col, push, swap, slab, screen, slabs, screens, local_sem,
           orb_send, slab_send, slab_recv, screen_send, screen_recv):
    n_far = n_col // 4
    me, far, mid, core, index = place(n_col)
    part = lax.axis_index("orb")
    other = 1 - part
    others = [lax.rem(me + d, n_col) for d in range(1, n_col)]

    def arrived(k, col):
        landed(slabs.at[k, col], orb_send.at[swap], slab_recv.at[k, col], {"orb": other})

    counter = [0]

    def give(k, col, target, src=None):
        push(
            slabs.at[k, col] if src is None else src, slabs.at[k, col],
            slab_send.at[counter[0]], slab_recv.at[k, col], {"col": target},
        )
        counter[0] += 1

    x_peer, core_peer = index(far, 1 - mid, core), index(far, mid, 1 - core)
    fars = [lax.rem(far + d, n_far) for d in range(1, n_far)]
    own = slab.at[part]
    targets = [index(f, mid, core) for f in fars] + [x_peer, core_peer]
    for target in targets:
        give(0, me, target, own)
    arrived(1, me)
    for target in targets:
        give(1, me, target)
    for n, p in enumerate(others):
        push(screen.at[p], screens.at[me], screen_send.at[n], screen_recv.at[me], {"col": p})
    local = [
        pltpu.make_async_copy(own, slabs.at[0, me], local_sem.at[0]),
        pltpu.make_async_copy(screen.at[me], screens.at[me], local_sem.at[1]),
    ]
    for copy in local:
        copy.start()
    for f in fars:
        col = index(f, mid, core)
        for k in range(2):
            arrived(k, col)
            give(k, col, x_peer)
            give(k, col, core_peer)
    for f in [far] + fars:
        col = index(f, 1 - mid, core)
        for k in range(2):
            arrived(k, col)
            give(k, col, core_peer)
    for f in [far] + fars:
        for m in (mid, 1 - mid):
            for k in range(2):
                arrived(k, index(f, m, 1 - core))
    for p in others:
        landed(screens.at[p], orb_send.at[swap], screen_recv.at[p], {"orb": other})
    for copy in local:
        copy.wait()


def spread_semaphores(n_col):
    n_far = n_col // 4
    dma = pltpu.SemaphoreType.DMA
    n_give = 2 * ((n_far + 1) + 2 * (n_far - 1) + n_far)
    return [dma((n_give,)), dma((2, n_col)), dma((n_col,)), dma((n_col,))]


def gather_kernel(
    n_col, slab, occ, vir, screen, slabs, peer_occ, peer_vir, screens,
    local_sem, orb_send, orb_recv, slab_send, slab_recv, screen_send, screen_recv,
):
    me = lax.axis_index("col")
    other = 1 - lax.axis_index("orb")
    greet([lax.rem(me + d, n_col) for d in range(1, n_col)], [other])
    sends, push = sender()
    push(slab.at[other], slabs.at[1, me], orb_send.at[2], slab_recv.at[1, me], {"orb": other})
    push(vir, peer_vir, orb_send.at[0], orb_recv.at[0], {"orb": other})
    push(occ, peer_occ, orb_send.at[1], orb_recv.at[1], {"orb": other})
    spread(n_col, push, 2, slab, screen, slabs, screens, local_sem,
           orb_send, slab_send, slab_recv, screen_send, screen_recv)
    for n, ref in ((0, peer_vir), (1, peer_occ)):
        landed(ref, orb_send.at[n], orb_recv.at[n], {"orb": other})
    for copy in sends:
        copy.wait_send()


def gather(n_col, slab, occ, vir, screen):
    dma = pltpu.SemaphoreType.DMA
    return pl.pallas_call(
        functools.partial(gather_kernel, n_col),
        out_shape=(
            jax.ShapeDtypeStruct((2, n_col) + slab.shape[1:], slab.dtype),
            jax.ShapeDtypeStruct(occ.shape, occ.dtype),
            jax.ShapeDtypeStruct(vir.shape, vir.dtype),
            jax.ShapeDtypeStruct(screen.shape, screen.dtype),
        ),
        in_specs=[ANY] * 4,
        out_specs=(ANY,) * 4,
        scratch_shapes=[dma((2,)), dma((3,)), dma((2,))] + spread_semaphores(n_col),
        compiler_params=pltpu.CompilerParams(collective_id=0, has_side_effects=True),
    )(slab, occ, vir, screen)


def reduce_rows(n_col, pieces, ins, refs, ready, finish, flush=()):
    n_far = n_col // 4
    near, out_x, in_x, total, out_far, in_far = [
        refs[i * pieces : (i + 1) * pieces] for i in range(6)
    ]
    near_send, near_recv, x_send, x_recv, far_send, far_recv = refs[6 * pieces :]
    me, far, mid, core, index = place(n_col)
    x_peer, core_peer = index(far, 1 - mid, core), index(far, mid, 1 - core)
    fars = [lax.rem(far + d, n_far) for d in range(1, n_far)]
    sends, push = sender()
    wide = lambda value: value.astype(jnp.float32)
    first, second, third = [], [], []

    def to_core(t):
        ready(t)
        first.append(
            [
                push(
                    ins[t].at[:, m, 1 - core], near[t].at[slot],
                    near_send.at[t, slot], near_recv.at[t, slot], {"col": core_peer},
                )
                for slot, m in ((0, 1 - mid), (1, mid))
            ]
        )

    def to_mid(t):
        first[t][0].wait_recv()
        for f in range(n_far):
            out_x[t][f] = (wide(ins[t][f, 1 - mid, core]) + wide(near[t][0, f])).astype(
                out_x[t].dtype
            )
        second.append(push(out_x[t], in_x[t], x_send.at[t], x_recv.at[t], {"col": x_peer}))
        first[t][1].wait_recv()
        for f in range(n_far):
            total[t][f] = wide(ins[t][f, mid, core]) + wide(near[t][1, f])

    def to_far(t):
        second[t].wait_recv()
        for f in range(n_far):
            total[t][f] = total[t][f] + wide(in_x[t][f])
            out_far[t][f] = total[t][f].astype(out_far[t].dtype)
        for d, f in enumerate(fars):
            third.append(
                push(
                    out_far[t].at[f], in_far[t].at[d],
                    far_send.at[t, d], far_recv.at[t, d], {"col": index(f, mid, core)},
                )
            )

    acts, count = (to_core, to_mid, to_far), [0, 0, 0]

    def advance(stage, end):
        while count[stage] < end:
            acts[stage](count[stage])
            count[stage] += 1

    for t in range(pieces):
        if t in flush:
            advance(1, t)
            advance(2, t)
        advance(0, t + 1)
        advance(1, t + 1 - LAGS[0])
        advance(2, t + 1 - sum(LAGS))
    advance(1, pieces)
    advance(2, pieces)
    for t in range(pieces):
        value = total[t][far]
        for d in range(n_far - 1):
            third[t * (n_far - 1) + d].wait_recv()
            value = value + wide(in_far[t][d])
        finish(t, value)
    for made in sends:
        made.wait_send()


def reduce_scratch(n_col, block, kind):
    n_far = n_col // 4
    dma = pltpu.SemaphoreType.DMA
    pieces = len(block)

    def buffers(lead, dtype=kind):
        return [pltpu.VMEM(lead + tuple(b), dtype) for b in block]

    return (
        buffers((2, n_far))
        + buffers((n_far,))
        + buffers((n_far,))
        + buffers((n_far,), jnp.float32)
        + buffers((n_far,))
        + buffers((n_far - 1,))
        + [
            dma((pieces, 2)), dma((pieces, 2)), dma((pieces,)), dma((pieces,)),
            dma((pieces, n_far - 1)), dma((pieces, n_far - 1)),
        ]
    )


def scatter_kernel(n_col, pieces, *refs):
    me, far, mid, core, index = place(n_col)
    n_far = n_col // 4
    fars = [lax.rem(far + d, n_far) for d in range(1, n_far)]
    greet(
        [index(far, mid, 1 - core), index(far, 1 - mid, core)]
        + [index(f, mid, core) for f in fars],
        [],
    )
    outs = refs[pieces : 2 * pieces]

    def finish(t, value):
        outs[t][...] = value.astype(outs[t].dtype)

    reduce_rows(n_col, pieces, refs[:pieces], refs[2 * pieces :], lambda t: None, finish)


def scatter(n_col, terms):
    pieces = len(terms)
    block, kind = [t.shape[-2:] for t in terms], terms[0].dtype
    return pl.pallas_call(
        functools.partial(scatter_kernel, n_col, pieces),
        out_shape=[jax.ShapeDtypeStruct(b, kind) for b in block],
        in_specs=[VMEM] * pieces,
        out_specs=[VMEM] * pieces,
        scratch_shapes=reduce_scratch(n_col, block, kind),
        compiler_params=pltpu.CompilerParams(collective_id=1, has_side_effects=True),
    )(*terms)


def order(far, j):
    if j == 0:
        return far
    if j == 1:
        return far + 1 - 2 * lax.rem(far, 2)
    return lax.rem(far + 2, 4) if j == 2 else 3 - far


def fused_kernel(n_col, slab_occ, slab_vir, occ, vir, occ_energy, vir_energy, screen, *refs):
    out_occ, out_vir = refs[:2]
    (raw_occ, raw_vir, e_occ, e_vir, sv, so, ov, od, screens, green, green_out, green_in, side,
     part_vir, part_occ, near_vir, near_occ, out_x_vir, out_x_occ, in_x_vir, in_x_occ,
     sum_vir, sum_occ, out_far_vir, out_far_occ, in_far_vir, joint_occ, in_far_occ, in_own_occ,
     half_vir, half_occ, in_half_vir, in_half_occ, value_occ, in_last_vir) = refs[2:37]
    (load_sem, slab_send, slab_recv, swap_send, swap_recv, screen_send, screen_recv,
     green_send, green_recv, side_send, side_recv, near_send, near_recv, x_send, x_recv,
     far_send, far_recv, half_send, half_recv, joint_send, joint_recv, occ_send, occ_recv,
     own_send, own_recv, last_send, last_recv) = refs[37:]
    n_far = n_col // 4
    me, far, mid, core, index = place(n_col)
    part = lax.axis_index("orb")
    other = 1 - part
    x_peer, core_peer = index(far, 1 - mid, core), index(far, mid, 1 - core)
    other_mid = 1 - mid
    diagonal = index(far, other_mid, 1 - core)
    inner = lax.rem(far, 3) > 0
    outer = lax.rem(far, 3) == 0
    planes = [order(far, j) for j in range(n_far)]
    n_occ = occ.shape[0]
    n_vir = vir.shape[0]
    half = ov.shape[2]
    block = sv.shape[1]
    rows = 4 * block
    kind = sv.dtype
    wide = lambda value: value.astype(jnp.float32)

    def dot(a, b):
        return jnp.dot(a, b, preferred_element_type=jnp.float32)

    def dot_t(a, b):
        return lax.dot_general(a, b, (((1,), (1,)), ((), ())), preferred_element_type=jnp.float32)

    barrier = pltpu.get_barrier_semaphore()
    for d in range(1, n_col):
        pl.semaphore_signal(
            barrier, inc=1, device_id={"col": lax.rem(me + d, n_col)}, device_id_type=MESH
        )
    across = [me, x_peer, diagonal] + [index(f, mid, core) for f in planes[1:]]
    for col in across:
        pl.semaphore_signal(
            barrier, inc=1, device_id={"col": col, "orb": other}, device_id_type=MESH
        )

    def piece(p, k):
        start = p * (2 * half) + k * half
        return screen.at[:, pl.ds(pl.multiple_of(start, half), half)]

    def columns_of(ref, k):
        return ref.at[:, pl.ds(pl.multiple_of(k * half, half), half)]

    loads = [
        pltpu.make_async_copy(src, dst, load_sem.at[n])
        for n, (src, dst) in enumerate(
            (
                (vir_energy, e_vir), (slab_vir, raw_vir), (occ_energy, e_occ), (slab_occ, raw_occ),
                (columns_of(vir, other), ov.at[other, pl.ds(0, n_vir)]),
                (columns_of(vir, part), ov.at[part, pl.ds(0, n_vir)]),
                (columns_of(occ, part), od.at[part, pl.ds(0, n_occ)]),
                (piece(me, part), screens.at[me]),
            )
        )
    ]
    for load in loads:
        load.start()
    for ref, n in ((ov, n_vir), (od, n_occ)):
        short = ref.shape[1] - n
        if short:
            for k in range(2):
                ref[k, pl.ds(n, short)] = jnp.zeros((short, half), kind)
    for load in loads[:4]:
        load.wait()
    sv[me, :, :n_vir] = (wide(raw_vir[...]) * jnp.exp(-e_vir[...])[None, :]).astype(kind)
    if sv.shape[2] > n_vir:
        sv[me, :, n_vir:] = jnp.zeros((block, sv.shape[2] - n_vir), kind)
    so[me, part, :, :n_occ] = (wide(raw_occ[...]) * jnp.exp(e_occ[...])[None, :]).astype(kind)
    if so.shape[3] > n_occ:
        so[me, part, :, n_occ:] = jnp.zeros((block, so.shape[3] - n_occ), kind)
    pl.semaphore_wait(barrier, n_col - 1 + len(across))

    sends = []

    def push(src, dst, send, recv, device, only=None, shared=False):
        copy = pltpu.make_async_remote_copy(
            src_ref=src, dst_ref=dst, send_sem=send, recv_sem=recv,
            device_id=device, device_id_type=MESH,
        )
        if only is None:
            copy.start()
        else:
            pl.when(only)(copy.start)
        if not shared:
            sends.append((only, copy))
        return copy

    slabs = (sv, so)

    def give(k, col, target, only=None, chain=False):
        push(slabs[k].at[col], slabs[k].at[col], slab_send.at[k, int(chain)], slab_recv.at[k, col],
             {"col": target}, only, True)

    def sent(ref, n, send):
        ref = ref.at[pl.ds(0, n)]
        pltpu.make_async_remote_copy(
            src_ref=ref, dst_ref=ref, send_sem=send, recv_sem=swap_recv.at[0],
            device_id={"orb": other}, device_id_type=MESH,
        ).wait_send()

    def arrived(k, col, only=None):
        def act():
            landed(slabs[k].at[col], swap_send.at[0], slab_recv.at[k, col], {"orb": other})

        act() if only is None else pl.when(only)(act)

    def give_own(k):
        give(k, me, x_peer)
        give(k, me, index(planes[1], mid, core))
        give(k, me, index(planes[3], mid, core), inner, True)
        give(k, me, core_peer)

    def relay(k, j, only=None):
        col = index(planes[j], mid, core)
        arrived(k, col, only)
        step = planes[3 if j == 1 else 1]
        if only is not outer and (k, j) != (0, 1):
            give(k, col, index(step, mid, core), inner, True)
        give(k, col, x_peer, only)
        give(k, col, core_peer, only)

    def give_middle():
        give(0, index(planes[1], mid, core), index(planes[3], mid, core), inner, True)

    def cross(k, j, only=None):
        col = index(planes[j], 1 - mid, core)
        arrived(k, col, only)
        give(k, col, core_peer, only)

    def settle(k, j, only=None):
        arrived(k, index(planes[j], mid, 1 - core), only)
        arrived(k, index(planes[j], 1 - mid, 1 - core), only)

    def give_screen(target):
        push(piece(target, part), screens.at[me], screen_send, screen_recv.at[far],
             {"col": target}, None, True)

    def give_screens(j):
        for m, c in ((mid, core), (1 - mid, core), (mid, 1 - core), (1 - mid, 1 - core)):
            give_screen(index(planes[j], m, c))

    def screened(j):
        if j == 0:
            loads[7].wait()
        ref = screens.at[pl.ds(planes[j] * 4, 4) if j else pl.ds(0, 3)]
        landed(ref, swap_send.at[0], screen_recv.at[planes[j]], {"orb": other})

    def plane(j):
        return pl.ds(planes[j] * 4, 4)

    def shade(j, cut):
        return wide(screens[plane(j), :, cut].reshape((rows, -1)))

    cuts = [slice(start, start + 256) for start in range(0, half, 256)]
    swaps = {}

    def chip(m):
        return pl.ds(planes[0] * 4 + 2 * m, 2), pl.ds(pl.multiple_of(m * (2 * block), 2 * block), 2 * block)

    def when(only, act):
        act() if only is None else pl.when(only)(act)

    def make_green(j, m=None, only=None):
        owners, lines = (plane(j), pl.ds(0, rows)) if m is None else chip(m)
        slot = j if m is not other_mid else n_far

        def fill(target, k, dtype):
            slab = sv[owners].reshape((-1, sv.shape[2]))
            for cut in cuts:
                target[j, lines, cut] = dot(slab, ov[k, :, cut]).astype(dtype)

        when(only, functools.partial(fill, green_out, other, kind))
        swaps["green", slot] = push(green_out.at[j, lines], green_in.at[j, lines], green_send.at[slot],
                                    green_recv.at[slot], {"orb": other}, only)
        when(only, functools.partial(fill, green, part, jnp.float32))

    def make_side(j):
        for cut in cuts:
            value = dot(so[plane(j), 0].reshape((rows, -1)), od[0, :, cut])
            value = value + dot(so[plane(j), 1].reshape((rows, -1)), od[1, :, cut])
            side[j, part, :, cut] = (value * shade(j, cut)).astype(kind)
        swaps["side", j] = push(side.at[j, part], side.at[j, part], side_send.at[j],
                                side_recv.at[j], {"orb": other})

    lines = block // 2
    mine = pl.ds(pl.multiple_of(part * lines, lines), lines)
    theirs = pl.ds(pl.multiple_of(other * lines, lines), lines)

    class Reduce:
        def __init__(self, n, part, near, out_x, in_x, total, out_far):
            self.n, self.part, self.near, self.out_x, self.in_x = n, part, near, out_x, in_x
            self.total, self.out_far = total, out_far
            self.first, self.second = {}, {}

        def to_core(self, j, slots=(0, 1)):
            n = self.n
            for slot in slots:
                m = (other_mid, mid)[slot]
                self.first[j, slot] = push(
                    self.part.at[j, m, 1 - core], self.near.at[j, slot],
                    near_send.at[n, j, slot], near_recv.at[n, j, slot], {"col": core_peer},
                )

        def to_mid(self, j):
            n = self.n
            self.first[j, 0].wait_recv()
            self.out_x[j] = (wide(self.part[j, 1 - mid, core]) + wide(self.near[j, 0])).astype(kind)
            self.second[j] = push(self.out_x.at[j], self.in_x.at[j], x_send.at[n, j],
                                  x_recv.at[n, j], {"col": x_peer})
            self.keep(j)

        def keep(self, j):
            self.first[j, 1].wait_recv()
            self.total[j] = wide(self.part[j, mid, core]) + wide(self.near[j, 1])

        def crossed(self, j):
            self.second[j].wait_recv()
            self.total[j] = self.total[j] + wide(self.in_x[j])

    class ReduceVir(Reduce):
        def to_far(self, j):
            self.crossed(j)
            if j == n_far - 1:
                pl.when(inner)(functools.partial(self.take, planes[2], j))
            if j > 0:
                out_far_vir[j - 1] = self.total[j].astype(kind)
                target, slot = planes[j], far
                if j == n_far - 1:
                    col = index(target, mid, core)
                    for n, (where, device) in enumerate(
                        ((mine, {"col": col}), (theirs, {"col": col, "orb": other}))
                    ):
                        push(out_far_vir.at[j - 1, where], in_last_vir.at[part],
                             last_send.at[n], last_recv.at[part], device)
                    return
                if j == 2:
                    target = lax.select(inner, planes[2], planes[1])
                    slot = lax.select(inner, far, planes[3])
                push(out_far_vir.at[j - 1], in_far_vir.at[slot], far_send.at[j - 1],
                     far_recv.at[slot], {"col": index(target, mid, core)})

        def take(self, source, j):
            landed(in_far_vir.at[source], swap_send.at[0], far_recv.at[source], {"orb": other})
            self.total[j] = self.total[j] + wide(in_far_vir[source])

        def gather(self):
            self.take(planes[1], 0)
            pl.when(outer)(functools.partial(self.take, planes[2], 0))
            half_vir[...] = self.total[0, theirs].astype(kind)
            self.last = push(half_vir, in_half_vir, half_send.at[0], half_recv.at[0], {"orb": other})

        def end(self):
            self.last.wait_recv()
            for k in range(2):
                landed(in_last_vir.at[k], swap_send.at[0], last_recv.at[k], {"orb": other})
            own = self.total[0, mine] + wide(in_last_vir[part])
            return own, wide(in_half_vir[...]) + wide(in_last_vir[other])

    class ReduceOcc(Reduce):
        def to_far(self, j):
            self.crossed(j)
            if j == n_far - 1:
                pl.when(inner)(self.join)
            out_far_occ[j - 1] = self.total[j].astype(kind)
            col = index(planes[j], mid, core)
            if j == 2:
                self.joined = push(out_far_occ.at[1], joint_occ, joint_send, joint_recv,
                                   {"col": index(planes[1], mid, core)}, outer)
            for n, (where, device) in enumerate(
                ((mine, {"col": col}), (theirs, {"col": col, "orb": other}))
            ):
                push(out_far_occ.at[j - 1, where], in_far_occ.at[far, part], far_send.at[n_far - 1 + 2 * (j - 1) + n],
                     occ_recv.at[far, part], device, inner if j == 2 else None)

        def join(self):
            self.joined.wait_recv()
            self.total[n_far - 1] = self.total[n_far - 1] + wide(joint_occ[...])

        def own_half(self):
            self.keep(0)
            half_occ[...] = self.total[0, theirs].astype(kind)
            self.last = push(half_occ, in_half_occ, half_send.at[1], half_recv.at[1], {"orb": other})

        def direct(self):
            n = 0
            for c, col in ((core, x_peer), (1 - core, diagonal)):
                for where, device in ((mine, {"col": col}), (theirs, {"col": col, "orb": other})):
                    push(part_occ.at[0, other_mid, c, where], in_own_occ.at[core, part],
                         own_send.at[n], own_recv.at[core, part], device)
                    n += 1

        def take(self, ref, recv):
            landed(ref, swap_send.at[0], recv, {"orb": other})
            value_occ[...] = value_occ[...] + wide(ref[...])

        def take_far(self, source):
            for k in range(2):
                self.take(in_far_occ.at[source, k], occ_recv.at[source, k])

        def collect(self):
            self.last.wait_recv()
            value_occ[...] = self.total[0, mine] + wide(in_half_occ[...])

        def gather(self):
            self.take_far(planes[1])
            pl.when(outer)(functools.partial(self.take_far, planes[2]))
            self.take_far(planes[3])
            for c in range(2):
                for k in range(2):
                    self.take(in_own_occ.at[c, k], own_recv.at[c, k])

    of_vir = ReduceVir(0, part_vir, near_vir, out_x_vir, in_x_vir, sum_vir, out_far_vir)
    of_occ = ReduceOcc(1, part_occ, near_occ, out_x_occ, in_x_occ, sum_occ, out_far_occ)

    def project_vir(j):
        swaps["side", j].wait_recv()
        width = part_vir.shape[-1]
        for start in range(0, width, 256):
            cut = slice(start, min(start + 256, width))
            term = dot_t(side[j, 0], ov[0, cut]) + dot_t(side[j, 1], ov[1, cut])
            part_vir[j, :, :, :, cut] = term.astype(kind).reshape((2, 2, block, -1))
        of_vir.to_core(j)

    def project_occ(j, m=None):
        slot = j if m is not other_mid else n_far
        swaps["green", slot].wait_recv()
        owners, lines = (plane(j), pl.ds(0, rows)) if m is None else chip(m)
        shades = wide(screens[owners].reshape((-1, half)))
        value = (green[j, lines] + wide(green_in[j, lines])) * shades
        value = value.astype(kind)
        wide_occ = od.shape[1]
        for k in range(2):
            term = dot_t(value, od[k]).astype(kind).reshape((-1, 2, block, wide_occ))
            cut = slice(k * wide_occ, (k + 1) * wide_occ)
            if m is None:
                part_occ[j, :, :, :, cut] = term
            else:
                part_occ[j, m, :, :, cut] = term[0]
        if m is other_mid:
            of_occ.direct()
        else:
            of_occ.to_core(j, (0, 1) if m is None else (1,))

    push(so.at[me, part], so.at[me, part], swap_send.at[0], swap_recv.at[0], {"orb": other})
    swap = push(columns_of(occ, other), od.at[part, pl.ds(0, n_occ)], swap_send.at[1],
                swap_recv.at[1], {"orb": other})
    give_own(0)
    for load in loads[4:7]:
        load.wait()
    arrived(0, core_peer)
    make_green(0, mid)
    landed(so.at[me, other], swap_send.at[0], swap_recv.at[0], {"orb": other})
    give_own(1)
    for target in (x_peer, core_peer, diagonal):
        give_screen(target)
    give_screens(1)
    cross(1, 0)
    relay(1, 1)
    relay(1, 3, inner)
    relay(0, 1)
    give_screens(2)
    settle(1, 0)
    screened(0)
    swap.wait_recv()
    make_side(0)
    cross(0, 0)
    relay(1, 2, inner)
    give_screens(3)
    relay(0, 3, inner)
    cross(1, 1)
    settle(1, 1)
    screened(1)
    make_side(1)
    relay(1, 2, outer)
    cross(0, 1)
    settle(0, 1)
    make_green(1)
    give_middle()
    project_vir(0)
    relay(1, 3, outer)
    cross(1, 2)
    project_occ(0, mid)
    of_vir.to_mid(0)
    of_occ.own_half()
    settle(1, 2)
    screened(2)
    make_side(2)
    cross(1, 3)
    relay(0, 2, outer)
    relay(0, 2, inner)
    project_vir(1)
    settle(1, 3)
    screened(3)
    make_side(3)
    of_vir.to_mid(1)
    cross(0, 2)
    of_vir.to_far(0)
    settle(0, 2)
    make_green(2)
    relay(0, 3, outer)
    project_vir(2)
    project_occ(1)
    of_vir.to_far(1)
    of_vir.to_mid(2)
    of_occ.to_mid(1)
    cross(0, 3)
    settle(0, 3)
    make_green(3)
    arrived(0, diagonal)
    make_green(0, other_mid)
    project_vir(3)
    of_vir.to_far(2)
    of_vir.to_mid(3)
    project_occ(2)
    of_occ.to_far(1)
    of_occ.to_mid(2)
    of_vir.to_far(3)
    project_occ(3)
    of_occ.to_mid(3)
    of_occ.to_far(2)
    project_occ(0, other_mid)
    of_occ.collect()
    of_vir.gather()
    of_occ.to_far(3)
    low = part == 0
    own, peer = of_vir.end()
    own, peer = own[:, :n_vir], peer[:, :n_vir]
    out_vir[:, :n_vir] = jnp.where(low, own, peer).astype(kind)
    out_vir[:, n_vir:] = jnp.where(low, peer, own).astype(kind)
    of_occ.gather()
    value = value_occ[...]
    wide_occ = od.shape[1]
    out_occ[:, :n_occ] = value[:, :n_occ].astype(kind)
    out_occ[:, n_occ:] = value[:, wide_occ : wide_occ + n_occ].astype(kind)
    sent(screens, n_col - 1, screen_send)
    for k in range(2):
        sent(slabs[k], 3 + 2 * (n_far - 1) + n_far, slab_send.at[k, 0])
        pl.when(inner)(functools.partial(sent, slabs[k], n_far, slab_send.at[k, 1]))
    for only, copy in sends:
        if only is None:
            copy.wait_send()
        else:
            pl.when(only)(copy.wait_send)


def fused(n_col, slab_occ, slab_vir, occ, vir, occ_energy, vir_energy, screen):
    up = lambda n: -(-n // 128) * 128
    block = slab_occ.shape[0]
    n_occ, columns = occ.shape
    n_vir = vir.shape[0]
    kind, f32 = slab_occ.dtype, jnp.float32
    half = columns // 2
    wide_occ, wide_vir = up(n_occ), up(n_vir)
    n_far = n_col // 4
    rows = 4 * block
    both = 2 * wide_occ
    dma = pltpu.SemaphoreType.DMA

    def pair(lead, lines, dtype=kind):
        return [pltpu.VMEM(lead + (lines, w), dtype) for w in (wide_vir, both)]

    return pl.pallas_call(
        functools.partial(fused_kernel, n_col),
        out_shape=[pltpu.VMEM((block // 2, 2 * n), kind) for n in (n_occ, n_vir)],
        in_specs=[ANY] * 7,
        out_specs=[VMEM] * 2,
        scratch_shapes=[
            pltpu.VMEM(slab_occ.shape, kind),
            pltpu.VMEM(slab_vir.shape, kind),
            pltpu.VMEM(occ_energy.shape, f32),
            pltpu.VMEM(vir_energy.shape, f32),
            pltpu.VMEM((n_col, block, wide_vir), kind),
            pltpu.VMEM((n_col, 2, block, wide_occ), kind),
            pltpu.VMEM((2, wide_vir, half), kind),
            pltpu.VMEM((2, wide_occ, half), kind),
            pltpu.VMEM((n_col, block, half), kind),
            pltpu.VMEM((n_far, rows, half), f32),
            pltpu.VMEM((n_far, rows, half), kind),
            pltpu.VMEM((n_far, rows, half), kind),
            pltpu.VMEM((n_far, 2, rows, half), kind),
        ]
        + pair((n_far, 2, 2), block)
        + pair((n_far, 2), block)
        + pair((n_far,), block)
        + pair((n_far,), block)
        + pair((n_far,), block, f32)
        + pair((n_far - 1,), block)
        + [
            pltpu.VMEM((n_far, block, wide_vir), kind),
            pltpu.VMEM((block, both), kind),
            pltpu.VMEM((n_far, 2, block // 2, both), kind),
            pltpu.VMEM((2, 2, block // 2, both), kind),
        ]
        + pair((), block // 2)
        + pair((), block // 2)
        + [pltpu.VMEM((block // 2, both), f32), pltpu.VMEM((2, block // 2, wide_vir), kind)]
        + [
            dma((8,)), dma((2, 2)), dma((2, n_col)), dma((2,)), dma((2,)), dma, dma((n_far,)),
            dma((n_far + 1,)), dma((n_far + 1,)), dma((n_far,)), dma((n_far,)),
            dma((2, n_far, 2)), dma((2, n_far, 2)), dma((2, n_far)), dma((2, n_far)),
            dma((3 * (n_far - 1),)), dma((n_far,)), dma((2,)), dma((2,)), dma, dma,
            dma((1,)), dma((n_far, 2)), dma((4,)), dma((2, 2)), dma((2,)), dma((2,)),
        ],
        compiler_params=pltpu.CompilerParams(
            collective_id=2, has_side_effects=True, vmem_limit_bytes=60 * 2**20
        ),
    )(slab_occ, slab_vir, occ, vir, occ_energy, vir_energy, screen)


def local(slab_occ, slab_vir, orbitals_occ, orbitals_vir, occ_energy, vir_energy, screened):
    n_orb, n_col = lax.axis_size("orb"), lax.axis_size("col")
    part = lax.axis_index("orb")
    block = slab_occ.shape[0] // n_orb
    n_occ, columns = orbitals_occ.shape
    n_vir = orbitals_vir.shape[0]
    kind = slab_occ.dtype
    if n_col == 16 and n_orb == 2 and block % 16 == 0 and columns % 512 == 0:
        return tuple(
            fused(
                n_col, slab_occ, slab_vir, orbitals_occ, orbitals_vir,
                occ_energy, vir_energy, screened,
            )
        )
    up = lambda n: -(-n // 128) * 128
    scaled_occ = (slab_occ.astype(jnp.float32) * jnp.exp(occ_energy)[None, :]).astype(kind)
    scaled_vir = (slab_vir.astype(jnp.float32) * jnp.exp(-vir_energy)[None, :]).astype(kind)
    start = up(n_vir)
    slab = jnp.concatenate(
        [
            jnp.pad(scaled_vir, ((0, 0), (0, start - n_vir))),
            jnp.pad(scaled_occ, ((0, 0), (0, up(n_occ) - n_occ))),
        ],
        axis=1,
    ).reshape((n_orb, block, start + up(n_occ)))
    mine = lax.dynamic_slice_in_dim(screened, part * block, block, 0)
    mine = mine.reshape((block, n_col, columns)).transpose((1, 0, 2))

    def order(own, peer, n):
        own, peer = own[:, :n], peer[:, :n]
        return jnp.where(
            part == 0, jnp.concatenate([own, peer], 1), jnp.concatenate([peer, own], 1)
        )

    slabs, peer_occ, peer_vir, screens = gather(n_col, slab, orbitals_occ, orbitals_vir, mine)
    slabs = slabs.reshape((2, n_col * block, slab.shape[2]))
    own_slab, peer_slab = slabs[0], slabs[1]

    def dot(a, b):
        return jnp.dot(a, b, preferred_element_type=jnp.float32)

    green_vir = dot(own_slab[:, :n_vir], orbitals_vir) + dot(peer_slab[:, :n_vir], peer_vir)
    green_occ = dot(own_slab[:, start : start + n_occ], orbitals_occ) + dot(
        peer_slab[:, start : start + n_occ], peer_occ
    )
    screen = screens.reshape((n_col * block, columns)).astype(jnp.float32)
    occ_side = (green_vir * screen).astype(kind)
    vir_side = (green_occ * screen).astype(kind)
    dims = (((1,), (1,)), ((), ()))

    def project(side, orbitals):
        term = lax.dot_general(side, orbitals, dims, preferred_element_type=jnp.float32)
        return term.astype(kind).reshape((n_col // 4, 2, 2, block, orbitals.shape[0]))

    vir_own, vir_peer, occ_own, occ_peer = scatter(
        n_col,
        [
            project(vir_side, orbitals_vir),
            project(vir_side, peer_vir),
            project(occ_side, orbitals_occ),
            project(occ_side, peer_occ),
        ],
    )

    return order(occ_own, occ_peer, n_occ), order(vir_own, vir_peer, n_vir)


def solution(mesh):
    return jax.shard_map(
        local,
        mesh=mesh,
        in_specs=(
            P("col", "orb"),
            P("col", "orb"),
            P("orb", "col"),
            P("orb", "col"),
            P("orb"),
            P("orb"),
            P("col", None),
        ),
        out_specs=(P(("col", "orb"), None), P(("col", "orb"), None)),
        check_vma=False,
    )
```

```python
import functools

import jax
import jax.numpy as jnp
from jax import lax
from jax.experimental import pallas as pl
from jax.experimental.pallas import tpu as pltpu
from jax.sharding import PartitionSpec as P

MESH = pl.DeviceIdType.MESH
LAGS = (1, 2)
ANY = pl.BlockSpec(memory_space=pl.ANY)
VMEM = pl.BlockSpec(memory_space=pltpu.VMEM)


def place(n_col):
    me = lax.axis_index("col")
    far, mid, core = me // 4, lax.rem(me // 2, 2), lax.rem(me, 2)
    return me, far, mid, core, lambda f, m, c: (f * 2 + m) * 2 + c


def greet(cols, orbs):
    barrier = pltpu.get_barrier_semaphore()
    for col in cols:
        pl.semaphore_signal(barrier, inc=1, device_id={"col": col}, device_id_type=MESH)
    for orb in orbs:
        pl.semaphore_signal(barrier, inc=1, device_id={"orb": orb}, device_id_type=MESH)
    pl.semaphore_wait(barrier, len(cols) + len(orbs))


def sender():
    sends = []

    def push(src, dst, send, recv, device):
        copy = pltpu.make_async_remote_copy(
            src_ref=src, dst_ref=dst, send_sem=send, recv_sem=recv,
            device_id=device, device_id_type=MESH,
        )
        copy.start()
        sends.append(copy)
        return copy

    return sends, push


def landed(ref, send, recv, device):
    pltpu.make_async_remote_copy(
        src_ref=ref, dst_ref=ref, send_sem=send, recv_sem=recv,
        device_id=device, device_id_type=MESH,
    ).wait_recv()


def spread(n_col, push, swap, slab, screen, slabs, screens, local_sem,
           orb_send, slab_send, slab_recv, screen_send, screen_recv):
    n_far = n_col // 4
    me, far, mid, core, index = place(n_col)
    part = lax.axis_index("orb")
    other = 1 - part
    others = [lax.rem(me + d, n_col) for d in range(1, n_col)]

    def arrived(k, col):
        landed(slabs.at[k, col], orb_send.at[swap], slab_recv.at[k, col], {"orb": other})

    counter = [0]

    def give(k, col, target, src=None):
        push(
            slabs.at[k, col] if src is None else src, slabs.at[k, col],
            slab_send.at[counter[0]], slab_recv.at[k, col], {"col": target},
        )
        counter[0] += 1

    x_peer, core_peer = index(far, 1 - mid, core), index(far, mid, 1 - core)
    fars = [lax.rem(far + d, n_far) for d in range(1, n_far)]
    own = slab.at[part]
    targets = [index(f, mid, core) for f in fars] + [x_peer, core_peer]
    for target in targets:
        give(0, me, target, own)
    arrived(1, me)
    for target in targets:
        give(1, me, target)
    for n, p in enumerate(others):
        push(screen.at[p], screens.at[me], screen_send.at[n], screen_recv.at[me], {"col": p})
    local = [
        pltpu.make_async_copy(own, slabs.at[0, me], local_sem.at[0]),
        pltpu.make_async_copy(screen.at[me], screens.at[me], local_sem.at[1]),
    ]
    for copy in local:
        copy.start()
    for f in fars:
        col = index(f, mid, core)
        for k in range(2):
            arrived(k, col)
            give(k, col, x_peer)
            give(k, col, core_peer)
    for f in [far] + fars:
        col = index(f, 1 - mid, core)
        for k in range(2):
            arrived(k, col)
            give(k, col, core_peer)
    for f in [far] + fars:
        for m in (mid, 1 - mid):
            for k in range(2):
                arrived(k, index(f, m, 1 - core))
    for p in others:
        landed(screens.at[p], orb_send.at[swap], screen_recv.at[p], {"orb": other})
    for copy in local:
        copy.wait()


def spread_semaphores(n_col):
    n_far = n_col // 4
    dma = pltpu.SemaphoreType.DMA
    n_give = 2 * ((n_far + 1) + 2 * (n_far - 1) + n_far)
    return [dma((n_give,)), dma((2, n_col)), dma((n_col,)), dma((n_col,))]


def gather_kernel(
    n_col, slab, occ, vir, screen, slabs, peer_occ, peer_vir, screens,
    local_sem, orb_send, orb_recv, slab_send, slab_recv, screen_send, screen_recv,
):
    me = lax.axis_index("col")
    other = 1 - lax.axis_index("orb")
    greet([lax.rem(me + d, n_col) for d in range(1, n_col)], [other])
    sends, push = sender()
    push(slab.at[other], slabs.at[1, me], orb_send.at[2], slab_recv.at[1, me], {"orb": other})
    push(vir, peer_vir, orb_send.at[0], orb_recv.at[0], {"orb": other})
    push(occ, peer_occ, orb_send.at[1], orb_recv.at[1], {"orb": other})
    spread(n_col, push, 2, slab, screen, slabs, screens, local_sem,
           orb_send, slab_send, slab_recv, screen_send, screen_recv)
    for n, ref in ((0, peer_vir), (1, peer_occ)):
        landed(ref, orb_send.at[n], orb_recv.at[n], {"orb": other})
    for copy in sends:
        copy.wait_send()


def gather(n_col, slab, occ, vir, screen):
    dma = pltpu.SemaphoreType.DMA
    return pl.pallas_call(
        functools.partial(gather_kernel, n_col),
        out_shape=(
            jax.ShapeDtypeStruct((2, n_col) + slab.shape[1:], slab.dtype),
            jax.ShapeDtypeStruct(occ.shape, occ.dtype),
            jax.ShapeDtypeStruct(vir.shape, vir.dtype),
            jax.ShapeDtypeStruct(screen.shape, screen.dtype),
        ),
        in_specs=[ANY] * 4,
        out_specs=(ANY,) * 4,
        scratch_shapes=[dma((2,)), dma((3,)), dma((2,))] + spread_semaphores(n_col),
        compiler_params=pltpu.CompilerParams(collective_id=0, has_side_effects=True),
    )(slab, occ, vir, screen)


def reduce_rows(n_col, pieces, ins, refs, ready, finish, flush=()):
    n_far = n_col // 4
    near, out_x, in_x, total, out_far, in_far = [
        refs[i * pieces : (i + 1) * pieces] for i in range(6)
    ]
    near_send, near_recv, x_send, x_recv, far_send, far_recv = refs[6 * pieces :]
    me, far, mid, core, index = place(n_col)
    x_peer, core_peer = index(far, 1 - mid, core), index(far, mid, 1 - core)
    fars = [lax.rem(far + d, n_far) for d in range(1, n_far)]
    sends, push = sender()
    wide = lambda value: value.astype(jnp.float32)
    first, second, third = [], [], []

    def to_core(t):
        ready(t)
        first.append(
            [
                push(
                    ins[t].at[:, m, 1 - core], near[t].at[slot],
                    near_send.at[t, slot], near_recv.at[t, slot], {"col": core_peer},
                )
                for slot, m in ((0, 1 - mid), (1, mid))
            ]
        )

    def to_mid(t):
        first[t][0].wait_recv()
        for f in range(n_far):
            out_x[t][f] = (wide(ins[t][f, 1 - mid, core]) + wide(near[t][0, f])).astype(
                out_x[t].dtype
            )
        second.append(push(out_x[t], in_x[t], x_send.at[t], x_recv.at[t], {"col": x_peer}))
        first[t][1].wait_recv()
        for f in range(n_far):
            total[t][f] = wide(ins[t][f, mid, core]) + wide(near[t][1, f])

    def to_far(t):
        second[t].wait_recv()
        for f in range(n_far):
            total[t][f] = total[t][f] + wide(in_x[t][f])
            out_far[t][f] = total[t][f].astype(out_far[t].dtype)
        for d, f in enumerate(fars):
            third.append(
                push(
                    out_far[t].at[f], in_far[t].at[d],
                    far_send.at[t, d], far_recv.at[t, d], {"col": index(f, mid, core)},
                )
            )

    acts, count = (to_core, to_mid, to_far), [0, 0, 0]

    def advance(stage, end):
        while count[stage] < end:
            acts[stage](count[stage])
            count[stage] += 1

    for t in range(pieces):
        if t in flush:
            advance(1, t)
            advance(2, t)
        advance(0, t + 1)
        advance(1, t + 1 - LAGS[0])
        advance(2, t + 1 - sum(LAGS))
    advance(1, pieces)
    advance(2, pieces)
    for t in range(pieces):
        value = total[t][far]
        for d in range(n_far - 1):
            third[t * (n_far - 1) + d].wait_recv()
            value = value + wide(in_far[t][d])
        finish(t, value)
    for made in sends:
        made.wait_send()


def reduce_scratch(n_col, block, kind):
    n_far = n_col // 4
    dma = pltpu.SemaphoreType.DMA
    pieces = len(block)

    def buffers(lead, dtype=kind):
        return [pltpu.VMEM(lead + tuple(b), dtype) for b in block]

    return (
        buffers((2, n_far))
        + buffers((n_far,))
        + buffers((n_far,))
        + buffers((n_far,), jnp.float32)
        + buffers((n_far,))
        + buffers((n_far - 1,))
        + [
            dma((pieces, 2)), dma((pieces, 2)), dma((pieces,)), dma((pieces,)),
            dma((pieces, n_far - 1)), dma((pieces, n_far - 1)),
        ]
    )


def scatter_kernel(n_col, pieces, *refs):
    me, far, mid, core, index = place(n_col)
    n_far = n_col // 4
    fars = [lax.rem(far + d, n_far) for d in range(1, n_far)]
    greet(
        [index(far, mid, 1 - core), index(far, 1 - mid, core)]
        + [index(f, mid, core) for f in fars],
        [],
    )
    outs = refs[pieces : 2 * pieces]

    def finish(t, value):
        outs[t][...] = value.astype(outs[t].dtype)

    reduce_rows(n_col, pieces, refs[:pieces], refs[2 * pieces :], lambda t: None, finish)


def scatter(n_col, terms):
    pieces = len(terms)
    block, kind = [t.shape[-2:] for t in terms], terms[0].dtype
    return pl.pallas_call(
        functools.partial(scatter_kernel, n_col, pieces),
        out_shape=[jax.ShapeDtypeStruct(b, kind) for b in block],
        in_specs=[VMEM] * pieces,
        out_specs=[VMEM] * pieces,
        scratch_shapes=reduce_scratch(n_col, block, kind),
        compiler_params=pltpu.CompilerParams(collective_id=1, has_side_effects=True),
    )(*terms)


def order(far, j):
    if j == 0:
        return far
    if j == 1:
        return far + 1 - 2 * lax.rem(far, 2)
    return lax.rem(far + 2, 4) if j == 2 else 3 - far


def fused_kernel(n_col, slab_occ, slab_vir, occ, vir, occ_energy, vir_energy, screen, *refs):
    out_occ, out_vir = refs[:2]
    (raw_occ, raw_vir, e_occ, e_vir, sv, so, ov, od, screens, green, green_out, green_in, side,
     part_vir, part_occ, near_vir, near_occ, out_x_vir, out_x_occ, in_x_vir, in_x_occ,
     sum_vir, sum_occ, out_far_vir, out_far_occ, in_far_vir, joint_occ, in_far_occ, in_own_occ,
     half_vir, half_occ, in_half_vir, in_half_occ, value_occ, in_last_vir) = refs[2:37]
    (load_sem, slab_send, slab_recv, swap_send, swap_recv, screen_send, screen_recv,
     green_send, green_recv, side_send, side_recv, near_send, near_recv, x_send, x_recv,
     far_send, far_recv, half_send, half_recv, joint_send, joint_recv, occ_send, occ_recv,
     own_send, own_recv, last_send, last_recv) = refs[37:]
    n_far = n_col // 4
    me, far, mid, core, index = place(n_col)
    part = lax.axis_index("orb")
    other = 1 - part
    x_peer, core_peer = index(far, 1 - mid, core), index(far, mid, 1 - core)
    other_mid = 1 - mid
    diagonal = index(far, other_mid, 1 - core)
    inner = lax.rem(far, 3) > 0
    outer = lax.rem(far, 3) == 0
    planes = [order(far, j) for j in range(n_far)]
    n_occ = occ.shape[0]
    n_vir = vir.shape[0]
    half = ov.shape[2]
    block = sv.shape[1]
    rows = 4 * block
    kind = sv.dtype
    wide = lambda value: value.astype(jnp.float32)

    def dot(a, b):
        return jnp.dot(a, b, preferred_element_type=jnp.float32)

    def dot_t(a, b):
        return lax.dot_general(a, b, (((1,), (1,)), ((), ())), preferred_element_type=jnp.float32)

    barrier = pltpu.get_barrier_semaphore()
    for d in range(1, n_col):
        pl.semaphore_signal(
            barrier, inc=1, device_id={"col": lax.rem(me + d, n_col)}, device_id_type=MESH
        )
    across = [me, x_peer, diagonal] + [index(f, mid, core) for f in planes[1:]]
    for col in across:
        pl.semaphore_signal(
            barrier, inc=1, device_id={"col": col, "orb": other}, device_id_type=MESH
        )

    def piece(p, k):
        start = p * (2 * half) + k * half
        return screen.at[:, pl.ds(pl.multiple_of(start, half), half)]

    def columns_of(ref, k):
        return ref.at[:, pl.ds(pl.multiple_of(k * half, half), half)]

    loads = [
        pltpu.make_async_copy(src, dst, load_sem.at[n])
        for n, (src, dst) in enumerate(
            (
                (vir_energy, e_vir), (slab_vir, raw_vir), (occ_energy, e_occ), (slab_occ, raw_occ),
                (columns_of(vir, other), ov.at[other, pl.ds(0, n_vir)]),
                (columns_of(vir, part), ov.at[part, pl.ds(0, n_vir)]),
                (columns_of(occ, part), od.at[part, pl.ds(0, n_occ)]),
                (piece(me, part), screens.at[me]),
            )
        )
    ]
    for load in loads:
        load.start()
    for ref, n in ((ov, n_vir), (od, n_occ)):
        short = ref.shape[1] - n
        if short:
            for k in range(2):
                ref[k, pl.ds(n, short)] = jnp.zeros((short, half), kind)
    for load in loads[:4]:
        load.wait()
    sv[me, :, :n_vir] = (wide(raw_vir[...]) * jnp.exp(-e_vir[...])[None, :]).astype(kind)
    if sv.shape[2] > n_vir:
        sv[me, :, n_vir:] = jnp.zeros((block, sv.shape[2] - n_vir), kind)
    so[me, part, :, :n_occ] = (wide(raw_occ[...]) * jnp.exp(e_occ[...])[None, :]).astype(kind)
    if so.shape[3] > n_occ:
        so[me, part, :, n_occ:] = jnp.zeros((block, so.shape[3] - n_occ), kind)
    pl.semaphore_wait(barrier, n_col - 1 + len(across))

    sends = []

    def push(src, dst, send, recv, device, only=None, shared=False):
        copy = pltpu.make_async_remote_copy(
            src_ref=src, dst_ref=dst, send_sem=send, recv_sem=recv,
            device_id=device, device_id_type=MESH,
        )
        if only is None:
            copy.start()
        else:
            pl.when(only)(copy.start)
        if not shared:
            sends.append((only, copy))
        return copy

    slabs = (sv, so)

    def give(k, col, target, only=None, chain=False):
        push(slabs[k].at[col], slabs[k].at[col], slab_send.at[k, int(chain)], slab_recv.at[k, col],
             {"col": target}, only, True)

    def sent(ref, n, send):
        ref = ref if n is None else ref.at[pl.ds(0, n)]
        pltpu.make_async_remote_copy(
            src_ref=ref, dst_ref=ref, send_sem=send, recv_sem=swap_recv.at[0],
            device_id={"orb": other}, device_id_type=MESH,
        ).wait_send()

    def arrived(k, col, only=None):
        def act():
            landed(slabs[k].at[col], swap_send.at[0], slab_recv.at[k, col], {"orb": other})

        act() if only is None else pl.when(only)(act)

    def give_own(k):
        give(k, me, x_peer)
        give(k, me, index(planes[1], mid, core))
        give(k, me, index(planes[3], mid, core), inner, True)
        give(k, me, core_peer)

    def relay(k, j, only=None):
        col = index(planes[j], mid, core)
        arrived(k, col, only)
        step = planes[3 if j == 1 else 1]
        if only is not outer and (k, j) != (0, 1):
            give(k, col, index(step, mid, core), inner, True)
        give(k, col, x_peer, only)
        give(k, col, core_peer, only)

    def give_middle():
        give(0, index(planes[1], mid, core), index(planes[3], mid, core), inner, True)

    def cross(k, j, only=None):
        col = index(planes[j], 1 - mid, core)
        arrived(k, col, only)
        give(k, col, core_peer, only)

    def settle(k, j, only=None):
        arrived(k, index(planes[j], mid, 1 - core), only)
        arrived(k, index(planes[j], 1 - mid, 1 - core), only)

    def give_screen(target):
        push(piece(target, part), screens.at[me], screen_send, screen_recv.at[far],
             {"col": target}, None, True)

    def give_near():
        for target in (x_peer, core_peer, diagonal):
            give_screen(target)

    def give_screens(j):
        for m, c in ((mid, core), (1 - mid, core), (mid, 1 - core), (1 - mid, 1 - core)):
            give_screen(index(planes[j], m, c))

    def screened(j):
        if j == 0:
            loads[7].wait()
        ref = screens.at[pl.ds(planes[j] * 4, 4) if j else pl.ds(0, 3)]
        landed(ref, swap_send.at[0], screen_recv.at[planes[j]], {"orb": other})

    def plane(j):
        return pl.ds(planes[j] * 4, 4)

    def shade(j, cut):
        return wide(screens[plane(j), :, cut].reshape((rows, -1)))

    cuts = [slice(start, start + 256) for start in range(0, half, 256)]
    swaps = {}

    def chip(m):
        return pl.ds(planes[0] * 4 + 2 * m, 2), pl.ds(pl.multiple_of(m * (2 * block), 2 * block), 2 * block)

    def when(only, act):
        act() if only is None else pl.when(only)(act)

    def make_green(j, m=None, only=None):
        owners, lines = (plane(j), pl.ds(0, rows)) if m is None else chip(m)
        slot = j if m is not other_mid else n_far

        def fill(target, k, dtype):
            slab = sv[owners].reshape((-1, sv.shape[2]))
            for cut in cuts:
                target[j, lines, cut] = dot(slab, ov[k, :, cut]).astype(dtype)

        when(only, functools.partial(fill, green_out, other, kind))
        swaps["green", slot] = push(green_out.at[j, lines], green_in.at[j, lines], green_send,
                                    green_recv.at[slot], {"orb": other}, only, True)
        when(only, functools.partial(fill, green, part, jnp.float32))

    def make_side(j):
        for cut in cuts:
            value = dot(so[plane(j), 0].reshape((rows, -1)), od[0, :, cut])
            value = value + dot(so[plane(j), 1].reshape((rows, -1)), od[1, :, cut])
            side[j, part, :, cut] = (value * shade(j, cut)).astype(kind)
        swaps["side", j] = push(side.at[j, part], side.at[j, part], side_send,
                                side_recv.at[j], {"orb": other}, None, True)

    lines = block // 2
    mine = pl.ds(pl.multiple_of(part * lines, lines), lines)
    theirs = pl.ds(pl.multiple_of(other * lines, lines), lines)

    def part_of(q, width):
        if q < n_far - 1:
            return q, pl.ds(0, width)
        return n_far - 1, pl.ds((q - n_far + 1) * (width // 2), width // 2)

    class Reduce:
        def __init__(self, n, part, near, out_x, in_x, total, out_far):
            self.n, self.part, self.near, self.out_x, self.in_x = n, part, near, out_x, in_x
            self.total, self.out_far = total, out_far
            self.first, self.second = {}, {}

        def at(self, q):
            return q, pl.ds(0, self.part.shape[-1])

        def to_core(self, q, slots=(0, 1)):
            n = self.n
            j, cut = self.at(q)
            for slot in slots:
                m = (other_mid, mid)[slot]
                self.first[q, slot] = push(
                    self.part.at[j, m, 1 - core, :, cut], self.near.at[j, slot, :, cut],
                    near_send.at[n], near_recv.at[n, q, slot], {"col": core_peer}, None, True,
                )

        def to_mid(self, q):
            n = self.n
            j, cut = self.at(q)
            self.first[q, 0].wait_recv()
            self.out_x[j, :, cut] = (
                wide(self.part[j, 1 - mid, core, :, cut]) + wide(self.near[j, 0, :, cut])
            ).astype(kind)
            self.second[q] = push(self.out_x.at[j, :, cut], self.in_x.at[j, :, cut], x_send.at[n],
                                  x_recv.at[n, q], {"col": x_peer}, None, True)
            self.keep(q)

        def keep(self, q):
            j, cut = self.at(q)
            self.first[q, 1].wait_recv()
            self.total[j, :, cut] = wide(self.part[j, mid, core, :, cut]) + wide(self.near[j, 1, :, cut])

        def crossed(self, q):
            j, cut = self.at(q)
            self.second[q].wait_recv()
            self.total[j, :, cut] = self.total[j, :, cut] + wide(self.in_x[j, :, cut])

    class ReduceVir(Reduce):
        def at(self, q):
            return part_of(q, self.part.shape[-1])

        def to_far(self, q):
            j, cut = self.at(q)
            self.crossed(q)
            if q == n_far - 1:
                pl.when(inner)(functools.partial(self.arrive, planes[2]))
            if j == n_far - 1:
                pl.when(inner)(functools.partial(self.add, planes[2], j, cut))
            if j > 0:
                out_far_vir[j - 1, :, cut] = self.total[j, :, cut].astype(kind)
                target, slot = planes[j], far
                if j == n_far - 1:
                    col = index(target, mid, core)
                    h = q - j
                    for where, device in ((mine, {"col": col}), (theirs, {"col": col, "orb": other})):
                        push(out_far_vir.at[j - 1, where, cut], in_last_vir.at[part, :, cut],
                             last_send, last_recv.at[h, part], device, None, True)
                    return
                if j == 2:
                    target = lax.select(inner, planes[2], planes[1])
                    slot = lax.select(inner, far, planes[3])
                push(out_far_vir.at[j - 1], in_far_vir.at[slot], far_send.at[j - 1],
                     far_recv.at[slot], {"col": index(target, mid, core)})

        def arrive(self, source):
            landed(in_far_vir.at[source], swap_send.at[0], far_recv.at[source], {"orb": other})

        def add(self, source, j, cut):
            self.total[j, :, cut] = self.total[j, :, cut] + wide(in_far_vir[source, :, cut])

        def take(self, source):
            self.arrive(source)
            self.add(source, 0, pl.ds(0, self.part.shape[-1]))

        def gather(self):
            self.take(planes[1])
            pl.when(outer)(functools.partial(self.take, planes[2]))
            half_vir[...] = self.total[0, theirs].astype(kind)
            self.last = push(half_vir, in_half_vir, half_send.at[0], half_recv.at[0], {"orb": other})

        def end(self):
            self.last.wait_recv()
            for h in range(2):
                cut = self.at(n_far - 1 + h)[1]
                for k in range(2):
                    landed(in_last_vir.at[k, :, cut], swap_send.at[0], last_recv.at[h, k], {"orb": other})
            own = self.total[0, mine] + wide(in_last_vir[part])
            return own, wide(in_half_vir[...]) + wide(in_last_vir[other])

    class ReduceOcc(Reduce):
        def to_far(self, j):
            self.crossed(j)
            if j == n_far - 1:
                pl.when(inner)(self.join)
            out_far_occ[j - 1] = self.total[j].astype(kind)
            col = index(planes[j], mid, core)
            if j == 2:
                self.joined = push(out_far_occ.at[1], joint_occ, joint_send, joint_recv,
                                   {"col": index(planes[1], mid, core)}, outer)
            for n, (where, device) in enumerate(
                ((mine, {"col": col}), (theirs, {"col": col, "orb": other}))
            ):
                push(out_far_occ.at[j - 1, where], in_far_occ.at[far, part], far_send.at[n_far - 1 + 2 * (j - 1) + n],
                     occ_recv.at[far, part], device, inner if j == 2 else None)

        def join(self):
            self.joined.wait_recv()
            self.total[n_far - 1] = self.total[n_far - 1] + wide(joint_occ[...])

        def own_half(self):
            self.keep(0)
            half_occ[...] = self.total[0, theirs].astype(kind)
            self.last = push(half_occ, in_half_occ, half_send.at[1], half_recv.at[1], {"orb": other})

        def direct(self):
            for c, col in ((core, x_peer), (1 - core, diagonal)):
                for where, device in ((mine, {"col": col}), (theirs, {"col": col, "orb": other})):
                    push(part_occ.at[0, other_mid, c, where], in_own_occ.at[core, part],
                         own_send, own_recv.at[core, part], device, None, True)

        def take(self, ref, recv):
            landed(ref, swap_send.at[0], recv, {"orb": other})
            value_occ[...] = value_occ[...] + wide(ref[...])

        def take_far(self, source):
            for k in range(2):
                self.take(in_far_occ.at[source, k], occ_recv.at[source, k])

        def collect(self):
            self.last.wait_recv()
            value_occ[...] = self.total[0, mine] + wide(in_half_occ[...])

        def gather(self):
            self.take_far(planes[1])
            pl.when(outer)(functools.partial(self.take_far, planes[2]))
            self.take_far(planes[3])
            for c in range(2):
                for k in range(2):
                    self.take(in_own_occ.at[c, k], own_recv.at[c, k])

    of_vir = ReduceVir(0, part_vir, near_vir, out_x_vir, in_x_vir, sum_vir, out_far_vir)
    of_occ = ReduceOcc(1, part_occ, near_occ, out_x_occ, in_x_occ, sum_occ, out_far_occ)

    def project_vir(q):
        j, _ = of_vir.at(q)
        swap = swaps["side", j]
        if q <= n_far - 1:
            swap.wait_recv()
        width = part_vir.shape[-1] // (1 if q < n_far - 1 else 2)
        first = (q - j) * width
        for start in range(first, first + width, 256):
            cut = slice(start, min(start + 256, first + width))
            term = dot_t(side[j, 0], ov[0, cut]) + dot_t(side[j, 1], ov[1, cut])
            part_vir[j, :, :, :, cut] = term.astype(kind).reshape((2, 2, block, -1))
        of_vir.to_core(q)

    def project_occ(j, m=None):
        slot = j if m is not other_mid else n_far
        swaps["green", slot].wait_recv()
        owners, lines = (plane(j), pl.ds(0, rows)) if m is None else chip(m)
        shades = wide(screens[owners].reshape((-1, half)))
        value = (green[j, lines] + wide(green_in[j, lines])) * shades
        value = value.astype(kind)
        wide_occ = od.shape[1]
        for k in range(2):
            term = dot_t(value, od[k]).astype(kind).reshape((-1, 2, block, wide_occ))
            cut = slice(k * wide_occ, (k + 1) * wide_occ)
            if m is None:
                part_occ[j, :, :, :, cut] = term
            else:
                part_occ[j, m, :, :, cut] = term[0]
        if m is other_mid:
            of_occ.direct()
        else:
            of_occ.to_core(j, (0, 1) if m is None else (1,))

    push(so.at[me, part], so.at[me, part], swap_send.at[0], swap_recv.at[0], {"orb": other})
    swap = push(columns_of(occ, other), od.at[part, pl.ds(0, n_occ)], swap_send.at[1],
                swap_recv.at[1], {"orb": other})
    give_own(0)
    for load in loads[4:7]:
        load.wait()
    arrived(0, core_peer)
    make_green(0, mid)
    landed(so.at[me, other], swap_send.at[0], swap_recv.at[0], {"orb": other})
    give_own(1)
    give_near()
    give_screens(1)
    cross(1, 0)
    relay(1, 1)
    relay(1, 3, inner)
    relay(0, 1)
    give_screens(2)
    settle(1, 0)
    screened(0)
    swap.wait_recv()
    make_side(0)
    relay(1, 2, inner)
    cross(0, 0)
    give_screens(3)
    relay(0, 3, inner)
    cross(1, 1)
    settle(1, 1)
    screened(1)
    make_side(1)
    relay(1, 2, outer)
    cross(0, 1)
    settle(0, 1)
    make_green(1)
    give_middle()
    project_vir(0)
    relay(1, 3, outer)
    cross(1, 2)
    project_occ(0, mid)
    of_vir.to_mid(0)
    of_occ.own_half()
    settle(1, 2)
    screened(2)
    make_side(2)
    cross(1, 3)
    relay(0, 2, outer)
    relay(0, 2, inner)
    project_vir(1)
    settle(1, 3)
    screened(3)
    make_side(3)
    cross(0, 2)
    of_vir.to_mid(1)
    of_vir.to_far(0)
    settle(0, 2)
    make_green(2)
    relay(0, 3, outer)
    project_vir(2)
    project_occ(1)
    of_vir.to_mid(2)
    of_occ.to_mid(1)
    cross(0, 3)
    settle(0, 3)
    make_green(3)
    arrived(0, diagonal)
    of_vir.to_far(1)
    make_green(0, other_mid)
    project_vir(3)
    project_vir(4)
    of_vir.to_far(2)
    of_vir.to_mid(3)
    of_vir.to_mid(4)
    project_occ(2)
    of_occ.to_mid(2)
    of_vir.to_far(3)
    of_vir.to_far(4)
    project_occ(3)
    of_occ.to_mid(3)
    of_occ.to_far(1)
    of_occ.to_far(2)
    project_occ(0, other_mid)
    of_occ.collect()
    of_vir.gather()
    of_occ.to_far(3)
    low = part == 0
    own, peer = of_vir.end()
    own, peer = own[:, :n_vir], peer[:, :n_vir]
    out_vir[:, :n_vir] = jnp.where(low, own, peer).astype(kind)
    out_vir[:, n_vir:] = jnp.where(low, peer, own).astype(kind)
    of_occ.gather()
    value = value_occ[...]
    wide_occ = od.shape[1]
    out_occ[:, :n_occ] = value[:, :n_occ].astype(kind)
    out_occ[:, n_occ:] = value[:, wide_occ : wide_occ + n_occ].astype(kind)
    sent(screens, n_col - 1, screen_send)
    sent(green_out, None, green_send)
    sent(side, n_far // 2, side_send)
    sent(near_vir, None, near_send.at[0])
    sent(so, 2 * n_far - 1, near_send.at[1])
    sent(out_x_vir, None, x_send.at[0])
    sent(out_x_occ, n_far - 1, x_send.at[1])
    sent(in_last_vir, None, last_send)
    sent(in_own_occ, None, own_send)
    for k in range(2):
        sent(slabs[k], 3 + 2 * (n_far - 1) + n_far, slab_send.at[k, 0])
        pl.when(inner)(functools.partial(sent, slabs[k], n_far, slab_send.at[k, 1]))
    for only, copy in sends:
        if only is None:
            copy.wait_send()
        else:
            pl.when(only)(copy.wait_send)


def fused(n_col, slab_occ, slab_vir, occ, vir, occ_energy, vir_energy, screen):
    up = lambda n: -(-n // 128) * 128
    block = slab_occ.shape[0]
    n_occ, columns = occ.shape
    n_vir = vir.shape[0]
    kind, f32 = slab_occ.dtype, jnp.float32
    half = columns // 2
    wide_occ, wide_vir = up(n_occ), up(n_vir)
    n_far = n_col // 4
    rows = 4 * block
    both = 2 * wide_occ
    dma = pltpu.SemaphoreType.DMA

    def pair(lead, lines, dtype=kind):
        return [pltpu.VMEM(lead + (lines, w), dtype) for w in (wide_vir, both)]

    return pl.pallas_call(
        functools.partial(fused_kernel, n_col),
        out_shape=[pltpu.VMEM((block // 2, 2 * n), kind) for n in (n_occ, n_vir)],
        in_specs=[ANY] * 7,
        out_specs=[VMEM] * 2,
        scratch_shapes=[
            pltpu.VMEM(slab_occ.shape, kind),
            pltpu.VMEM(slab_vir.shape, kind),
            pltpu.VMEM(occ_energy.shape, f32),
            pltpu.VMEM(vir_energy.shape, f32),
            pltpu.VMEM((n_col, block, wide_vir), kind),
            pltpu.VMEM((n_col, 2, block, wide_occ), kind),
            pltpu.VMEM((2, wide_vir, half), kind),
            pltpu.VMEM((2, wide_occ, half), kind),
            pltpu.VMEM((n_col, block, half), kind),
            pltpu.VMEM((n_far, rows, half), f32),
            pltpu.VMEM((n_far, rows, half), kind),
            pltpu.VMEM((n_far, rows, half), kind),
            pltpu.VMEM((n_far, 2, rows, half), kind),
        ]
        + pair((n_far, 2, 2), block)
        + pair((n_far, 2), block)
        + pair((n_far,), block)
        + pair((n_far,), block)
        + pair((n_far,), block, f32)
        + pair((n_far - 1,), block)
        + [
            pltpu.VMEM((n_far, block, wide_vir), kind),
            pltpu.VMEM((block, both), kind),
            pltpu.VMEM((n_far, 2, block // 2, both), kind),
            pltpu.VMEM((2, 2, block // 2, both), kind),
        ]
        + pair((), block // 2)
        + pair((), block // 2)
        + [pltpu.VMEM((block // 2, both), f32), pltpu.VMEM((2, block // 2, wide_vir), kind)]
        + [
            dma((8,)), dma((2, 2)), dma((2, n_col)), dma((2,)), dma((2,)), dma, dma((n_far,)),
            dma, dma((n_far + 1,)), dma, dma((n_far,)),
            dma((2,)), dma((2, n_far + 1, 2)), dma((2,)), dma((2, n_far + 1)),
            dma((3 * (n_far - 1),)), dma((n_far,)), dma((2,)), dma((2,)), dma, dma,
            dma((1,)), dma((n_far, 2)), dma, dma((2, 2)), dma, dma((2, 2)),
        ],
        compiler_params=pltpu.CompilerParams(
            collective_id=2, has_side_effects=True, vmem_limit_bytes=60 * 2**20
        ),
    )(slab_occ, slab_vir, occ, vir, occ_energy, vir_energy, screen)


def local(slab_occ, slab_vir, orbitals_occ, orbitals_vir, occ_energy, vir_energy, screened):
    n_orb, n_col = lax.axis_size("orb"), lax.axis_size("col")
    part = lax.axis_index("orb")
    block = slab_occ.shape[0] // n_orb
    n_occ, columns = orbitals_occ.shape
    n_vir = orbitals_vir.shape[0]
    kind = slab_occ.dtype
    if n_col == 16 and n_orb == 2 and block % 16 == 0 and columns % 512 == 0:
        return tuple(
            fused(
                n_col, slab_occ, slab_vir, orbitals_occ, orbitals_vir,
                occ_energy, vir_energy, screened,
            )
        )
    up = lambda n: -(-n // 128) * 128
    scaled_occ = (slab_occ.astype(jnp.float32) * jnp.exp(occ_energy)[None, :]).astype(kind)
    scaled_vir = (slab_vir.astype(jnp.float32) * jnp.exp(-vir_energy)[None, :]).astype(kind)
    start = up(n_vir)
    slab = jnp.concatenate(
        [
            jnp.pad(scaled_vir, ((0, 0), (0, start - n_vir))),
            jnp.pad(scaled_occ, ((0, 0), (0, up(n_occ) - n_occ))),
        ],
        axis=1,
    ).reshape((n_orb, block, start + up(n_occ)))
    mine = lax.dynamic_slice_in_dim(screened, part * block, block, 0)
    mine = mine.reshape((block, n_col, columns)).transpose((1, 0, 2))

    def order(own, peer, n):
        own, peer = own[:, :n], peer[:, :n]
        return jnp.where(
            part == 0, jnp.concatenate([own, peer], 1), jnp.concatenate([peer, own], 1)
        )

    slabs, peer_occ, peer_vir, screens = gather(n_col, slab, orbitals_occ, orbitals_vir, mine)
    slabs = slabs.reshape((2, n_col * block, slab.shape[2]))
    own_slab, peer_slab = slabs[0], slabs[1]

    def dot(a, b):
        return jnp.dot(a, b, preferred_element_type=jnp.float32)

    green_vir = dot(own_slab[:, :n_vir], orbitals_vir) + dot(peer_slab[:, :n_vir], peer_vir)
    green_occ = dot(own_slab[:, start : start + n_occ], orbitals_occ) + dot(
        peer_slab[:, start : start + n_occ], peer_occ
    )
    screen = screens.reshape((n_col * block, columns)).astype(jnp.float32)
    occ_side = (green_vir * screen).astype(kind)
    vir_side = (green_occ * screen).astype(kind)
    dims = (((1,), (1,)), ((), ()))

    def project(side, orbitals):
        term = lax.dot_general(side, orbitals, dims, preferred_element_type=jnp.float32)
        return term.astype(kind).reshape((n_col // 4, 2, 2, block, orbitals.shape[0]))

    vir_own, vir_peer, occ_own, occ_peer = scatter(
        n_col,
        [
            project(vir_side, orbitals_vir),
            project(vir_side, peer_vir),
            project(occ_side, orbitals_occ),
            project(occ_side, peer_occ),
        ],
    )

    return order(occ_own, occ_peer, n_occ), order(vir_own, vir_peer, n_vir)


def solution(mesh):
    return jax.shard_map(
        local,
        mesh=mesh,
        in_specs=(
            P("col", "orb"),
            P("col", "orb"),
            P("orb", "col"),
            P("orb", "col"),
            P("orb"),
            P("orb"),
            P("col", None),
        ),
        out_specs=(P(("col", "orb"), None), P(("col", "orb"), None)),
        check_vma=False,
    )
```

```python
import functools

import jax
import jax.numpy as jnp
from jax import lax
from jax.experimental import pallas as pl
from jax.experimental.pallas import tpu as pltpu
from jax.sharding import PartitionSpec as P

MESH = pl.DeviceIdType.MESH
LAGS = (1, 2)
ANY = pl.BlockSpec(memory_space=pl.ANY)
VMEM = pl.BlockSpec(memory_space=pltpu.VMEM)


def place(n_col):
    me = lax.axis_index("col")
    far, mid, core = me // 4, lax.rem(me // 2, 2), lax.rem(me, 2)
    return me, far, mid, core, lambda f, m, c: (f * 2 + m) * 2 + c


def greet(cols, orbs):
    barrier = pltpu.get_barrier_semaphore()
    for col in cols:
        pl.semaphore_signal(barrier, inc=1, device_id={"col": col}, device_id_type=MESH)
    for orb in orbs:
        pl.semaphore_signal(barrier, inc=1, device_id={"orb": orb}, device_id_type=MESH)
    pl.semaphore_wait(barrier, len(cols) + len(orbs))


def sender():
    sends = []

    def push(src, dst, send, recv, device):
        copy = pltpu.make_async_remote_copy(
            src_ref=src, dst_ref=dst, send_sem=send, recv_sem=recv,
            device_id=device, device_id_type=MESH,
        )
        copy.start()
        sends.append(copy)
        return copy

    return sends, push


def landed(ref, send, recv, device):
    pltpu.make_async_remote_copy(
        src_ref=ref, dst_ref=ref, send_sem=send, recv_sem=recv,
        device_id=device, device_id_type=MESH,
    ).wait_recv()


def spread(n_col, push, swap, slab, screen, slabs, screens, local_sem,
           orb_send, slab_send, slab_recv, screen_send, screen_recv):
    n_far = n_col // 4
    me, far, mid, core, index = place(n_col)
    part = lax.axis_index("orb")
    other = 1 - part
    others = [lax.rem(me + d, n_col) for d in range(1, n_col)]

    def arrived(k, col):
        landed(slabs.at[k, col], orb_send.at[swap], slab_recv.at[k, col], {"orb": other})

    counter = [0]

    def give(k, col, target, src=None):
        push(
            slabs.at[k, col] if src is None else src, slabs.at[k, col],
            slab_send.at[counter[0]], slab_recv.at[k, col], {"col": target},
        )
        counter[0] += 1

    x_peer, core_peer = index(far, 1 - mid, core), index(far, mid, 1 - core)
    fars = [lax.rem(far + d, n_far) for d in range(1, n_far)]
    own = slab.at[part]
    targets = [index(f, mid, core) for f in fars] + [x_peer, core_peer]
    for target in targets:
        give(0, me, target, own)
    arrived(1, me)
    for target in targets:
        give(1, me, target)
    for n, p in enumerate(others):
        push(screen.at[p], screens.at[me], screen_send.at[n], screen_recv.at[me], {"col": p})
    local = [
        pltpu.make_async_copy(own, slabs.at[0, me], local_sem.at[0]),
        pltpu.make_async_copy(screen.at[me], screens.at[me], local_sem.at[1]),
    ]
    for copy in local:
        copy.start()
    for f in fars:
        col = index(f, mid, core)
        for k in range(2):
            arrived(k, col)
            give(k, col, x_peer)
            give(k, col, core_peer)
    for f in [far] + fars:
        col = index(f, 1 - mid, core)
        for k in range(2):
            arrived(k, col)
            give(k, col, core_peer)
    for f in [far] + fars:
        for m in (mid, 1 - mid):
            for k in range(2):
                arrived(k, index(f, m, 1 - core))
    for p in others:
        landed(screens.at[p], orb_send.at[swap], screen_recv.at[p], {"orb": other})
    for copy in local:
        copy.wait()


def spread_semaphores(n_col):
    n_far = n_col // 4
    dma = pltpu.SemaphoreType.DMA
    n_give = 2 * ((n_far + 1) + 2 * (n_far - 1) + n_far)
    return [dma((n_give,)), dma((2, n_col)), dma((n_col,)), dma((n_col,))]


def gather_kernel(
    n_col, slab, occ, vir, screen, slabs, peer_occ, peer_vir, screens,
    local_sem, orb_send, orb_recv, slab_send, slab_recv, screen_send, screen_recv,
):
    me = lax.axis_index("col")
    other = 1 - lax.axis_index("orb")
    greet([lax.rem(me + d, n_col) for d in range(1, n_col)], [other])
    sends, push = sender()
    push(slab.at[other], slabs.at[1, me], orb_send.at[2], slab_recv.at[1, me], {"orb": other})
    push(vir, peer_vir, orb_send.at[0], orb_recv.at[0], {"orb": other})
    push(occ, peer_occ, orb_send.at[1], orb_recv.at[1], {"orb": other})
    spread(n_col, push, 2, slab, screen, slabs, screens, local_sem,
           orb_send, slab_send, slab_recv, screen_send, screen_recv)
    for n, ref in ((0, peer_vir), (1, peer_occ)):
        landed(ref, orb_send.at[n], orb_recv.at[n], {"orb": other})
    for copy in sends:
        copy.wait_send()


def gather(n_col, slab, occ, vir, screen):
    dma = pltpu.SemaphoreType.DMA
    return pl.pallas_call(
        functools.partial(gather_kernel, n_col),
        out_shape=(
            jax.ShapeDtypeStruct((2, n_col) + slab.shape[1:], slab.dtype),
            jax.ShapeDtypeStruct(occ.shape, occ.dtype),
            jax.ShapeDtypeStruct(vir.shape, vir.dtype),
            jax.ShapeDtypeStruct(screen.shape, screen.dtype),
        ),
        in_specs=[ANY] * 4,
        out_specs=(ANY,) * 4,
        scratch_shapes=[dma((2,)), dma((3,)), dma((2,))] + spread_semaphores(n_col),
        compiler_params=pltpu.CompilerParams(collective_id=0, has_side_effects=True),
    )(slab, occ, vir, screen)


def reduce_rows(n_col, pieces, ins, refs, ready, finish, flush=()):
    n_far = n_col // 4
    near, out_x, in_x, total, out_far, in_far = [
        refs[i * pieces : (i + 1) * pieces] for i in range(6)
    ]
    near_send, near_recv, x_send, x_recv, far_send, far_recv = refs[6 * pieces :]
    me, far, mid, core, index = place(n_col)
    x_peer, core_peer = index(far, 1 - mid, core), index(far, mid, 1 - core)
    fars = [lax.rem(far + d, n_far) for d in range(1, n_far)]
    sends, push = sender()
    wide = lambda value: value.astype(jnp.float32)
    first, second, third = [], [], []

    def to_core(t):
        ready(t)
        first.append(
            [
                push(
                    ins[t].at[:, m, 1 - core], near[t].at[slot],
                    near_send.at[t, slot], near_recv.at[t, slot], {"col": core_peer},
                )
                for slot, m in ((0, 1 - mid), (1, mid))
            ]
        )

    def to_mid(t):
        first[t][0].wait_recv()
        for f in range(n_far):
            out_x[t][f] = (wide(ins[t][f, 1 - mid, core]) + wide(near[t][0, f])).astype(
                out_x[t].dtype
            )
        second.append(push(out_x[t], in_x[t], x_send.at[t], x_recv.at[t], {"col": x_peer}))
        first[t][1].wait_recv()
        for f in range(n_far):
            total[t][f] = wide(ins[t][f, mid, core]) + wide(near[t][1, f])

    def to_far(t):
        second[t].wait_recv()
        for f in range(n_far):
            total[t][f] = total[t][f] + wide(in_x[t][f])
            out_far[t][f] = total[t][f].astype(out_far[t].dtype)
        for d, f in enumerate(fars):
            third.append(
                push(
                    out_far[t].at[f], in_far[t].at[d],
                    far_send.at[t, d], far_recv.at[t, d], {"col": index(f, mid, core)},
                )
            )

    acts, count = (to_core, to_mid, to_far), [0, 0, 0]

    def advance(stage, end):
        while count[stage] < end:
            acts[stage](count[stage])
            count[stage] += 1

    for t in range(pieces):
        if t in flush:
            advance(1, t)
            advance(2, t)
        advance(0, t + 1)
        advance(1, t + 1 - LAGS[0])
        advance(2, t + 1 - sum(LAGS))
    advance(1, pieces)
    advance(2, pieces)
    for t in range(pieces):
        value = total[t][far]
        for d in range(n_far - 1):
            third[t * (n_far - 1) + d].wait_recv()
            value = value + wide(in_far[t][d])
        finish(t, value)
    for made in sends:
        made.wait_send()


def reduce_scratch(n_col, block, kind):
    n_far = n_col // 4
    dma = pltpu.SemaphoreType.DMA
    pieces = len(block)

    def buffers(lead, dtype=kind):
        return [pltpu.VMEM(lead + tuple(b), dtype) for b in block]

    return (
        buffers((2, n_far))
        + buffers((n_far,))
        + buffers((n_far,))
        + buffers((n_far,), jnp.float32)
        + buffers((n_far,))
        + buffers((n_far - 1,))
        + [
            dma((pieces, 2)), dma((pieces, 2)), dma((pieces,)), dma((pieces,)),
            dma((pieces, n_far - 1)), dma((pieces, n_far - 1)),
        ]
    )


def scatter_kernel(n_col, pieces, *refs):
    me, far, mid, core, index = place(n_col)
    n_far = n_col // 4
    fars = [lax.rem(far + d, n_far) for d in range(1, n_far)]
    greet(
        [index(far, mid, 1 - core), index(far, 1 - mid, core)]
        + [index(f, mid, core) for f in fars],
        [],
    )
    outs = refs[pieces : 2 * pieces]

    def finish(t, value):
        outs[t][...] = value.astype(outs[t].dtype)

    reduce_rows(n_col, pieces, refs[:pieces], refs[2 * pieces :], lambda t: None, finish)


def scatter(n_col, terms):
    pieces = len(terms)
    block, kind = [t.shape[-2:] for t in terms], terms[0].dtype
    return pl.pallas_call(
        functools.partial(scatter_kernel, n_col, pieces),
        out_shape=[jax.ShapeDtypeStruct(b, kind) for b in block],
        in_specs=[VMEM] * pieces,
        out_specs=[VMEM] * pieces,
        scratch_shapes=reduce_scratch(n_col, block, kind),
        compiler_params=pltpu.CompilerParams(collective_id=1, has_side_effects=True),
    )(*terms)


def order(far, j):
    if j == 0:
        return far
    if j == 1:
        return far + 1 - 2 * lax.rem(far, 2)
    return lax.rem(far + 2, 4) if j == 2 else 3 - far


def fused_kernel(n_col, slab_occ, slab_vir, occ, vir, occ_energy, vir_energy, screen, *refs):
    out_occ, out_vir = refs[:2]
    (raw_occ, raw_vir, e_occ, e_vir, sv, so, ov, od, screens, green, green_out, green_in, side,
     part_vir, part_occ, near_vir, near_occ, out_x_vir, out_x_occ, in_x_vir, in_x_occ,
     sum_vir, sum_occ, out_far_vir, out_far_occ, in_far_vir, joint_occ, in_far_occ, in_own_occ,
     half_vir, half_occ, in_half_vir, in_half_occ, value_occ, in_last_vir) = refs[2:37]
    (load_sem, slab_send, slab_recv, swap_send, swap_recv, screen_send, screen_recv,
     green_send, green_recv, side_send, side_recv, near_send, near_recv, x_send, x_recv,
     far_send, far_recv, half_send, half_recv, joint_send, joint_recv, occ_send, occ_recv,
     own_send, own_recv, last_send, last_recv) = refs[37:]
    n_far = n_col // 4
    me, far, mid, core, index = place(n_col)
    part = lax.axis_index("orb")
    other = 1 - part
    x_peer, core_peer = index(far, 1 - mid, core), index(far, mid, 1 - core)
    other_mid = 1 - mid
    diagonal = index(far, other_mid, 1 - core)
    inner = lax.rem(far, 3) > 0
    outer = lax.rem(far, 3) == 0
    planes = [order(far, j) for j in range(n_far)]
    n_occ = occ.shape[0]
    n_vir = vir.shape[0]
    half = ov.shape[2]
    block = sv.shape[1]
    rows = 4 * block
    kind = sv.dtype
    wide = lambda value: value.astype(jnp.float32)

    def dot(a, b):
        return jnp.dot(a, b, preferred_element_type=jnp.float32)

    def dot_t(a, b):
        return lax.dot_general(a, b, (((1,), (1,)), ((), ())), preferred_element_type=jnp.float32)

    barrier = pltpu.get_barrier_semaphore()
    for d in range(1, n_col):
        pl.semaphore_signal(
            barrier, inc=1, device_id={"col": lax.rem(me + d, n_col)}, device_id_type=MESH
        )
    across = [me, x_peer, diagonal] + [index(f, mid, core) for f in planes[1:]]
    for col in across:
        pl.semaphore_signal(
            barrier, inc=1, device_id={"col": col, "orb": other}, device_id_type=MESH
        )

    def piece(p, k):
        start = p * (2 * half) + k * half
        return screen.at[:, pl.ds(pl.multiple_of(start, half), half)]

    def columns_of(ref, k):
        return ref.at[:, pl.ds(pl.multiple_of(k * half, half), half)]

    loads = [
        pltpu.make_async_copy(src, dst, load_sem.at[n])
        for n, (src, dst) in enumerate(
            (
                (vir_energy, e_vir), (slab_vir, raw_vir), (occ_energy, e_occ), (slab_occ, raw_occ),
                (columns_of(vir, other), ov.at[other, pl.ds(0, n_vir)]),
                (columns_of(vir, part), ov.at[part, pl.ds(0, n_vir)]),
                (columns_of(occ, part), od.at[part, pl.ds(0, n_occ)]),
                (piece(me, part), screens.at[me]),
            )
        )
    ]
    for load in loads:
        load.start()
    for ref, n in ((ov, n_vir), (od, n_occ)):
        short = ref.shape[1] - n
        if short:
            for k in range(2):
                ref[k, pl.ds(n, short)] = jnp.zeros((short, half), kind)
    for load in loads[:4]:
        load.wait()
    sv[me, :, :n_vir] = (wide(raw_vir[...]) * jnp.exp(-e_vir[...])[None, :]).astype(kind)
    if sv.shape[2] > n_vir:
        sv[me, :, n_vir:] = jnp.zeros((block, sv.shape[2] - n_vir), kind)
    so[me, part, :, :n_occ] = (wide(raw_occ[...]) * jnp.exp(e_occ[...])[None, :]).astype(kind)
    if so.shape[3] > n_occ:
        so[me, part, :, n_occ:] = jnp.zeros((block, so.shape[3] - n_occ), kind)
    pl.semaphore_wait(barrier, n_col - 1 + len(across))

    sends = []

    def push(src, dst, send, recv, device, only=None, shared=False):
        copy = pltpu.make_async_remote_copy(
            src_ref=src, dst_ref=dst, send_sem=send, recv_sem=recv,
            device_id=device, device_id_type=MESH,
        )
        if only is None:
            copy.start()
        else:
            pl.when(only)(copy.start)
        if not shared:
            sends.append((only, copy))
        return copy

    slabs = (sv, so)

    def give(k, col, target, only=None, chain=False):
        push(slabs[k].at[col], slabs[k].at[col], slab_send.at[k, int(chain)], slab_recv.at[k, col],
             {"col": target}, only, True)

    def sent(ref, n, send):
        ref = ref if n is None else ref.at[pl.ds(0, n)]
        pltpu.make_async_remote_copy(
            src_ref=ref, dst_ref=ref, send_sem=send, recv_sem=swap_recv.at[0],
            device_id={"orb": other}, device_id_type=MESH,
        ).wait_send()

    def arrived(k, col, only=None):
        def act():
            landed(slabs[k].at[col], swap_send.at[0], slab_recv.at[k, col], {"orb": other})

        act() if only is None else pl.when(only)(act)

    def give_own(k):
        give(k, me, x_peer)
        give(k, me, index(planes[1], mid, core))
        give(k, me, index(planes[3], mid, core), inner, True)
        give(k, me, core_peer)

    def relay(k, j, only=None):
        col = index(planes[j], mid, core)
        arrived(k, col, only)
        step = planes[3 if j == 1 else 1]
        if only is not outer and (k, j) != (0, 1):
            give(k, col, index(step, mid, core), inner, True)
        give(k, col, x_peer, only)
        give(k, col, core_peer, only)

    def give_middle():
        give(0, index(planes[1], mid, core), index(planes[3], mid, core), inner, True)

    def cross(k, j, only=None):
        col = index(planes[j], 1 - mid, core)
        arrived(k, col, only)
        give(k, col, core_peer, only)

    def settle(k, j, only=None):
        arrived(k, index(planes[j], mid, 1 - core), only)
        arrived(k, index(planes[j], 1 - mid, 1 - core), only)

    def give_screen(target):
        push(piece(target, part), screens.at[me], screen_send, screen_recv.at[far],
             {"col": target}, None, True)

    def give_near():
        for target in (x_peer, core_peer, diagonal):
            give_screen(target)

    def give_screens(j):
        for m, c in ((mid, core), (1 - mid, core), (mid, 1 - core), (1 - mid, 1 - core)):
            give_screen(index(planes[j], m, c))

    def screened(j):
        if j == 0:
            loads[7].wait()
        ref = screens.at[pl.ds(planes[j] * 4, 4) if j else pl.ds(0, 3)]
        landed(ref, swap_send.at[0], screen_recv.at[planes[j]], {"orb": other})

    def plane(j):
        return pl.ds(planes[j] * 4, 4)

    def shade(j, cut):
        return wide(screens[plane(j), :, cut].reshape((rows, -1)))

    cuts = [slice(start, start + 256) for start in range(0, half, 256)]
    swaps = {}

    def chip(m):
        return pl.ds(planes[0] * 4 + 2 * m, 2), pl.ds(pl.multiple_of(m * (2 * block), 2 * block), 2 * block)

    def when(only, act):
        act() if only is None else pl.when(only)(act)

    def make_green(j, m=None, only=None):
        owners, lines = (plane(j), pl.ds(0, rows)) if m is None else chip(m)
        slot = j if m is not other_mid else n_far

        def fill(target, k, dtype):
            slab = sv[owners].reshape((-1, sv.shape[2]))
            for cut in cuts:
                target[j, lines, cut] = dot(slab, ov[k, :, cut]).astype(dtype)

        when(only, functools.partial(fill, green_out, other, kind))
        swaps["green", slot] = push(green_out.at[j, lines], green_in.at[j, lines], green_send,
                                    green_recv.at[slot], {"orb": other}, only, True)
        when(only, functools.partial(fill, green, part, jnp.float32))

    def make_side(j):
        for cut in cuts:
            value = dot(so[plane(j), 0].reshape((rows, -1)), od[0, :, cut])
            value = value + dot(so[plane(j), 1].reshape((rows, -1)), od[1, :, cut])
            side[j, part, :, cut] = (value * shade(j, cut)).astype(kind)
        swaps["side", j] = push(side.at[j, part], side.at[j, part], side_send,
                                side_recv.at[j], {"orb": other}, None, True)

    lines = block // 2
    mine = pl.ds(pl.multiple_of(part * lines, lines), lines)
    theirs = pl.ds(pl.multiple_of(other * lines, lines), lines)

    def part_of(q, width):
        if q < n_far - 1:
            return q, pl.ds(0, width)
        return n_far - 1, pl.ds((q - n_far + 1) * (width // 2), width // 2)

    class Reduce:
        def __init__(self, n, part, near, out_x, in_x, total, out_far):
            self.n, self.part, self.near, self.out_x, self.in_x = n, part, near, out_x, in_x
            self.total, self.out_far = total, out_far
            self.first, self.second = {}, {}

        def at(self, q):
            return q, pl.ds(0, self.part.shape[-1])

        def to_core(self, q, slots=(0, 1)):
            n = self.n
            j, cut = self.at(q)
            for slot in slots:
                m = (other_mid, mid)[slot]
                self.first[q, slot] = push(
                    self.part.at[j, m, 1 - core, :, cut], self.near.at[j, slot, :, cut],
                    near_send.at[n], near_recv.at[n, q, slot], {"col": core_peer}, None, True,
                )

        def to_mid(self, q):
            n = self.n
            j, cut = self.at(q)
            self.first[q, 0].wait_recv()
            self.out_x[j, :, cut] = (
                wide(self.part[j, 1 - mid, core, :, cut]) + wide(self.near[j, 0, :, cut])
            ).astype(kind)
            self.second[q] = push(self.out_x.at[j, :, cut], self.in_x.at[j, :, cut], x_send.at[n],
                                  x_recv.at[n, q], {"col": x_peer}, None, True)
            self.keep(q)

        def keep(self, q):
            j, cut = self.at(q)
            self.first[q, 1].wait_recv()
            self.total[j, :, cut] = wide(self.part[j, mid, core, :, cut]) + wide(self.near[j, 1, :, cut])

        def crossed(self, q):
            j, cut = self.at(q)
            self.second[q].wait_recv()
            self.total[j, :, cut] = self.total[j, :, cut] + wide(self.in_x[j, :, cut])

    class ReduceVir(Reduce):
        def at(self, q):
            return part_of(q, self.part.shape[-1])

        def to_far(self, q):
            j, cut = self.at(q)
            self.crossed(q)
            if q == n_far - 1:
                pl.when(inner)(functools.partial(self.arrive, planes[2]))
            if j == n_far - 1:
                pl.when(inner)(functools.partial(self.add, planes[2], j, cut))
            if j > 0:
                out_far_vir[j - 1, :, cut] = self.total[j, :, cut].astype(kind)
                target, slot = planes[j], far
                if j == n_far - 1:
                    col = index(target, mid, core)
                    h = q - j
                    for where, device in ((mine, {"col": col}), (theirs, {"col": col, "orb": other})):
                        push(out_far_vir.at[j - 1, where, cut], in_last_vir.at[part, :, cut],
                             last_send, last_recv.at[h, part], device, None, True)
                    return
                if j == 2:
                    target = lax.select(inner, planes[2], planes[1])
                    slot = lax.select(inner, far, planes[3])
                push(out_far_vir.at[j - 1], in_far_vir.at[slot], far_send.at[j - 1],
                     far_recv.at[slot], {"col": index(target, mid, core)})

        def arrive(self, source):
            landed(in_far_vir.at[source], swap_send.at[0], far_recv.at[source], {"orb": other})

        def add(self, source, j, cut):
            self.total[j, :, cut] = self.total[j, :, cut] + wide(in_far_vir[source, :, cut])

        def take(self, source):
            self.arrive(source)
            self.add(source, 0, pl.ds(0, self.part.shape[-1]))

        def gather(self):
            self.take(planes[1])
            pl.when(outer)(functools.partial(self.take, planes[2]))
            half_vir[...] = self.total[0, theirs].astype(kind)
            self.last = push(half_vir, in_half_vir, half_send.at[0], half_recv.at[0], {"orb": other})

        def end(self):
            self.last.wait_recv()
            for h in range(2):
                cut = self.at(n_far - 1 + h)[1]
                for k in range(2):
                    landed(in_last_vir.at[k, :, cut], swap_send.at[0], last_recv.at[h, k], {"orb": other})
            own = self.total[0, mine] + wide(in_last_vir[part])
            return own, wide(in_half_vir[...]) + wide(in_last_vir[other])

    class ReduceOcc(Reduce):
        def to_far(self, j):
            self.crossed(j)
            if j == n_far - 1:
                pl.when(inner)(self.join)
            out_far_occ[j - 1] = self.total[j].astype(kind)
            col = index(planes[j], mid, core)
            if j == 2:
                self.joined = push(out_far_occ.at[1], joint_occ, joint_send, joint_recv,
                                   {"col": index(planes[1], mid, core)}, outer)
            for n, (where, device) in enumerate(
                ((mine, {"col": col}), (theirs, {"col": col, "orb": other}))
            ):
                push(out_far_occ.at[j - 1, where], in_far_occ.at[far, part], far_send.at[n_far - 1 + 2 * (j - 1) + n],
                     occ_recv.at[far, part], device, inner if j == 2 else None)

        def join(self):
            self.joined.wait_recv()
            self.total[n_far - 1] = self.total[n_far - 1] + wide(joint_occ[...])

        def own_half(self):
            self.keep(0)
            half_occ[...] = self.total[0, theirs].astype(kind)
            self.last = push(half_occ, in_half_occ, half_send.at[1], half_recv.at[1], {"orb": other})

        def direct(self):
            for c, col in ((core, x_peer), (1 - core, diagonal)):
                for where, device in ((mine, {"col": col}), (theirs, {"col": col, "orb": other})):
                    push(part_occ.at[0, other_mid, c, where], in_own_occ.at[core, part],
                         own_send, own_recv.at[core, part], device, None, True)

        def take(self, ref, recv):
            landed(ref, swap_send.at[0], recv, {"orb": other})
            value_occ[...] = value_occ[...] + wide(ref[...])

        def take_far(self, source):
            for k in range(2):
                self.take(in_far_occ.at[source, k], occ_recv.at[source, k])

        def collect(self):
            self.last.wait_recv()
            value_occ[...] = self.total[0, mine] + wide(in_half_occ[...])

        def gather(self):
            self.take_far(planes[1])
            pl.when(outer)(functools.partial(self.take_far, planes[2]))
            self.take_far(planes[3])
            for c in range(2):
                for k in range(2):
                    self.take(in_own_occ.at[c, k], own_recv.at[c, k])

    of_vir = ReduceVir(0, part_vir, near_vir, out_x_vir, in_x_vir, sum_vir, out_far_vir)
    of_occ = ReduceOcc(1, part_occ, near_occ, out_x_occ, in_x_occ, sum_occ, out_far_occ)

    def project_vir(q):
        j, _ = of_vir.at(q)
        swap = swaps["side", j]
        if q <= n_far - 1:
            swap.wait_recv()
        width = part_vir.shape[-1] // (1 if q < n_far - 1 else 2)
        first = (q - j) * width
        for start in range(first, first + width, 256):
            cut = slice(start, min(start + 256, first + width))
            term = dot_t(side[j, 0], ov[0, cut]) + dot_t(side[j, 1], ov[1, cut])
            part_vir[j, :, :, :, cut] = term.astype(kind).reshape((2, 2, block, -1))
        of_vir.to_core(q)

    def project_occ(j, m=None):
        slot = j if m is not other_mid else n_far
        swaps["green", slot].wait_recv()
        owners, lines = (plane(j), pl.ds(0, rows)) if m is None else chip(m)
        shades = wide(screens[owners].reshape((-1, half)))
        value = (green[j, lines] + wide(green_in[j, lines])) * shades
        value = value.astype(kind)
        wide_occ = od.shape[1]
        for k in range(2):
            term = dot_t(value, od[k]).astype(kind).reshape((-1, 2, block, wide_occ))
            cut = slice(k * wide_occ, (k + 1) * wide_occ)
            if m is None:
                part_occ[j, :, :, :, cut] = term
            else:
                part_occ[j, m, :, :, cut] = term[0]
        if m is other_mid:
            of_occ.direct()
        else:
            of_occ.to_core(j, (0, 1) if m is None else (1,))

    push(so.at[me, part], so.at[me, part], swap_send.at[0], swap_recv.at[0], {"orb": other})
    swap = push(columns_of(occ, other), od.at[part, pl.ds(0, n_occ)], swap_send.at[1],
                swap_recv.at[1], {"orb": other})
    give_own(0)
    for load in loads[4:7]:
        load.wait()
    arrived(0, core_peer)
    make_green(0, mid)
    landed(so.at[me, other], swap_send.at[0], swap_recv.at[0], {"orb": other})
    give_own(1)
    give_near()
    give_screens(1)
    cross(1, 0)
    relay(1, 1)
    relay(1, 3, inner)
    relay(0, 1)
    give_screens(2)
    settle(1, 0)
    screened(0)
    swap.wait_recv()
    make_side(0)
    relay(1, 2, inner)
    cross(0, 0)
    give_screens(3)
    relay(0, 3, inner)
    cross(1, 1)
    settle(1, 1)
    screened(1)
    make_side(1)
    relay(1, 2, outer)
    cross(0, 1)
    settle(0, 1)
    make_green(1)
    give_middle()
    project_vir(0)
    relay(1, 3, outer)
    cross(1, 2)
    project_occ(0, mid)
    of_vir.to_mid(0)
    of_occ.own_half()
    settle(1, 2)
    screened(2)
    make_side(2)
    cross(1, 3)
    relay(0, 2, outer)
    relay(0, 2, inner)
    project_vir(1)
    settle(1, 3)
    screened(3)
    make_side(3)
    cross(0, 2)
    of_vir.to_mid(1)
    of_vir.to_far(0)
    settle(0, 2)
    make_green(2)
    relay(0, 3, outer)
    project_vir(2)
    project_occ(1)
    of_vir.to_mid(2)
    of_occ.to_mid(1)
    cross(0, 3)
    settle(0, 3)
    make_green(3)
    of_vir.to_far(1)
    project_vir(3)
    project_vir(4)
    of_vir.to_far(2)
    of_vir.to_mid(3)
    of_vir.to_mid(4)
    arrived(0, diagonal)
    make_green(0, other_mid)
    project_occ(2)
    of_occ.to_mid(2)
    of_vir.to_far(3)
    of_vir.to_far(4)
    project_occ(3)
    of_occ.to_mid(3)
    of_occ.to_far(1)
    of_occ.to_far(2)
    project_occ(0, other_mid)
    of_occ.collect()
    of_vir.gather()
    of_occ.to_far(3)
    low = part == 0
    own, peer = of_vir.end()
    own, peer = own[:, :n_vir], peer[:, :n_vir]
    out_vir[:, :n_vir] = jnp.where(low, own, peer).astype(kind)
    out_vir[:, n_vir:] = jnp.where(low, peer, own).astype(kind)
    of_occ.gather()
    value = value_occ[...]
    wide_occ = od.shape[1]
    out_occ[:, :n_occ] = value[:, :n_occ].astype(kind)
    out_occ[:, n_occ:] = value[:, wide_occ : wide_occ + n_occ].astype(kind)
    sent(screens, n_col - 1, screen_send)
    sent(green_out, None, green_send)
    sent(side, n_far // 2, side_send)
    sent(near_vir, None, near_send.at[0])
    sent(so, 2 * n_far - 1, near_send.at[1])
    sent(out_x_vir, None, x_send.at[0])
    sent(out_x_occ, n_far - 1, x_send.at[1])
    sent(in_last_vir, None, last_send)
    sent(in_own_occ, None, own_send)
    for k in range(2):
        sent(slabs[k], 3 + 2 * (n_far - 1) + n_far, slab_send.at[k, 0])
        pl.when(inner)(functools.partial(sent, slabs[k], n_far, slab_send.at[k, 1]))
    for only, copy in sends:
        if only is None:
            copy.wait_send()
        else:
            pl.when(only)(copy.wait_send)


def fused(n_col, slab_occ, slab_vir, occ, vir, occ_energy, vir_energy, screen):
    up = lambda n: -(-n // 128) * 128
    block = slab_occ.shape[0]
    n_occ, columns = occ.shape
    n_vir = vir.shape[0]
    kind, f32 = slab_occ.dtype, jnp.float32
    half = columns // 2
    wide_occ, wide_vir = up(n_occ), up(n_vir)
    n_far = n_col // 4
    rows = 4 * block
    both = 2 * wide_occ
    dma = pltpu.SemaphoreType.DMA

    def pair(lead, lines, dtype=kind):
        return [pltpu.VMEM(lead + (lines, w), dtype) for w in (wide_vir, both)]

    return pl.pallas_call(
        functools.partial(fused_kernel, n_col),
        out_shape=[pltpu.VMEM((block // 2, 2 * n), kind) for n in (n_occ, n_vir)],
        in_specs=[ANY] * 7,
        out_specs=[VMEM] * 2,
        scratch_shapes=[
            pltpu.VMEM(slab_occ.shape, kind),
            pltpu.VMEM(slab_vir.shape, kind),
            pltpu.VMEM(occ_energy.shape, f32),
            pltpu.VMEM(vir_energy.shape, f32),
            pltpu.VMEM((n_col, block, wide_vir), kind),
            pltpu.VMEM((n_col, 2, block, wide_occ), kind),
            pltpu.VMEM((2, wide_vir, half), kind),
            pltpu.VMEM((2, wide_occ, half), kind),
            pltpu.VMEM((n_col, block, half), kind),
            pltpu.VMEM((n_far, rows, half), f32),
            pltpu.VMEM((n_far, rows, half), kind),
            pltpu.VMEM((n_far, rows, half), kind),
            pltpu.VMEM((n_far, 2, rows, half), kind),
        ]
        + pair((n_far, 2, 2), block)
        + pair((n_far, 2), block)
        + pair((n_far,), block)
        + pair((n_far,), block)
        + pair((n_far,), block, f32)
        + pair((n_far - 1,), block)
        + [
            pltpu.VMEM((n_far, block, wide_vir), kind),
            pltpu.VMEM((block, both), kind),
            pltpu.VMEM((n_far, 2, block // 2, both), kind),
            pltpu.VMEM((2, 2, block // 2, both), kind),
        ]
        + pair((), block // 2)
        + pair((), block // 2)
        + [pltpu.VMEM((block // 2, both), f32), pltpu.VMEM((2, block // 2, wide_vir), kind)]
        + [
            dma((8,)), dma((2, 2)), dma((2, n_col)), dma((2,)), dma((2,)), dma, dma((n_far,)),
            dma, dma((n_far + 1,)), dma, dma((n_far,)),
            dma((2,)), dma((2, n_far + 1, 2)), dma((2,)), dma((2, n_far + 1)),
            dma((3 * (n_far - 1),)), dma((n_far,)), dma((2,)), dma((2,)), dma, dma,
            dma((1,)), dma((n_far, 2)), dma, dma((2, 2)), dma, dma((2, 2)),
        ],
        compiler_params=pltpu.CompilerParams(
            collective_id=2, has_side_effects=True, vmem_limit_bytes=60 * 2**20
        ),
    )(slab_occ, slab_vir, occ, vir, occ_energy, vir_energy, screen)


def write_kernel(occ, vir, out_occ, out_vir, sem):
    copies = [
        pltpu.make_async_copy(src, dst, sem.at[n])
        for n, (src, dst) in enumerate(((vir, out_vir), (occ, out_occ)))
    ]
    for copy in copies:
        copy.start()
    for copy in copies:
        copy.wait()


def settle_outputs(occ, vir):
    return pl.pallas_call(
        write_kernel,
        out_shape=[jax.ShapeDtypeStruct(x.shape, x.dtype) for x in (occ, vir)],
        in_specs=[VMEM] * 2,
        out_specs=[ANY] * 2,
        scratch_shapes=[pltpu.SemaphoreType.DMA((2,))],
    )(*(pltpu.with_memory_space_constraint(x, pltpu.VMEM) for x in (occ, vir)))


def local(slab_occ, slab_vir, orbitals_occ, orbitals_vir, occ_energy, vir_energy, screened):
    n_orb, n_col = lax.axis_size("orb"), lax.axis_size("col")
    part = lax.axis_index("orb")
    block = slab_occ.shape[0] // n_orb
    n_occ, columns = orbitals_occ.shape
    n_vir = orbitals_vir.shape[0]
    kind = slab_occ.dtype
    if n_col == 16 and n_orb == 2 and block % 16 == 0 and columns % 512 == 0:
        return tuple(
            settle_outputs(
                *fused(
                    n_col, slab_occ, slab_vir, orbitals_occ, orbitals_vir,
                    occ_energy, vir_energy, screened,
                )
            )
        )
    up = lambda n: -(-n // 128) * 128
    scaled_occ = (slab_occ.astype(jnp.float32) * jnp.exp(occ_energy)[None, :]).astype(kind)
    scaled_vir = (slab_vir.astype(jnp.float32) * jnp.exp(-vir_energy)[None, :]).astype(kind)
    start = up(n_vir)
    slab = jnp.concatenate(
        [
            jnp.pad(scaled_vir, ((0, 0), (0, start - n_vir))),
            jnp.pad(scaled_occ, ((0, 0), (0, up(n_occ) - n_occ))),
        ],
        axis=1,
    ).reshape((n_orb, block, start + up(n_occ)))
    mine = lax.dynamic_slice_in_dim(screened, part * block, block, 0)
    mine = mine.reshape((block, n_col, columns)).transpose((1, 0, 2))

    def order(own, peer, n):
        own, peer = own[:, :n], peer[:, :n]
        return jnp.where(
            part == 0, jnp.concatenate([own, peer], 1), jnp.concatenate([peer, own], 1)
        )

    slabs, peer_occ, peer_vir, screens = gather(n_col, slab, orbitals_occ, orbitals_vir, mine)
    slabs = slabs.reshape((2, n_col * block, slab.shape[2]))
    own_slab, peer_slab = slabs[0], slabs[1]

    def dot(a, b):
        return jnp.dot(a, b, preferred_element_type=jnp.float32)

    green_vir = dot(own_slab[:, :n_vir], orbitals_vir) + dot(peer_slab[:, :n_vir], peer_vir)
    green_occ = dot(own_slab[:, start : start + n_occ], orbitals_occ) + dot(
        peer_slab[:, start : start + n_occ], peer_occ
    )
    screen = screens.reshape((n_col * block, columns)).astype(jnp.float32)
    occ_side = (green_vir * screen).astype(kind)
    vir_side = (green_occ * screen).astype(kind)
    dims = (((1,), (1,)), ((), ()))

    def project(side, orbitals):
        term = lax.dot_general(side, orbitals, dims, preferred_element_type=jnp.float32)
        return term.astype(kind).reshape((n_col // 4, 2, 2, block, orbitals.shape[0]))

    vir_own, vir_peer, occ_own, occ_peer = scatter(
        n_col,
        [
            project(vir_side, orbitals_vir),
            project(vir_side, peer_vir),
            project(occ_side, orbitals_occ),
            project(occ_side, peer_occ),
        ],
    )

    return order(occ_own, occ_peer, n_occ), order(vir_own, vir_peer, n_vir)


def solution(mesh):
    return jax.shard_map(
        local,
        mesh=mesh,
        in_specs=(
            P("col", "orb"),
            P("col", "orb"),
            P("orb", "col"),
            P("orb", "col"),
            P("orb"),
            P("orb"),
            P("col", None),
        ),
        out_specs=(P(("col", "orb"), None), P(("col", "orb"), None)),
        check_vma=False,
    )
```

```python
import functools

import jax
import jax.numpy as jnp
from jax import lax
from jax.experimental import pallas as pl
from jax.experimental.pallas import tpu as pltpu
from jax.sharding import PartitionSpec as P

MESH = pl.DeviceIdType.MESH
LAGS = (1, 2)
ANY = pl.BlockSpec(memory_space=pl.ANY)
VMEM = pl.BlockSpec(memory_space=pltpu.VMEM)


def place(n_col):
    me = lax.axis_index("col")
    far, mid, core = me // 4, lax.rem(me // 2, 2), lax.rem(me, 2)
    return me, far, mid, core, lambda f, m, c: (f * 2 + m) * 2 + c


def greet(cols, orbs):
    barrier = pltpu.get_barrier_semaphore()
    for col in cols:
        pl.semaphore_signal(barrier, inc=1, device_id={"col": col}, device_id_type=MESH)
    for orb in orbs:
        pl.semaphore_signal(barrier, inc=1, device_id={"orb": orb}, device_id_type=MESH)
    pl.semaphore_wait(barrier, len(cols) + len(orbs))


def sender():
    sends = []

    def push(src, dst, send, recv, device):
        copy = pltpu.make_async_remote_copy(
            src_ref=src, dst_ref=dst, send_sem=send, recv_sem=recv,
            device_id=device, device_id_type=MESH,
        )
        copy.start()
        sends.append(copy)
        return copy

    return sends, push


def landed(ref, send, recv, device):
    pltpu.make_async_remote_copy(
        src_ref=ref, dst_ref=ref, send_sem=send, recv_sem=recv,
        device_id=device, device_id_type=MESH,
    ).wait_recv()


def spread(n_col, push, swap, slab, screen, slabs, screens, local_sem,
           orb_send, slab_send, slab_recv, screen_send, screen_recv):
    n_far = n_col // 4
    me, far, mid, core, index = place(n_col)
    part = lax.axis_index("orb")
    other = 1 - part
    others = [lax.rem(me + d, n_col) for d in range(1, n_col)]

    def arrived(k, col):
        landed(slabs.at[k, col], orb_send.at[swap], slab_recv.at[k, col], {"orb": other})

    counter = [0]

    def give(k, col, target, src=None):
        push(
            slabs.at[k, col] if src is None else src, slabs.at[k, col],
            slab_send.at[counter[0]], slab_recv.at[k, col], {"col": target},
        )
        counter[0] += 1

    x_peer, core_peer = index(far, 1 - mid, core), index(far, mid, 1 - core)
    fars = [lax.rem(far + d, n_far) for d in range(1, n_far)]
    own = slab.at[part]
    targets = [index(f, mid, core) for f in fars] + [x_peer, core_peer]
    for target in targets:
        give(0, me, target, own)
    arrived(1, me)
    for target in targets:
        give(1, me, target)
    for n, p in enumerate(others):
        push(screen.at[p], screens.at[me], screen_send.at[n], screen_recv.at[me], {"col": p})
    local = [
        pltpu.make_async_copy(own, slabs.at[0, me], local_sem.at[0]),
        pltpu.make_async_copy(screen.at[me], screens.at[me], local_sem.at[1]),
    ]
    for copy in local:
        copy.start()
    for f in fars:
        col = index(f, mid, core)
        for k in range(2):
            arrived(k, col)
            give(k, col, x_peer)
            give(k, col, core_peer)
    for f in [far] + fars:
        col = index(f, 1 - mid, core)
        for k in range(2):
            arrived(k, col)
            give(k, col, core_peer)
    for f in [far] + fars:
        for m in (mid, 1 - mid):
            for k in range(2):
                arrived(k, index(f, m, 1 - core))
    for p in others:
        landed(screens.at[p], orb_send.at[swap], screen_recv.at[p], {"orb": other})
    for copy in local:
        copy.wait()


def spread_semaphores(n_col):
    n_far = n_col // 4
    dma = pltpu.SemaphoreType.DMA
    n_give = 2 * ((n_far + 1) + 2 * (n_far - 1) + n_far)
    return [dma((n_give,)), dma((2, n_col)), dma((n_col,)), dma((n_col,))]


def gather_kernel(
    n_col, slab, occ, vir, screen, slabs, peer_occ, peer_vir, screens,
    local_sem, orb_send, orb_recv, slab_send, slab_recv, screen_send, screen_recv,
):
    me = lax.axis_index("col")
    other = 1 - lax.axis_index("orb")
    greet([lax.rem(me + d, n_col) for d in range(1, n_col)], [other])
    sends, push = sender()
    push(slab.at[other], slabs.at[1, me], orb_send.at[2], slab_recv.at[1, me], {"orb": other})
    push(vir, peer_vir, orb_send.at[0], orb_recv.at[0], {"orb": other})
    push(occ, peer_occ, orb_send.at[1], orb_recv.at[1], {"orb": other})
    spread(n_col, push, 2, slab, screen, slabs, screens, local_sem,
           orb_send, slab_send, slab_recv, screen_send, screen_recv)
    for n, ref in ((0, peer_vir), (1, peer_occ)):
        landed(ref, orb_send.at[n], orb_recv.at[n], {"orb": other})
    for copy in sends:
        copy.wait_send()


def gather(n_col, slab, occ, vir, screen):
    dma = pltpu.SemaphoreType.DMA
    return pl.pallas_call(
        functools.partial(gather_kernel, n_col),
        out_shape=(
            jax.ShapeDtypeStruct((2, n_col) + slab.shape[1:], slab.dtype),
            jax.ShapeDtypeStruct(occ.shape, occ.dtype),
            jax.ShapeDtypeStruct(vir.shape, vir.dtype),
            jax.ShapeDtypeStruct(screen.shape, screen.dtype),
        ),
        in_specs=[ANY] * 4,
        out_specs=(ANY,) * 4,
        scratch_shapes=[dma((2,)), dma((3,)), dma((2,))] + spread_semaphores(n_col),
        compiler_params=pltpu.CompilerParams(collective_id=0, has_side_effects=True),
    )(slab, occ, vir, screen)


def reduce_rows(n_col, pieces, ins, refs, ready, finish, flush=()):
    n_far = n_col // 4
    near, out_x, in_x, total, out_far, in_far = [
        refs[i * pieces : (i + 1) * pieces] for i in range(6)
    ]
    near_send, near_recv, x_send, x_recv, far_send, far_recv = refs[6 * pieces :]
    me, far, mid, core, index = place(n_col)
    x_peer, core_peer = index(far, 1 - mid, core), index(far, mid, 1 - core)
    fars = [lax.rem(far + d, n_far) for d in range(1, n_far)]
    sends, push = sender()
    wide = lambda value: value.astype(jnp.float32)
    first, second, third = [], [], []

    def to_core(t):
        ready(t)
        first.append(
            [
                push(
                    ins[t].at[:, m, 1 - core], near[t].at[slot],
                    near_send.at[t, slot], near_recv.at[t, slot], {"col": core_peer},
                )
                for slot, m in ((0, 1 - mid), (1, mid))
            ]
        )

    def to_mid(t):
        first[t][0].wait_recv()
        for f in range(n_far):
            out_x[t][f] = (wide(ins[t][f, 1 - mid, core]) + wide(near[t][0, f])).astype(
                out_x[t].dtype
            )
        second.append(push(out_x[t], in_x[t], x_send.at[t], x_recv.at[t], {"col": x_peer}))
        first[t][1].wait_recv()
        for f in range(n_far):
            total[t][f] = wide(ins[t][f, mid, core]) + wide(near[t][1, f])

    def to_far(t):
        second[t].wait_recv()
        for f in range(n_far):
            total[t][f] = total[t][f] + wide(in_x[t][f])
            out_far[t][f] = total[t][f].astype(out_far[t].dtype)
        for d, f in enumerate(fars):
            third.append(
                push(
                    out_far[t].at[f], in_far[t].at[d],
                    far_send.at[t, d], far_recv.at[t, d], {"col": index(f, mid, core)},
                )
            )

    acts, count = (to_core, to_mid, to_far), [0, 0, 0]

    def advance(stage, end):
        while count[stage] < end:
            acts[stage](count[stage])
            count[stage] += 1

    for t in range(pieces):
        if t in flush:
            advance(1, t)
            advance(2, t)
        advance(0, t + 1)
        advance(1, t + 1 - LAGS[0])
        advance(2, t + 1 - sum(LAGS))
    advance(1, pieces)
    advance(2, pieces)
    for t in range(pieces):
        value = total[t][far]
        for d in range(n_far - 1):
            third[t * (n_far - 1) + d].wait_recv()
            value = value + wide(in_far[t][d])
        finish(t, value)
    for made in sends:
        made.wait_send()


def reduce_scratch(n_col, block, kind):
    n_far = n_col // 4
    dma = pltpu.SemaphoreType.DMA
    pieces = len(block)

    def buffers(lead, dtype=kind):
        return [pltpu.VMEM(lead + tuple(b), dtype) for b in block]

    return (
        buffers((2, n_far))
        + buffers((n_far,))
        + buffers((n_far,))
        + buffers((n_far,), jnp.float32)
        + buffers((n_far,))
        + buffers((n_far - 1,))
        + [
            dma((pieces, 2)), dma((pieces, 2)), dma((pieces,)), dma((pieces,)),
            dma((pieces, n_far - 1)), dma((pieces, n_far - 1)),
        ]
    )


def scatter_kernel(n_col, pieces, *refs):
    me, far, mid, core, index = place(n_col)
    n_far = n_col // 4
    fars = [lax.rem(far + d, n_far) for d in range(1, n_far)]
    greet(
        [index(far, mid, 1 - core), index(far, 1 - mid, core)]
        + [index(f, mid, core) for f in fars],
        [],
    )
    outs = refs[pieces : 2 * pieces]

    def finish(t, value):
        outs[t][...] = value.astype(outs[t].dtype)

    reduce_rows(n_col, pieces, refs[:pieces], refs[2 * pieces :], lambda t: None, finish)


def scatter(n_col, terms):
    pieces = len(terms)
    block, kind = [t.shape[-2:] for t in terms], terms[0].dtype
    return pl.pallas_call(
        functools.partial(scatter_kernel, n_col, pieces),
        out_shape=[jax.ShapeDtypeStruct(b, kind) for b in block],
        in_specs=[VMEM] * pieces,
        out_specs=[VMEM] * pieces,
        scratch_shapes=reduce_scratch(n_col, block, kind),
        compiler_params=pltpu.CompilerParams(collective_id=1, has_side_effects=True),
    )(*terms)


def order(far, j):
    if j == 0:
        return far
    if j == 1:
        return far + 1 - 2 * lax.rem(far, 2)
    return lax.rem(far + 2, 4) if j == 2 else 3 - far


def fused_kernel(n_col, slab_occ, slab_vir, occ, vir, occ_energy, vir_energy, screen, *refs):
    out_occ, out_vir = refs[:2]
    (raw_occ, raw_vir, e_occ, e_vir, sv, so, ov, od, screens, green, green_out, green_in, side,
     part_vir, part_occ, near_vir, near_occ, out_x_vir, out_x_occ, in_x_vir, in_x_occ,
     sum_vir, sum_occ, out_far_vir, out_far_occ, in_far_vir, joint_occ, in_far_occ, in_own_occ,
     half_vir, half_occ, in_half_vir, in_half_occ, value_occ, in_last_vir) = refs[2:37]
    (load_sem, slab_send, slab_recv, swap_send, swap_recv, screen_send, screen_recv,
     green_send, green_recv, side_send, side_recv, near_send, near_recv, x_send, x_recv,
     far_send, far_recv, half_send, half_recv, joint_send, joint_recv, occ_send, occ_recv,
     own_send, own_recv, last_send, last_recv) = refs[37:]
    n_far = n_col // 4
    me, far, mid, core, index = place(n_col)
    part = lax.axis_index("orb")
    other = 1 - part
    x_peer, core_peer = index(far, 1 - mid, core), index(far, mid, 1 - core)
    other_mid = 1 - mid
    diagonal = index(far, other_mid, 1 - core)
    inner = lax.rem(far, 3) > 0
    outer = lax.rem(far, 3) == 0
    planes = [order(far, j) for j in range(n_far)]
    n_occ = occ.shape[0]
    n_vir = vir.shape[0]
    half = ov.shape[2]
    block = sv.shape[1]
    rows = 4 * block
    kind = sv.dtype
    wide = lambda value: value.astype(jnp.float32)

    def dot(a, b):
        return jnp.dot(a, b, preferred_element_type=jnp.float32)

    def dot_t(a, b):
        return lax.dot_general(a, b, (((1,), (1,)), ((), ())), preferred_element_type=jnp.float32)

    barrier = pltpu.get_barrier_semaphore()
    for d in range(1, n_col):
        pl.semaphore_signal(
            barrier, inc=1, device_id={"col": lax.rem(me + d, n_col)}, device_id_type=MESH
        )
    across = [me, x_peer] + [index(f, mid, core) for f in planes[1:]]
    for col in across:
        pl.semaphore_signal(
            barrier, inc=1, device_id={"col": col, "orb": other}, device_id_type=MESH
        )

    def piece(p, k):
        start = p * (2 * half) + k * half
        return screen.at[:, pl.ds(pl.multiple_of(start, half), half)]

    def columns_of(ref, k):
        return ref.at[:, pl.ds(pl.multiple_of(k * half, half), half)]

    loads = [
        pltpu.make_async_copy(src, dst, load_sem.at[n])
        for n, (src, dst) in enumerate(
            (
                (vir_energy, e_vir), (slab_vir, raw_vir), (occ_energy, e_occ), (slab_occ, raw_occ),
                (columns_of(vir, other), ov.at[other, pl.ds(0, n_vir)]),
                (columns_of(vir, part), ov.at[part, pl.ds(0, n_vir)]),
                (columns_of(occ, part), od.at[part, pl.ds(0, n_occ)]),
                (piece(me, part), screens.at[me]),
            )
        )
    ]
    for load in loads:
        load.start()
    for ref, n in ((ov, n_vir), (od, n_occ)):
        short = ref.shape[1] - n
        if short:
            for k in range(2):
                ref[k, pl.ds(n, short)] = jnp.zeros((short, half), kind)
    for load in loads[:4]:
        load.wait()
    sv[me, :, :n_vir] = (wide(raw_vir[...]) * jnp.exp(-e_vir[...])[None, :]).astype(kind)
    if sv.shape[2] > n_vir:
        sv[me, :, n_vir:] = jnp.zeros((block, sv.shape[2] - n_vir), kind)
    so[me, part, :, :n_occ] = (wide(raw_occ[...]) * jnp.exp(e_occ[...])[None, :]).astype(kind)
    if so.shape[3] > n_occ:
        so[me, part, :, n_occ:] = jnp.zeros((block, so.shape[3] - n_occ), kind)
    pl.semaphore_wait(barrier, n_col - 1 + len(across))

    sends = []

    def push(src, dst, send, recv, device, only=None, shared=False):
        copy = pltpu.make_async_remote_copy(
            src_ref=src, dst_ref=dst, send_sem=send, recv_sem=recv,
            device_id=device, device_id_type=MESH,
        )
        if only is None:
            copy.start()
        else:
            pl.when(only)(copy.start)
        if not shared:
            sends.append((only, copy))
        return copy

    slabs = (sv, so)

    def give(k, col, target, only=None, chain=False):
        push(slabs[k].at[col], slabs[k].at[col], slab_send.at[k, int(chain)], slab_recv.at[k, col],
             {"col": target}, only, True)

    def sent(ref, n, send):
        ref = ref if n is None else ref.at[pl.ds(0, n)]
        pltpu.make_async_remote_copy(
            src_ref=ref, dst_ref=ref, send_sem=send, recv_sem=swap_recv.at[0],
            device_id={"orb": other}, device_id_type=MESH,
        ).wait_send()

    def arrived(k, col, only=None):
        def act():
            landed(slabs[k].at[col], swap_send.at[0], slab_recv.at[k, col], {"orb": other})

        act() if only is None else pl.when(only)(act)

    def give_own(k):
        give(k, me, x_peer)
        give(k, me, index(planes[1], mid, core))
        give(k, me, index(planes[3], mid, core), inner, True)
        give(k, me, core_peer)

    def relay(k, j, only=None):
        col = index(planes[j], mid, core)
        arrived(k, col, only)
        step = planes[3 if j == 1 else 1]
        if only is not outer and (k, j) != (0, 1):
            give(k, col, index(step, mid, core), inner, True)
        give(k, col, x_peer, only)
        give(k, col, core_peer, only)

    def give_middle():
        give(0, index(planes[1], mid, core), index(planes[3], mid, core), inner, True)

    def cross(k, j, only=None):
        col = index(planes[j], 1 - mid, core)
        arrived(k, col, only)
        give(k, col, core_peer, only)

    def settle(k, j, only=None):
        arrived(k, index(planes[j], mid, 1 - core), only)
        arrived(k, index(planes[j], 1 - mid, 1 - core), only)

    def give_screen(target):
        push(piece(target, part), screens.at[me], screen_send, screen_recv.at[far],
             {"col": target}, None, True)

    def give_near():
        for target in (x_peer, core_peer, diagonal):
            give_screen(target)

    def give_screens(j):
        for m, c in ((mid, core), (1 - mid, core), (mid, 1 - core), (1 - mid, 1 - core)):
            give_screen(index(planes[j], m, c))

    def screened(j):
        if j == 0:
            loads[7].wait()
        ref = screens.at[pl.ds(planes[j] * 4, 4) if j else pl.ds(0, 3)]
        landed(ref, swap_send.at[0], screen_recv.at[planes[j]], {"orb": other})

    def plane(j):
        return pl.ds(planes[j] * 4, 4)

    def shade(j, cut):
        return wide(screens[plane(j), :, cut].reshape((rows, -1)))

    cuts = [slice(start, start + 256) for start in range(0, half, 256)]
    swaps = {}

    def chip(m):
        return pl.ds(planes[0] * 4 + 2 * m, 2), pl.ds(pl.multiple_of(m * (2 * block), 2 * block), 2 * block)

    def when(only, act):
        act() if only is None else pl.when(only)(act)

    def make_green(j, m=None, only=None):
        owners, lines = (plane(j), pl.ds(0, rows)) if m is None else chip(m)
        slot = j if m is not other_mid else n_far

        def fill(target, k, dtype):
            slab = sv[owners].reshape((-1, sv.shape[2]))
            for cut in cuts:
                target[j, lines, cut] = dot(slab, ov[k, :, cut]).astype(dtype)

        when(only, functools.partial(fill, green_out, other, kind))
        swaps["green", slot] = push(green_out.at[j, lines], green_in.at[j, lines], green_send,
                                    green_recv.at[slot], {"orb": other}, only, True)
        when(only, functools.partial(fill, green, part, jnp.float32))

    def make_side(j):
        for cut in cuts:
            value = dot(so[plane(j), 0].reshape((rows, -1)), od[0, :, cut])
            value = value + dot(so[plane(j), 1].reshape((rows, -1)), od[1, :, cut])
            side[j, part, :, cut] = (value * shade(j, cut)).astype(kind)
        swaps["side", j] = push(side.at[j, part], side.at[j, part], side_send,
                                side_recv.at[j], {"orb": other}, None, True)

    lines = block // 2
    mine = pl.ds(pl.multiple_of(part * lines, lines), lines)
    theirs = pl.ds(pl.multiple_of(other * lines, lines), lines)

    def part_of(q, width):
        if q < n_far - 1:
            return q, pl.ds(0, width)
        return n_far - 1, pl.ds((q - n_far + 1) * (width // 2), width // 2)

    class Reduce:
        def __init__(self, n, part, near, out_x, in_x, total, out_far):
            self.n, self.part, self.near, self.out_x, self.in_x = n, part, near, out_x, in_x
            self.total, self.out_far = total, out_far
            self.first, self.second = {}, {}

        def at(self, q):
            return q, pl.ds(0, self.part.shape[-1])

        def to_core(self, q, slots=(0, 1)):
            n = self.n
            j, cut = self.at(q)
            for slot in slots:
                m = (other_mid, mid)[slot]
                self.first[q, slot] = push(
                    self.part.at[j, m, 1 - core, :, cut], self.near.at[j, slot, :, cut],
                    near_send.at[n], near_recv.at[n, q, slot], {"col": core_peer}, None, True,
                )

        def to_mid(self, q):
            n = self.n
            j, cut = self.at(q)
            self.first[q, 0].wait_recv()
            self.out_x[j, :, cut] = (
                wide(self.part[j, 1 - mid, core, :, cut]) + wide(self.near[j, 0, :, cut])
            ).astype(kind)
            self.second[q] = push(self.out_x.at[j, :, cut], self.in_x.at[j, :, cut], x_send.at[n],
                                  x_recv.at[n, q], {"col": x_peer}, None, True)
            self.keep(q)

        def keep(self, q):
            j, cut = self.at(q)
            self.first[q, 1].wait_recv()
            self.total[j, :, cut] = wide(self.part[j, mid, core, :, cut]) + wide(self.near[j, 1, :, cut])

        def crossed(self, q):
            j, cut = self.at(q)
            self.second[q].wait_recv()
            self.total[j, :, cut] = self.total[j, :, cut] + wide(self.in_x[j, :, cut])

    class ReduceVir(Reduce):
        def at(self, q):
            return part_of(q, self.part.shape[-1])

        def to_far(self, q):
            j, cut = self.at(q)
            self.crossed(q)
            if q == n_far - 1:
                pl.when(inner)(functools.partial(self.arrive, planes[2]))
            if j == n_far - 1:
                pl.when(inner)(functools.partial(self.add, planes[2], j, cut))
            if j > 0:
                out_far_vir[j - 1, :, cut] = self.total[j, :, cut].astype(kind)
                target, slot = planes[j], far
                if j == n_far - 1:
                    col = index(target, mid, core)
                    h = q - j
                    for where, device in ((mine, {"col": col}), (theirs, {"col": col, "orb": other})):
                        push(out_far_vir.at[j - 1, where, cut], in_last_vir.at[part, :, cut],
                             last_send, last_recv.at[h, part], device, None, True)
                    return
                if j == 2:
                    target = lax.select(inner, planes[2], planes[1])
                    slot = lax.select(inner, far, planes[3])
                push(out_far_vir.at[j - 1], in_far_vir.at[slot], far_send.at[j - 1],
                     far_recv.at[slot], {"col": index(target, mid, core)})

        def arrive(self, source):
            landed(in_far_vir.at[source], swap_send.at[0], far_recv.at[source], {"orb": other})

        def add(self, source, j, cut):
            self.total[j, :, cut] = self.total[j, :, cut] + wide(in_far_vir[source, :, cut])

        def take(self, source):
            self.arrive(source)
            self.add(source, 0, pl.ds(0, self.part.shape[-1]))

        def gather(self):
            self.take(planes[1])
            pl.when(outer)(functools.partial(self.take, planes[2]))
            half_vir[...] = self.total[0, theirs].astype(kind)
            self.last = push(half_vir, in_half_vir, half_send.at[0], half_recv.at[0], {"orb": other})

        def end(self):
            self.last.wait_recv()
            for h in range(2):
                cut = self.at(n_far - 1 + h)[1]
                for k in range(2):
                    landed(in_last_vir.at[k, :, cut], swap_send.at[0], last_recv.at[h, k], {"orb": other})
            own = self.total[0, mine] + wide(in_last_vir[part])
            return own, wide(in_half_vir[...]) + wide(in_last_vir[other])

    class ReduceOcc(Reduce):
        def to_far(self, j):
            self.crossed(j)
            if j == n_far - 1:
                pl.when(inner)(self.join)
            out_far_occ[j - 1] = self.total[j].astype(kind)
            col = index(planes[j], mid, core)
            if j == 2:
                self.joined = push(out_far_occ.at[1], joint_occ, joint_send, joint_recv,
                                   {"col": index(planes[1], mid, core)}, outer)
            for n, (where, device) in enumerate(
                ((mine, {"col": col}), (theirs, {"col": col, "orb": other}))
            ):
                push(out_far_occ.at[j - 1, where], in_far_occ.at[far, part], far_send.at[n_far - 1 + 2 * (j - 1) + n],
                     occ_recv.at[far, part], device, inner if j == 2 else None)

        def join(self):
            self.joined.wait_recv()
            self.total[n_far - 1] = self.total[n_far - 1] + wide(joint_occ[...])

        def own_half(self):
            self.keep(0)
            half_occ[...] = self.total[0, theirs].astype(kind)
            self.last = push(half_occ, in_half_occ, half_send.at[1], half_recv.at[1], {"orb": other})

        def cross_own(self):
            self.first[0, 0].wait_recv()
            self.out_x[0] = (wide(self.part[0, other_mid, core]) + wide(self.near[0, 0])).astype(kind)
            for where, device in (
                (mine, {"col": x_peer}), (theirs, {"col": x_peer, "orb": other})
            ):
                push(self.out_x.at[0, where], in_own_occ.at[part], own_send, own_recv.at[part],
                     device, None, True)

        def take(self, ref, recv):
            landed(ref, swap_send.at[0], recv, {"orb": other})
            value_occ[...] = value_occ[...] + wide(ref[...])

        def take_far(self, source):
            for k in range(2):
                self.take(in_far_occ.at[source, k], occ_recv.at[source, k])

        def collect(self):
            self.last.wait_recv()
            value_occ[...] = self.total[0, mine] + wide(in_half_occ[...])

        def gather(self):
            self.take_far(planes[1])
            pl.when(outer)(functools.partial(self.take_far, planes[2]))
            self.take_far(planes[3])
            for k in range(2):
                self.take(in_own_occ.at[k], own_recv.at[k])

    of_vir = ReduceVir(0, part_vir, near_vir, out_x_vir, in_x_vir, sum_vir, out_far_vir)
    of_occ = ReduceOcc(1, part_occ, near_occ, out_x_occ, in_x_occ, sum_occ, out_far_occ)

    def project_vir(q):
        j, _ = of_vir.at(q)
        swap = swaps["side", j]
        if q <= n_far - 1:
            swap.wait_recv()
        width = part_vir.shape[-1] // (1 if q < n_far - 1 else 2)
        first = (q - j) * width
        for start in range(first, first + width, 256):
            cut = slice(start, min(start + 256, first + width))
            term = dot_t(side[j, 0], ov[0, cut]) + dot_t(side[j, 1], ov[1, cut])
            part_vir[j, :, :, :, cut] = term.astype(kind).reshape((2, 2, block, -1))
        of_vir.to_core(q)

    def project_occ(j, m=None):
        slot = j if m is not other_mid else n_far
        swaps["green", slot].wait_recv()
        owners, lines = (plane(j), pl.ds(0, rows)) if m is None else chip(m)
        shades = wide(screens[owners].reshape((-1, half)))
        value = (green[j, lines] + wide(green_in[j, lines])) * shades
        value = value.astype(kind)
        wide_occ = od.shape[1]
        for k in range(2):
            term = dot_t(value, od[k]).astype(kind).reshape((-1, 2, block, wide_occ))
            cut = slice(k * wide_occ, (k + 1) * wide_occ)
            if m is None:
                part_occ[j, :, :, :, cut] = term
            else:
                part_occ[j, m, :, :, cut] = term[0]
        of_occ.to_core(j, (0, 1) if m is None else (0,) if m is other_mid else (1,))

    push(so.at[me, part], so.at[me, part], swap_send.at[0], swap_recv.at[0], {"orb": other})
    swap = push(columns_of(occ, other), od.at[part, pl.ds(0, n_occ)], swap_send.at[1],
                swap_recv.at[1], {"orb": other})
    give_own(0)
    for load in loads[4:7]:
        load.wait()
    arrived(0, core_peer)
    make_green(0, mid)
    landed(so.at[me, other], swap_send.at[0], swap_recv.at[0], {"orb": other})
    give_own(1)
    give_near()
    give_screens(1)
    cross(1, 0)
    relay(1, 1)
    relay(1, 3, inner)
    relay(0, 1)
    give_screens(2)
    settle(1, 0)
    screened(0)
    swap.wait_recv()
    make_side(0)
    relay(1, 2, inner)
    cross(0, 0)
    give_screens(3)
    relay(0, 3, inner)
    cross(1, 1)
    settle(1, 1)
    screened(1)
    make_side(1)
    relay(1, 2, outer)
    cross(0, 1)
    settle(0, 1)
    make_green(1)
    give_middle()
    project_vir(0)
    relay(1, 3, outer)
    cross(1, 2)
    project_occ(0, mid)
    of_vir.to_mid(0)
    of_occ.own_half()
    settle(1, 2)
    screened(2)
    make_side(2)
    cross(1, 3)
    relay(0, 2, outer)
    relay(0, 2, inner)
    project_vir(1)
    settle(1, 3)
    screened(3)
    make_side(3)
    cross(0, 2)
    of_vir.to_mid(1)
    of_vir.to_far(0)
    settle(0, 2)
    make_green(2)
    relay(0, 3, outer)
    project_vir(2)
    project_occ(1)
    of_vir.to_mid(2)
    of_occ.to_mid(1)
    cross(0, 3)
    settle(0, 3)
    make_green(3)
    of_vir.to_far(1)
    project_vir(3)
    project_vir(4)
    of_vir.to_far(2)
    of_vir.to_mid(3)
    of_vir.to_mid(4)
    arrived(0, diagonal)
    make_green(0, other_mid)
    project_occ(2)
    of_occ.to_mid(2)
    of_vir.to_far(3)
    of_vir.to_far(4)
    project_occ(3)
    of_occ.to_mid(3)
    of_occ.to_far(1)
    of_occ.to_far(2)
    project_occ(0, other_mid)
    of_occ.collect()
    of_vir.gather()
    of_occ.cross_own()
    of_occ.to_far(3)
    low = part == 0
    own, peer = of_vir.end()
    own, peer = own[:, :n_vir], peer[:, :n_vir]
    out_vir[:, :n_vir] = jnp.where(low, own, peer).astype(kind)
    out_vir[:, n_vir:] = jnp.where(low, peer, own).astype(kind)
    of_occ.gather()
    value = value_occ[...]
    wide_occ = od.shape[1]
    out_occ[:, :n_occ] = value[:, :n_occ].astype(kind)
    out_occ[:, n_occ:] = value[:, wide_occ : wide_occ + n_occ].astype(kind)
    sent(screens, n_col - 1, screen_send)
    sent(green_out, None, green_send)
    sent(side, n_far // 2, side_send)
    sent(near_vir, None, near_send.at[0])
    sent(near_occ, None, near_send.at[1])
    sent(out_x_vir, None, x_send.at[0])
    sent(out_x_occ, n_far - 1, x_send.at[1])
    sent(in_last_vir, None, last_send)
    sent(in_own_occ, None, own_send)
    for k in range(2):
        sent(slabs[k], 3 + 2 * (n_far - 1) + n_far, slab_send.at[k, 0])
        pl.when(inner)(functools.partial(sent, slabs[k], n_far, slab_send.at[k, 1]))
    for only, copy in sends:
        if only is None:
            copy.wait_send()
        else:
            pl.when(only)(copy.wait_send)


def fused(n_col, slab_occ, slab_vir, occ, vir, occ_energy, vir_energy, screen):
    up = lambda n: -(-n // 128) * 128
    block = slab_occ.shape[0]
    n_occ, columns = occ.shape
    n_vir = vir.shape[0]
    kind, f32 = slab_occ.dtype, jnp.float32
    half = columns // 2
    wide_occ, wide_vir = up(n_occ), up(n_vir)
    n_far = n_col // 4
    rows = 4 * block
    both = 2 * wide_occ
    dma = pltpu.SemaphoreType.DMA

    def pair(lead, lines, dtype=kind):
        return [pltpu.VMEM(lead + (lines, w), dtype) for w in (wide_vir, both)]

    return pl.pallas_call(
        functools.partial(fused_kernel, n_col),
        out_shape=[pltpu.VMEM((block // 2, 2 * n), kind) for n in (n_occ, n_vir)],
        in_specs=[ANY] * 7,
        out_specs=[VMEM] * 2,
        scratch_shapes=[
            pltpu.VMEM(slab_occ.shape, kind),
            pltpu.VMEM(slab_vir.shape, kind),
            pltpu.VMEM(occ_energy.shape, f32),
            pltpu.VMEM(vir_energy.shape, f32),
            pltpu.VMEM((n_col, block, wide_vir), kind),
            pltpu.VMEM((n_col, 2, block, wide_occ), kind),
            pltpu.VMEM((2, wide_vir, half), kind),
            pltpu.VMEM((2, wide_occ, half), kind),
            pltpu.VMEM((n_col, block, half), kind),
            pltpu.VMEM((n_far, rows, half), f32),
            pltpu.VMEM((n_far, rows, half), kind),
            pltpu.VMEM((n_far, rows, half), kind),
            pltpu.VMEM((n_far, 2, rows, half), kind),
        ]
        + pair((n_far, 2, 2), block)
        + pair((n_far, 2), block)
        + pair((n_far,), block)
        + pair((n_far,), block)
        + pair((n_far,), block, f32)
        + pair((n_far - 1,), block)
        + [
            pltpu.VMEM((n_far, block, wide_vir), kind),
            pltpu.VMEM((block, both), kind),
            pltpu.VMEM((n_far, 2, block // 2, both), kind),
            pltpu.VMEM((2, block // 2, both), kind),
        ]
        + pair((), block // 2)
        + pair((), block // 2)
        + [pltpu.VMEM((block // 2, both), f32), pltpu.VMEM((2, block // 2, wide_vir), kind)]
        + [
            dma((8,)), dma((2, 2)), dma((2, n_col)), dma((2,)), dma((2,)), dma, dma((n_far,)),
            dma, dma((n_far + 1,)), dma, dma((n_far,)),
            dma((2,)), dma((2, n_far + 1, 2)), dma((2,)), dma((2, n_far + 1)),
            dma((3 * (n_far - 1),)), dma((n_far,)), dma((2,)), dma((2,)), dma, dma,
            dma((1,)), dma((n_far, 2)), dma, dma((2,)), dma, dma((2, 2)),
        ],
        compiler_params=pltpu.CompilerParams(
            collective_id=2, has_side_effects=True, vmem_limit_bytes=60 * 2**20
        ),
    )(slab_occ, slab_vir, occ, vir, occ_energy, vir_energy, screen)


def write_kernel(occ, vir, out_occ, out_vir, sem):
    copies = [
        pltpu.make_async_copy(src, dst, sem.at[n])
        for n, (src, dst) in enumerate(((vir, out_vir), (occ, out_occ)))
    ]
    for copy in copies:
        copy.start()
    for copy in copies:
        copy.wait()


def settle_outputs(occ, vir):
    return pl.pallas_call(
        write_kernel,
        out_shape=[jax.ShapeDtypeStruct(x.shape, x.dtype) for x in (occ, vir)],
        in_specs=[VMEM] * 2,
        out_specs=[ANY] * 2,
        scratch_shapes=[pltpu.SemaphoreType.DMA((2,))],
    )(*(pltpu.with_memory_space_constraint(x, pltpu.VMEM) for x in (occ, vir)))


def local(slab_occ, slab_vir, orbitals_occ, orbitals_vir, occ_energy, vir_energy, screened):
    n_orb, n_col = lax.axis_size("orb"), lax.axis_size("col")
    part = lax.axis_index("orb")
    block = slab_occ.shape[0] // n_orb
    n_occ, columns = orbitals_occ.shape
    n_vir = orbitals_vir.shape[0]
    kind = slab_occ.dtype
    if n_col == 16 and n_orb == 2 and block % 16 == 0 and columns % 512 == 0:
        return tuple(
            settle_outputs(
                *fused(
                    n_col, slab_occ, slab_vir, orbitals_occ, orbitals_vir,
                    occ_energy, vir_energy, screened,
                )
            )
        )
    up = lambda n: -(-n // 128) * 128
    scaled_occ = (slab_occ.astype(jnp.float32) * jnp.exp(occ_energy)[None, :]).astype(kind)
    scaled_vir = (slab_vir.astype(jnp.float32) * jnp.exp(-vir_energy)[None, :]).astype(kind)
    start = up(n_vir)
    slab = jnp.concatenate(
        [
            jnp.pad(scaled_vir, ((0, 0), (0, start - n_vir))),
            jnp.pad(scaled_occ, ((0, 0), (0, up(n_occ) - n_occ))),
        ],
        axis=1,
    ).reshape((n_orb, block, start + up(n_occ)))
    mine = lax.dynamic_slice_in_dim(screened, part * block, block, 0)
    mine = mine.reshape((block, n_col, columns)).transpose((1, 0, 2))

    def order(own, peer, n):
        own, peer = own[:, :n], peer[:, :n]
        return jnp.where(
            part == 0, jnp.concatenate([own, peer], 1), jnp.concatenate([peer, own], 1)
        )

    slabs, peer_occ, peer_vir, screens = gather(n_col, slab, orbitals_occ, orbitals_vir, mine)
    slabs = slabs.reshape((2, n_col * block, slab.shape[2]))
    own_slab, peer_slab = slabs[0], slabs[1]

    def dot(a, b):
        return jnp.dot(a, b, preferred_element_type=jnp.float32)

    green_vir = dot(own_slab[:, :n_vir], orbitals_vir) + dot(peer_slab[:, :n_vir], peer_vir)
    green_occ = dot(own_slab[:, start : start + n_occ], orbitals_occ) + dot(
        peer_slab[:, start : start + n_occ], peer_occ
    )
    screen = screens.reshape((n_col * block, columns)).astype(jnp.float32)
    occ_side = (green_vir * screen).astype(kind)
    vir_side = (green_occ * screen).astype(kind)
    dims = (((1,), (1,)), ((), ()))

    def project(side, orbitals):
        term = lax.dot_general(side, orbitals, dims, preferred_element_type=jnp.float32)
        return term.astype(kind).reshape((n_col // 4, 2, 2, block, orbitals.shape[0]))

    vir_own, vir_peer, occ_own, occ_peer = scatter(
        n_col,
        [
            project(vir_side, orbitals_vir),
            project(vir_side, peer_vir),
            project(occ_side, orbitals_occ),
            project(occ_side, peer_occ),
        ],
    )

    return order(occ_own, occ_peer, n_occ), order(vir_own, vir_peer, n_vir)


def solution(mesh):
    return jax.shard_map(
        local,
        mesh=mesh,
        in_specs=(
            P("col", "orb"),
            P("col", "orb"),
            P("orb", "col"),
            P("orb", "col"),
            P("orb"),
            P("orb"),
            P("col", None),
        ),
        out_specs=(P(("col", "orb"), None), P(("col", "orb"), None)),
        check_vma=False,
    )
```
